32 devices in a mesh: ctx: 8 (over z, x), fsdp: 4 (over y, core).
Axes of the slice: x: 2, y: 2, z: 4, core: 2. Of those that a mesh axis runs over, the one named last changes fastest.
Arguments:
- tokens: bfloat16 [4, 2048, 768], P('fsdp', 'ctx'), may hold values from -6 to 6
- starts: int32 [4, 4], P('fsdp'), may hold values from 0 to 2047, as said below
- labels: int32 [4, 4], P('fsdp'), may hold values from 0 to 13
- cotangent: bfloat16 [4, 2048, 768], P('fsdp', 'ctx'), may hold values from -6 to 6
- w_query: bfloat16 [768, 768], P('fsdp'), may hold values from -0.21875 to 0.21875
- b_query: bfloat16 [768], P('fsdp'), may hold values from -1.75 to 1.75
- w_key: bfloat16 [768, 768], P('fsdp'), may hold values from -0.21875 to 0.21875
- w_value: bfloat16 [768, 768], P('fsdp'), may hold values from -0.21875 to 0.21875
- b_value: bfloat16 [768], P('fsdp'), may hold values from -0.125 to 0.125
- w_out: bfloat16 [768, 768], P('fsdp'), may hold values from -4 to 4
- b_out: bfloat16 [768], P('fsdp'), may hold values from -1.75 to 1.75
- norm1_gain: bfloat16 [768], P('fsdp'), may hold values from 0.5 to 1.5
- norm1_bias: bfloat16 [768], P('fsdp'), may hold values from -1.75 to 1.75
- w_up: bfloat16 [768, 3072], P('fsdp'), may hold values from -0.21875 to 0.21875
- b_up: bfloat16 [3072], P('fsdp'), may hold values from -1.75 to 1.75
- w_down: bfloat16 [3072, 768], P('fsdp'), may hold values from -0.109375 to 0.109375
- b_down: bfloat16 [768], P('fsdp'), may hold values from -1.75 to 1.75
- norm2_gain: bfloat16 [768], P('fsdp'), may hold values from 0.5 to 1.5
- norm2_bias: bfloat16 [768], P('fsdp'), may hold values from -1.75 to 1.75
- w_student: bfloat16 [768, 128], P('fsdp'), may hold values from -0.21875 to 0.21875
- b_student: bfloat16 [128], P('fsdp'), may hold values from -0.3125 to 0.3125
- pool_query: bfloat16 [128], P('fsdp'), may hold values from -6 to 6
- w_pool: bfloat16 [128, 128], P('fsdp'), may hold values from -1 to 1
- b_pool: bfloat16 [128], P('fsdp'), may hold values from -1.75 to 1.75
- w_class: bfloat16 [128, 14], P('fsdp'), may hold values from -1.5 to 1.5
- b_class: bfloat16 [14], replicated, may hold values from -3 to 3
Outputs:
- hidden: bfloat16 [4, 2048, 768], P('fsdp', 'ctx')
- logits: float32 [4, 4, 14], P('fsdp')
- grad_tokens: float32 [4, 2048, 768], P('fsdp', 'ctx')
- grad_w_query: float32 [768, 768], P('fsdp')
- grad_b_query: float32 [768], P('fsdp')
- grad_w_key: float32 [768, 768], P('fsdp')
- grad_w_value: float32 [768, 768], P('fsdp')
- grad_b_value: float32 [768], P('fsdp')
- grad_w_out: float32 [768, 768], P('fsdp')
- grad_b_out: float32 [768], P('fsdp')
- grad_norm1_gain: float32 [768], P('fsdp')
- grad_norm1_bias: float32 [768], P('fsdp')
- grad_w_up: float32 [768, 3072], P('fsdp')
- grad_b_up: float32 [3072], P('fsdp')
- grad_w_down: float32 [3072, 768], P('fsdp')
- grad_b_down: float32 [768], P('fsdp')
- grad_norm2_gain: float32 [768], P('fsdp')
- grad_norm2_bias: float32 [768], P('fsdp')
- grad_w_student: float32 [768, 128], P('fsdp')
- grad_b_student: float32 [128], P('fsdp')
- grad_pool_query: float32 [128], P('fsdp')
- grad_w_pool: float32 [128, 128], P('fsdp')
- grad_b_pool: float32 [128], P('fsdp')
- grad_w_class: float32 [128, 14], P('fsdp')
- grad_b_class: float32 [14], replicated
The draws below stay inside these ranges and needn't reach their ends.
Inputs may be any that keep to these rules, and one draw needn't show every extreme that they name: `starts`: each row lists the first positions of its stream's 4 documents in increasing order; the first is 0 and every document has at least one token. In one stream the last document is a single token.
All inputs are finite; a program needn't handle non-finite values.
Results may differ from the reference program's by a relative error of at most 0.022.
Values may be sent and summed in bfloat16 or wider, within the bound.
No kernel may reach another device: no remote copies, remote signals or barrier semaphores. Data moves between devices by JAX's collectives and lax.ppermute only.
A program may use at most 256 MiB of HBM per device.

```python
import math
import jax
import jax.numpy as jnp
from jax import lax

D = 768
HEADS = 12
HEAD_DIM = 64
FF = 3072
SW = 128
POOL_HEADS = 2
CLASSES = 14
NDOC = 4
TOK_DEV = 256
SEQ = 2048
STREAMS = 4


def draw_starts(key, part):
    key_head, key_tail, key_cut, key_pick = jax.random.split(jax.random.fold_in(key, 11), 4)
    head_len = jax.random.randint(key_head, (STREAMS,), 1, TOK_DEV, dtype=jnp.int32)
    tail_len = jax.random.randint(key_tail, (STREAMS,), 2, TOK_DEV, dtype=jnp.int32)
    cut_len = jax.random.randint(key_cut, (STREAMS,), 1, tail_len, dtype=jnp.int32)
    chosen = jax.random.randint(key_pick, (), 0, STREAMS, dtype=jnp.int32)
    cut_len = jnp.where(jnp.arange(STREAMS, dtype=jnp.int32) == chosen, tail_len - 1, cut_len)
    zero_col = jnp.zeros((STREAMS,), jnp.int32)
    return jnp.stack([zero_col, head_len, SEQ - tail_len, SEQ - tail_len + cut_len], axis=1).astype(jnp.int32)


def place_ends(array, key, smallest, high):
    extent = array.shape
    place = [jax.random.randint(jax.random.fold_in(key, axis), (), 0, extent[axis]) for axis in range(len(extent))]
    array = array.at[tuple(place)].set(smallest)
    longest = extent.index(max(extent))
    place[longest] = (place[longest] + 1) % extent[longest]
    return array.at[tuple(place)].set(high)


def block_levels(key, dims, cuts, smallest, top_value):
    def one(axis_at, shards_of):
        draws = jax.random.uniform(jax.random.fold_in(jax.random.fold_in(key, 6), axis_at), (shards_of,), jnp.float32, smallest / len(cuts), top_value / len(cuts))
        return jnp.repeat(jnp.exp(draws), dims[axis_at] // shards_of).reshape((-1,) + (1,) * (len(dims) - axis_at - 1))

    factor_of = one(*cuts[0])
    for cut in cuts[1:]:
        factor_of = factor_of * one(*cut)
    return factor_of


def normal_values(stream_key, dims, spread, bound, pieces=(), kind=jnp.bfloat16):
    result = jax.random.normal(stream_key, dims, jnp.float32) * spread
    if len(pieces) > 0:
        result = block_levels(stream_key, dims, pieces, -0.22, 0.18) * result
    return jnp.clip(result, min=-bound, max=bound).astype(kind)


def setup_inputs(seed: int = 0) -> dict:
    key_list = jax.random.split(jax.random.key(seed), 27)
    return {
        "tokens": normal_values(key_list[0], (STREAMS, SEQ, D), 1.0, 6.0, ((0, 4), (1, 8))),
        "starts": draw_starts(jax.random.fold_in(key_list[26], 71), 0),
        "labels": place_ends(jax.random.randint(key_list[2], (STREAMS, NDOC), 0, CLASSES), jax.random.fold_in(key_list[2], 1), 0, CLASSES - 1).astype(jnp.int32),
        "cotangent": normal_values(key_list[3], (STREAMS, SEQ, D), 1.0, 6.0, ((0, 4), (1, 8))),
        "w_query": normal_values(key_list[4], (D, D), D ** -0.5, 0.21875, ((0, 4),)),
        "b_query": normal_values(key_list[5], (D,), 0.3, 1.75, ((0, 4),)),
        "w_key": normal_values(key_list[6], (D, D), D ** -0.5, 0.21875, ((0, 4),)),
        "w_value": normal_values(key_list[7], (D, D), D ** -0.5, 0.21875, ((0, 4),)),
        "b_value": normal_values(key_list[8], (D,), 0.02, 0.125, ((0, 4),)),
        "w_out": normal_values(key_list[9], (D, D), (0.4 * SEQ ** 0.5 * D ** -0.5), 4.0, ((0, 4),)),
        "b_out": normal_values(key_list[10], (D,), 0.3, 1.75, ((0, 4),)),
        "norm1_gain": jnp.clip(1.0 + 0.1 * jax.random.normal(key_list[11], (D,), jnp.float32), 0.5, 1.5).astype(jnp.bfloat16),
        "norm1_bias": normal_values(key_list[12], (D,), 0.3, 1.75, ((0, 4),)),
        "w_up": normal_values(key_list[13], (D, FF), D ** -0.5, 0.21875, ((0, 4),)),
        "b_up": normal_values(key_list[14], (FF,), 0.3, 1.75, ((0, 4),)),
        "w_down": normal_values(key_list[15], (FF, D), FF ** -0.5, 0.109375, ((0, 4),)),
        "b_down": normal_values(key_list[16], (D,), 0.3, 1.75, ((0, 4),)),
        "norm2_gain": jnp.clip(1.0 + 0.1 * jax.random.normal(key_list[17], (D,), jnp.float32), 0.5, 1.5).astype(jnp.bfloat16),
        "norm2_bias": normal_values(key_list[18], (D,), 0.3, 1.75, ((0, 4),)),
        "w_student": normal_values(key_list[19], (D, SW), D ** -0.5, 0.21875, ((0, 4),)),
        "b_student": normal_values(key_list[20], (SW,), 0.05, 0.3125, ((0, 4),)),
        "pool_query": normal_values(key_list[21], (SW,), 1.0, 6.0, ((0, 4),)),
        "w_pool": normal_values(key_list[22], (SW, SW), (2.0 * SW ** -0.5), 1.0, ((0, 4),)),
        "b_pool": normal_values(key_list[23], (SW,), 0.3, 1.75, ((0, 4),)),
        "w_class": normal_values(key_list[24], (SW, CLASSES), (3.0 * SW ** -0.5), 1.5, ((0, 4),)),
        "b_class": normal_values(key_list[25], (CLASSES,), 0.5, 3.0),
    }


@jax.custom_vjp
def low(v):
    return lax.optimization_barrier(v.astype(jnp.bfloat16)).astype(jnp.float32)

@jax.custom_vjp
def low_back(v):
    return v

def low_keep(v):
    return (low(v), None)

def low_pass(kept, grad):
    return (grad,)

def back_keep(v):
    return (v, None)

def back_low(kept, grad):
    return (low(grad),)
low.defvjp(low_keep, low_pass)
low_back.defvjp(back_keep, back_low)
big_negative = -1e+30
norm_eps = 1e-05

def matmul(left_mat, right_mat):
    return jnp.dot(left_mat, right_mat, precision=lax.Precision.HIGHEST)

def layer_norm(field_in, gain_row, bias_row):
    centre = field_in - lax.optimization_barrier(jnp.mean(field_in, axis=-1, keepdims=True))
    spread_sq = lax.optimization_barrier(jnp.mean(centre * centre, axis=-1, keepdims=True))
    return centre * lax.rsqrt(spread_sq + norm_eps) * gain_row + bias_row

def stream_pass(x_row, starts_row, weight_pack):
    w_query, b_query, w_key, w_value, b_value, w_out, b_out, norm1_gain, norm1_bias, w_up, b_up, w_down, b_down, norm2_gain, norm2_bias, w_student, b_student, pool_query, w_pool, b_pool, w_class, b_class = weight_pack
    seq_len = x_row.shape[0]
    positions = jnp.arange(seq_len, dtype=jnp.int32)
    doc_ids = lax.optimization_barrier(jnp.sum((starts_row[None, :] <= positions[:, None]).astype(jnp.int32), axis=1)) - 1
    query_all = low_back(low(matmul(x_row, w_query) + b_query))
    key_all = low_back(low(matmul(x_row, w_key)))
    value_all = low_back(low(matmul(x_row, w_value) + b_value))
    key_heads = key_all.reshape(seq_len, HEADS, HEAD_DIM)
    value_heads = value_all.reshape(seq_len, HEADS, HEAD_DIM)
    score_scale = 1.0 / math.sqrt(HEAD_DIM)
    block_rows = math.gcd(seq_len, 512)
    block_count = seq_len // block_rows

    def attend(block_pack):
        query_blk, doc_blk = block_pack
        scores = jnp.einsum('qhd,khd->hqk', query_blk, key_heads, precision=lax.Precision.HIGHEST) * score_scale
        scores = low_back(scores)
        same_doc = (doc_blk[:, None] == doc_ids[None, :])[None]
        prob_blk = jax.nn.softmax(jnp.where(same_doc, scores, big_negative), axis=-1)
        mixed = jnp.einsum('hqk,khd->qhd', low(prob_blk), value_heads, precision=lax.Precision.HIGHEST)
        return mixed.reshape(block_rows, HEADS * HEAD_DIM)
    attn_out = lax.map(jax.checkpoint(attend), (query_all.reshape(block_count, block_rows, HEADS, HEAD_DIM), doc_ids.reshape(block_count, block_rows)))
    attn_out = low_back(low(attn_out.reshape(seq_len, HEADS * HEAD_DIM)))
    branch = low_back(matmul(attn_out, w_out) + b_out)
    hidden_one = layer_norm(x_row + branch, norm1_gain, norm1_bias)
    up_pre = low_back(matmul(low(hidden_one), w_up) + b_up)
    up_act = jax.nn.gelu(up_pre, approximate=False)
    down_out = low_back(matmul(low(up_act), w_down) + b_down)
    layer_out = layer_norm(hidden_one + down_out, norm2_gain, norm2_bias)
    student = low_back(matmul(low(layer_out), w_student) + b_student)
    pool_dim = student.shape[1] // POOL_HEADS
    pool_scale = 1.0 / math.sqrt(pool_dim)
    pool_scores = lax.optimization_barrier(jnp.sum((student * pool_query).reshape(seq_len, POOL_HEADS, pool_dim), axis=2)) * pool_scale
    onehot = doc_ids[:, None] == jnp.arange(NDOC, dtype=jnp.int32)[None, :]
    doc_max = lax.optimization_barrier(jnp.max(jnp.where(onehot[:, :, None], pool_scores[:, None, :], big_negative), axis=0))
    tok_weight = jnp.exp(pool_scores - doc_max[doc_ids])
    hot_float = onehot.astype(jnp.float32)
    doc_total = matmul(hot_float.T, tok_weight)
    doc_acc = matmul(hot_float.T, jnp.repeat(tok_weight, pool_dim, axis=1) * student)
    pooled = doc_acc / jnp.repeat(doc_total, pool_dim, axis=1)
    head_act = jnp.tanh(matmul(pooled, w_pool) + b_pool)
    logits = matmul(head_act, w_class) + b_class
    return (layer_out, logits)

def reference(tokens, starts, labels, cotangent, w_query, b_query, w_key, w_value, b_value, w_out, b_out, norm1_gain, norm1_bias, w_up, b_up, w_down, b_down, norm2_gain, norm2_bias, w_student, b_student, pool_query, w_pool, b_pool, w_class, b_class):
    weight_pack = tuple((weight_item.astype(jnp.float32) for weight_item in (w_query, b_query, w_key, w_value, b_value, w_out, b_out, norm1_gain, norm1_bias, w_up, b_up, w_down, b_down, norm2_gain, norm2_bias, w_student, b_student, pool_query, w_pool, b_pool, w_class, b_class)))
    inputs = tokens.astype(jnp.float32)

    def forward(x_all, weights_in):
        outs_layer = []
        outs_logit = []
        for stream_index in range(STREAMS):
            layer_one, logit_one = stream_pass(x_all[stream_index], starts[stream_index], weights_in)
            outs_layer.append(layer_one)
            outs_logit.append(logit_one)
        return (jnp.stack(outs_layer), jnp.stack(outs_logit))
    (layer_out, logits), pullback = jax.vjp(forward, inputs, weight_pack)
    class_probs = jax.nn.softmax(logits, axis=-1)
    label_hot = (labels[:, :, None] == jnp.arange(CLASSES, dtype=jnp.int32)[None, None, :]).astype(jnp.float32)
    grad_inputs, grad_weights = pullback((cotangent.astype(jnp.float32), class_probs - label_hot))
    return (layer_out.astype(jnp.bfloat16), logits, grad_inputs, grad_weights[0], grad_weights[1], grad_weights[2], grad_weights[3], grad_weights[4], grad_weights[5], grad_weights[6], grad_weights[7], grad_weights[8], grad_weights[9], grad_weights[10], grad_weights[11], grad_weights[12], grad_weights[13], grad_weights[14], grad_weights[15], grad_weights[16], grad_weights[17], grad_weights[18], grad_weights[19], grad_weights[20], grad_weights[21])
```

```python
import functools
import math

import jax
import jax.numpy as jnp
from jax import lax
from jax.experimental import pallas as pl
from jax.experimental.pallas import tpu as pltpu
from jax.sharding import PartitionSpec as P

HEADS = 12
HEAD_DIM = 64
POOL_HEADS = 2
CLASSES = 14
NDOC = 4

big_negative = -1e30
norm_eps = 1e-05
f32 = jnp.float32
bf16 = jnp.bfloat16
VMEM_LIMIT = 56 * 1024 * 1024


def doc_of(positions, starts_row):
    return jnp.sum((starts_row[None, :] <= positions[:, None]).astype(jnp.int32), axis=1) - 1


def layer_forward(field_in, gain_row, bias_row):
    centre = field_in - jnp.mean(field_in, axis=-1, keepdims=True)
    inv_std = lax.rsqrt(jnp.mean(centre * centre, axis=-1, keepdims=True) + norm_eps)
    normed = centre * inv_std
    return (normed * gain_row + bias_row, normed, inv_std)


def layer_backward(grad_in, normed, inv_std, gain_row):
    scaled = grad_in * gain_row
    back_out = inv_std * (
        scaled
        - jnp.mean(scaled, axis=-1, keepdims=True)
        - normed * jnp.mean(scaled * normed, axis=-1, keepdims=True)
    )
    return (back_out, jnp.sum(grad_in * normed, axis=0), jnp.sum(grad_in, axis=0))


def gelu_slope(field_in):
    normal_cdf = 0.5 * (1.0 + lax.erf(field_in * (1.0 / math.sqrt(2.0))))
    normal_pdf = jnp.exp(-0.5 * field_in * field_in) * (1.0 / math.sqrt(2.0 * math.pi))
    return normal_cdf + field_in * normal_pdf


def cross_rows(left_mat, right_mat):
    return lax.dot_general(
        left_mat, right_mat, (((0,), (0,)), ((), ())), preferred_element_type=f32
    )


def back_mul(left_mat, right_mat):
    return lax.dot_general(
        left_mat, right_mat, (((1,), (1,)), ((), ())), preferred_element_type=f32
    )


def small_dot(left_mat, right_mat):
    return jnp.dot(left_mat, right_mat, precision=lax.Precision.HIGHEST)


def _half_mask(shape, axis, half):
    return (lax.broadcasted_iota(jnp.int32, shape, axis) // HEAD_DIM) == half


def _split3(row):
    hi = row.astype(bf16)
    rest = row - hi.astype(f32)
    mid = rest.astype(bf16)
    low = (rest - mid.astype(f32)).astype(bf16)
    return hi.astype(f32), mid.astype(f32), low.astype(f32)


def _extra_rows(docrow, row=None):
    at = lax.broadcasted_iota(jnp.int32, (128, docrow.shape[1]), 0)
    out = jnp.where((at < NDOC) & (at != docrow), big_negative, 0.0)
    if row is not None:
        for k, part in enumerate(_split3(row)):
            out = out + jnp.where(at == NDOC + k, part, 0.0)
    return out.astype(bf16)


def attend_kernel(chunks, q_ref, k_ref, v_ref, extra_ref, doc_ref, attn_ref, low_ref, lse_ref, s_ref):
    rows = k_ref.shape[0] // chunks
    q_t = q_ref[...].astype(f32).T
    bias = _extra_rows(doc_ref[...])
    outs = []
    for half in range(2):
        q_aug = jnp.concatenate(
            [jnp.where(_half_mask(q_t.shape, 0, half), q_t, 0.0).astype(bf16), bias], axis=0
        )
        top = None
        for c in range(chunks):
            at = pl.ds(c * rows, rows)
            k_aug = jnp.concatenate([k_ref[at, :], extra_ref[at, :]], axis=1)
            s_now = jnp.dot(k_aug, q_aug, preferred_element_type=f32)
            s_ref[half, at, :] = s_now
            top_now = jnp.max(s_now, axis=0, keepdims=True)
            top = top_now if top is None else jnp.maximum(top, top_now)
        total = jnp.zeros_like(top)
        mixed = jnp.zeros((2 * HEAD_DIM, q_t.shape[1]), f32)
        for c in range(chunks):
            at = pl.ds(c * rows, rows)
            p_now = jnp.exp(s_ref[half, at, :] - top)
            total = total + jnp.sum(p_now, axis=0, keepdims=True)
            mixed = mixed + cross_rows(v_ref[at, :], p_now.astype(bf16))
        lse_ref[0, pl.ds(half, 1), :] = top + jnp.log(total)
        outs.append(mixed[half * HEAD_DIM : (half + 1) * HEAD_DIM] / total)
    out_t = jnp.concatenate(outs, axis=0)
    attn_ref[...] = out_t
    low_ref[...] = out_t.T.astype(bf16)


def attend(query, keys, values, extra, docs):
    tok, width = query.shape
    seq = keys.shape[0]
    pairs = width // (2 * HEAD_DIM)
    lanes = 2 * HEAD_DIM
    return pl.pallas_call(
        functools.partial(attend_kernel, 4),
        grid=(pairs,),
        in_specs=[
            pl.BlockSpec((tok, lanes), lambda p: (0, p)),
            pl.BlockSpec((seq, lanes), lambda p: (0, p)),
            pl.BlockSpec((seq, lanes), lambda p: (0, p)),
            pl.BlockSpec((seq, lanes), lambda p: (0, 0)),
            pl.BlockSpec((1, tok), lambda p: (0, 0)),
        ],
        out_specs=[
            pl.BlockSpec((lanes, tok), lambda p: (p, 0)),
            pl.BlockSpec((tok, lanes), lambda p: (0, p)),
            pl.BlockSpec((1, 2, tok), lambda p: (p, 0, 0)),
        ],
        out_shape=[
            jax.ShapeDtypeStruct((width, tok), f32),
            jax.ShapeDtypeStruct((tok, width), bf16),
            jax.ShapeDtypeStruct((pairs, 2, tok), f32),
        ],
        scratch_shapes=[pltpu.VMEM((2, seq, tok), f32)],
        compiler_params=pltpu.CompilerParams(vmem_limit_bytes=VMEM_LIMIT),
        cost_estimate=pl.CostEstimate(
            flops=4 * tok * seq * width, transcendentals=tok * seq * HEADS, bytes_accessed=4 * seq * width
        ),
        name="attend",
    )(query, keys, values, extra, docs)


def attend_back_kernel(
    chunks, q_ref, k_ref, v_ref, extra_ref, doc_ref, attn_ref, lse_ref, g_ref, dq_ref, dk_ref, dv_ref
):
    rows = k_ref.shape[0] // chunks
    q_low = q_ref[...]
    g_low = g_ref[...]
    q_t = q_low.astype(f32).T
    g_t = g_low.astype(f32).T
    prod = attn_ref[...] * g_t
    lanes = 2 * HEAD_DIM
    q_side, g_side, q_rows, g_rows = [], [], [], []
    for half in range(2):
        pick = _half_mask(q_t.shape, 0, half)
        delta = jnp.sum(prod[half * HEAD_DIM : (half + 1) * HEAD_DIM], axis=0, keepdims=True)
        q_side.append(
            jnp.concatenate(
                [
                    jnp.where(pick, q_t, 0.0).astype(bf16),
                    _extra_rows(doc_ref[...], -lse_ref[0, pl.ds(half, 1), :]),
                ],
                axis=0,
            )
        )
        g_side.append(
            jnp.concatenate(
                [
                    jnp.where(pick, g_t, 0.0).astype(bf16),
                    _extra_rows(jnp.full_like(doc_ref[...], -1), -delta)
                    * (lax.broadcasted_iota(jnp.int32, (128, q_t.shape[1]), 0) >= NDOC).astype(bf16),
                ],
                axis=0,
            )
        )
        pick_lane = _half_mask(q_low.shape, 1, half)
        q_rows.append(jnp.where(pick_lane, q_low.astype(f32), 0.0).astype(bf16))
        g_rows.append(jnp.where(pick_lane, g_low.astype(f32), 0.0).astype(bf16))
    q_rows = jnp.concatenate(q_rows, axis=0)
    g_rows = jnp.concatenate(g_rows, axis=0)
    dq_t = [jnp.zeros((lanes, q_t.shape[1]), f32) for half in range(2)]
    for c in range(chunks):
        at = pl.ds(c * rows, rows)
        k_now = k_ref[at, :]
        extra = extra_ref[at, :]
        k_aug = jnp.concatenate([k_now, extra], axis=1)
        v_aug = jnp.concatenate([v_ref[at, :], extra], axis=1)
        p_low, s_low = [], []
        for half in range(2):
            prob = jnp.exp(jnp.dot(k_aug, q_side[half], preferred_element_type=f32))
            slope = jnp.dot(v_aug, g_side[half], preferred_element_type=f32)
            p_low.append(prob.astype(bf16))
            s_low.append((prob * slope).astype(bf16))
            dq_t[half] = dq_t[half] + cross_rows(k_now, s_low[half])
        dk_ref[at, :] = jnp.dot(
            jnp.concatenate(s_low, axis=1), q_rows, preferred_element_type=f32
        ).astype(bf16)
        dv_ref[at, :] = jnp.dot(
            jnp.concatenate(p_low, axis=1), g_rows, preferred_element_type=f32
        ).astype(bf16)
    pick = _half_mask(q_t.shape, 0, 0)
    dq_ref[...] = (jnp.where(pick, dq_t[0], dq_t[1]).T * (1.0 / math.sqrt(HEAD_DIM))).astype(bf16)


def attend_back(query, keys, values, extra, docs, attn_t, lse, grad_attn):
    tok, width = query.shape
    seq = keys.shape[0]
    pairs = width // (2 * HEAD_DIM)
    lanes = 2 * HEAD_DIM
    return pl.pallas_call(
        functools.partial(attend_back_kernel, 4),
        grid=(pairs,),
        in_specs=[
            pl.BlockSpec((tok, lanes), lambda p: (0, p)),
            pl.BlockSpec((seq, lanes), lambda p: (0, p)),
            pl.BlockSpec((seq, lanes), lambda p: (0, p)),
            pl.BlockSpec((seq, lanes), lambda p: (0, 0)),
            pl.BlockSpec((1, tok), lambda p: (0, 0)),
            pl.BlockSpec((lanes, tok), lambda p: (p, 0)),
            pl.BlockSpec((1, 2, tok), lambda p: (p, 0, 0)),
            pl.BlockSpec((tok, lanes), lambda p: (0, p)),
        ],
        out_specs=[
            pl.BlockSpec((tok, lanes), lambda p: (0, p)),
            pl.BlockSpec((seq, lanes), lambda p: (0, p)),
            pl.BlockSpec((seq, lanes), lambda p: (0, p)),
        ],
        out_shape=[
            jax.ShapeDtypeStruct((tok, width), bf16),
            jax.ShapeDtypeStruct((seq, width), bf16),
            jax.ShapeDtypeStruct((seq, width), bf16),
        ],
        compiler_params=pltpu.CompilerParams(vmem_limit_bytes=VMEM_LIMIT),
        cost_estimate=pl.CostEstimate(
            flops=10 * tok * seq * width, transcendentals=tok * seq * HEADS, bytes_accessed=8 * seq * width
        ),
        name="attend_back",
    )(query, keys, values, extra, docs, attn_t, lse, grad_attn)


def swap(value, axis, bit):
    count = lax.axis_size(axis)
    return lax.ppermute(value, axis, [(i, i ^ bit) for i in range(count)])


def gather_shards(shard):
    index = lax.axis_index("fsdp")
    core, far = index % 2, index // 2
    other = swap(shard, "fsdp", 2)
    column = jnp.where(far == 0, jnp.stack([shard, other]), jnp.stack([other, shard]))
    across = swap(column, "fsdp", 1)
    full = jnp.where(
        core == 0, jnp.stack([column, across], axis=1), jnp.stack([across, column], axis=1)
    )
    return full.reshape(4 * shard.shape[0], shard.shape[1])


def bits_of(axis):
    return [1 << k for k in range(lax.axis_size(axis).bit_length() - 1)]


def halve(value, axis, bit, at):
    mine = (lax.axis_index(axis) // bit) % 2
    send = lax.dynamic_index_in_dim(value, 1 - mine, at, keepdims=False)
    keep = lax.dynamic_index_in_dim(value, mine, at, keepdims=False)
    got = swap(send, axis, bit)
    return (keep.astype(f32) + got.astype(f32)).astype(bf16)


def scatter_sum(full, axis):
    rows, n = full.shape[1:]
    for bit in bits_of(axis):
        full = halve(full.reshape(-1, 2, rows, n), axis, bit, 1)
    return full.reshape(rows, n)


def double(value, axis, bit):
    mine = (lax.axis_index(axis) // bit) % 2
    got = swap(value, axis, bit)
    return jnp.where(mine == 0, jnp.stack([value, got]), jnp.stack([got, value]))


def ring_sum(rows):
    total, n = rows.shape
    bits = bits_of("ctx")
    for bit in bits:
        rows = halve(rows.reshape(2, -1, n), "ctx", bit, 0)
    for bit in reversed(bits):
        rows = double(rows, "ctx", bit).reshape(-1, n)
    return rows


def reduce_grad(blocks):
    return ring_sum(scatter_sum(blocks, "fsdp"))


def shards(
    tokens,
    starts,
    labels,
    cotangent,
    w_query,
    b_query,
    w_key,
    w_value,
    b_value,
    w_out,
    b_out,
    norm1_gain,
    norm1_bias,
    w_up,
    b_up,
    w_down,
    b_down,
    norm2_gain,
    norm2_bias,
    w_student,
    b_student,
    pool_query,
    w_pool,
    b_pool,
    w_class,
    b_class,
):
    cycle_size = lax.axis_size("ctx")
    cycle_index = lax.axis_index("ctx")
    fsdp_size = lax.axis_size("fsdp")
    fsdp_index = lax.axis_index("fsdp")
    tok_rows = tokens.shape[1]
    width = tokens.shape[2]
    part = width // fsdp_size
    seq_total = tok_rows * cycle_size
    score_scale = 1.0 / math.sqrt(HEAD_DIM)
    starts_row = starts[0]
    x_in = tokens[0]
    x_all = lax.all_gather(x_in, "ctx", axis=0, tiled=True)

    hidden_part = b_up.shape[0]
    ups = hidden_part // part
    pool_part, pool_width = w_pool.shape

    def pack(tall, pools, classes, vectors, ups_vector, pool_vectors, extra_row):
        first = jnp.concatenate(jnp.split(tall, width // pool_width, axis=0), axis=1)
        kind = tall.dtype
        room = width - 2 * pool_width
        half_room = room // 2
        cells = [jnp.pad(v, (0, half_room - part)) for v in vectors]
        cells += [jnp.pad(v, (0, half_room - part)) for v in jnp.split(ups_vector, ups)]
        lines = jnp.concatenate(cells).reshape(-1, room)
        last = jnp.concatenate(pool_vectors + [extra_row])
        lines = jnp.concatenate([lines, jnp.pad(last, (0, room - last.shape[0]))[None]], axis=0)
        lines = jnp.pad(lines, ((0, pool_part - lines.shape[0]), (0, 0)))
        second = jnp.concatenate(
            [pools, jnp.pad(classes, ((0, 0), (0, pool_width - CLASSES))), lines], axis=1
        )
        return jnp.concatenate([first, second], axis=0).astype(kind)

    def unpack(rows):
        blocks = rows.shape[0]
        high = part * pool_width // width
        first = rows[:, :high].reshape(blocks, high, width // pool_width, pool_width)
        tall = jnp.concatenate([first[:, :, k] for k in range(width // pool_width)], axis=1)
        second = rows[:, high:]
        room = width - 2 * pool_width
        half_room = room // 2
        lines = second[:, :, 2 * pool_width :]
        cells = [
            lines[:, k // 2, (k % 2) * half_room : (k % 2) * half_room + part] for k in range(8 + ups)
        ]
        last = lines[:, (8 + ups) // 2]
        return (
            tall.reshape(-1, pool_width),
            second[:, :, :pool_width].reshape(-1, pool_width),
            second[:, :, pool_width : pool_width + CLASSES].reshape(-1, CLASSES),
            [c.reshape(-1) for c in cells[:8]],
            jnp.stack(cells[8:], axis=1).reshape(-1),
            [last[:, k * pool_part : (k + 1) * pool_part].reshape(-1) for k in range(3)],
            last[0, 3 * pool_part : 3 * pool_part + CLASSES],
        )

    vectors = [b_query, b_value, b_out, norm1_gain, norm1_bias, b_down, norm2_gain, norm2_bias]
    small = pack(
        w_student, w_pool, w_class, vectors, b_up, [b_student, pool_query, b_pool], jnp.zeros((CLASSES,), bf16)
    )
    first = gather_shards(jnp.concatenate([w_query, w_key, w_value, small], axis=0)).reshape(
        fsdp_size, -1, width
    )
    full_wq = first[:, :part].reshape(width, width)
    full_wk = first[:, part : 2 * part].reshape(width, width)
    full_wv = first[:, 2 * part : 3 * part].reshape(width, width)
    full_wo = gather_shards(w_out)
    full_w1 = gather_shards(w_up)
    full_w2 = gather_shards(w_down)
    full_ws, pool_w, class_w, vectors, full_c1, pool_vectors, _ = unpack(first[:, 3 * part :])
    full_bq, full_bv, full_bo, gain_one, full_e1, full_c2, gain_two, full_e2 = (
        v.astype(f32) for v in vectors
    )
    full_bs, query_pool, full_bp = (v.astype(f32) for v in pool_vectors)
    full_c1, pool_w, class_w = full_c1.astype(f32), pool_w.astype(f32), class_w.astype(f32)

    local_pos = cycle_index * tok_rows + jnp.arange(tok_rows, dtype=jnp.int32)
    local_doc = doc_of(local_pos, starts_row)
    all_doc = doc_of(jnp.arange(seq_total, dtype=jnp.int32), starts_row)
    at = jnp.arange(128, dtype=jnp.int32)[None, :]
    extra = ((at == all_doc[:, None]) | ((at >= NDOC) & (at < NDOC + 3))).astype(bf16)
    docs = local_doc[None, :]

    query_b = (jnp.dot(x_in, full_wq, preferred_element_type=f32) + full_bq).astype(bf16)
    query_s = (query_b.astype(f32) * score_scale).astype(bf16)
    key_b = jnp.dot(x_all, full_wk, preferred_element_type=f32).astype(bf16)
    value_b = (jnp.dot(x_all, full_wv, preferred_element_type=f32) + full_bv).astype(bf16)
    attn_t, attn_b, lse = attend(query_s, key_b, value_b, extra, docs)

    branch = jnp.dot(attn_b, full_wo, preferred_element_type=f32) + full_bo
    hidden_one, normed_one, inv_one = layer_forward(x_in.astype(f32) + branch, gain_one, full_e1)
    hidden_one_b = hidden_one.astype(bf16)
    up_pre = jnp.dot(hidden_one_b, full_w1, preferred_element_type=f32) + full_c1
    up_b = jax.nn.gelu(up_pre, approximate=False).astype(bf16)
    down_out = jnp.dot(up_b, full_w2, preferred_element_type=f32) + full_c2
    layer_out, normed_two, inv_two = layer_forward(hidden_one + down_out, gain_two, full_e2)
    out_b = layer_out.astype(bf16)
    pool_dim = pool_width // POOL_HEADS
    pool_scale = 1.0 / math.sqrt(pool_dim)
    student = jnp.dot(out_b, full_ws, preferred_element_type=f32) + full_bs
    onehot_bool = local_doc[:, None] == jnp.arange(NDOC, dtype=jnp.int32)[None, :]
    onehot = onehot_bool.astype(f32)

    def pick_rows(table):
        return jnp.sum(jnp.where(onehot_bool[:, :, None], table[None, :, :], 0.0), axis=1)

    pool_scores = (
        jnp.sum((student * query_pool[None, :]).reshape(tok_rows, POOL_HEADS, pool_dim), axis=2)
        * pool_scale
    )
    local_max = jnp.max(
        jnp.where(onehot_bool[:, :, None], pool_scores[:, None, :], big_negative), axis=0
    )
    tok_weight = jnp.exp(pool_scores - pick_rows(local_max))
    local_total = small_dot(onehot.T, tok_weight)
    local_acc = small_dot(onehot.T, jnp.repeat(tok_weight, pool_dim, axis=1) * student)
    packed = jnp.concatenate([local_acc, jnp.pad(local_max, ((0, 0), (0, 62))), jnp.pad(local_total, ((0, 0), (0, 62)))], axis=1)
    parts = lax.all_to_all(jnp.broadcast_to(packed[None], (cycle_size,) + packed.shape), "ctx", 0, 0, tiled=True)
    part_acc = parts[:, :, :pool_width]
    part_max = parts[:, :, pool_width : pool_width + POOL_HEADS]
    part_total = parts[:, :, pool_width + 64 : pool_width + 64 + POOL_HEADS]
    doc_max = jnp.max(part_max, axis=0)
    factor = jnp.exp(part_max - doc_max[None])
    doc_total = jnp.sum(part_total * factor, axis=0)
    doc_acc = jnp.sum(part_acc * jnp.repeat(factor, pool_dim, axis=2), axis=0)
    pooled = doc_acc / jnp.repeat(doc_total, pool_dim, axis=1)
    head_act = jnp.tanh(small_dot(pooled, pool_w) + full_bp)
    logits = small_dot(head_act, class_w) + b_class.astype(f32)
    label_hot = (labels[0][:, None] == jnp.arange(CLASSES, dtype=jnp.int32)[None, :]).astype(f32)
    grad_logits = jax.nn.softmax(logits, axis=-1) - label_hot
    grad_wc = small_dot(head_act.T, grad_logits)
    grad_bc = jnp.sum(grad_logits, axis=0)
    grad_pre = small_dot(grad_logits, class_w.T) * (1.0 - head_act * head_act)
    grad_wp = small_dot(pooled.T, grad_pre)
    grad_bp = jnp.sum(grad_pre, axis=0)
    grad_pooled = small_dot(grad_pre, pool_w.T)
    tok_norm_w = jnp.exp(pool_scores - pick_rows(doc_max)) / pick_rows(doc_total)
    tok_gpool = pick_rows(grad_pooled)
    tok_pooled = pick_rows(pooled)
    inner_dot = jnp.sum(
        (tok_gpool * (student - tok_pooled)).reshape(tok_rows, POOL_HEADS, pool_dim), axis=2
    )
    grad_score = tok_norm_w * inner_dot
    spread_score = jnp.repeat(grad_score, pool_dim, axis=1)
    grad_student_f = (
        jnp.repeat(tok_norm_w, pool_dim, axis=1) * tok_gpool
        + spread_score * query_pool[None, :] * pool_scale
    )
    grad_qp = jnp.sum(spread_score * student, axis=0) * pool_scale
    grad_student_b = grad_student_f.astype(bf16)
    grad_ws = cross_rows(out_b, grad_student_b)
    grad_bs = jnp.sum(grad_student_b.astype(f32), axis=0)
    grad_layer = cotangent[0].astype(f32) + back_mul(grad_student_b, full_ws)
    grad_res2, grad_g2, grad_e2 = layer_backward(grad_layer, normed_two, inv_two, gain_two)
    grad_down_b = grad_res2.astype(bf16)
    grad_w2 = cross_rows(up_b, grad_down_b).astype(bf16)
    done_w2 = reduce_grad(grad_w2.reshape(fsdp_size, -1, width))
    grad_c2 = jnp.sum(grad_down_b.astype(f32), axis=0)
    grad_up_b = (back_mul(grad_down_b, full_w2) * gelu_slope(up_pre)).astype(bf16)
    grad_w1 = cross_rows(hidden_one_b, grad_up_b).astype(bf16)
    grad_w1 = grad_w1.reshape(fsdp_size, part, -1)
    done_w1 = reduce_grad(
        jnp.concatenate([grad_w1[:, :, k * width : (k + 1) * width] for k in range(ups)], axis=1)
    )
    grad_c1 = jnp.sum(grad_up_b.astype(f32), axis=0)
    grad_hidden = grad_res2 + back_mul(grad_up_b, full_w1)
    grad_res1, grad_g1, grad_e1 = layer_backward(grad_hidden, normed_one, inv_one, gain_one)
    grad_branch_b = grad_res1.astype(bf16)
    grad_wo = cross_rows(attn_b, grad_branch_b).astype(bf16)
    grad_bo = jnp.sum(grad_branch_b.astype(f32), axis=0)
    grad_attn_b = back_mul(grad_branch_b, full_wo).astype(bf16)

    grad_query_b, grad_key_b, grad_value_b = attend_back(
        query_s, key_b, value_b, extra, docs, attn_t, lse, grad_attn_b
    )
    others = (back_mul(grad_key_b, full_wk) + back_mul(grad_value_b, full_wv)).astype(bf16)
    others = scatter_sum(others.reshape(cycle_size, tok_rows, width), "ctx")
    grad_wq = cross_rows(x_in, grad_query_b).astype(bf16)
    grad_bq = jnp.sum(grad_query_b.astype(f32), axis=0)
    grad_wk = cross_rows(x_all, grad_key_b).astype(bf16)
    grad_wv = cross_rows(x_all, grad_value_b).astype(bf16)
    grad_bv = jnp.sum(grad_value_b.astype(f32), axis=0)
    grad_tokens = grad_res1 + back_mul(grad_query_b, full_wq) + others.astype(f32)

    head_owner = (cycle_index == 0).astype(f32)
    zero_row = jnp.zeros((width,), f32)

    def block(value, k):
        size = value.shape[0] // fsdp_size
        return value[k * size : (k + 1) * size]

    vectors = [zero_row, zero_row, grad_bo, grad_g1, grad_e1, grad_c2, grad_g2, grad_e2]
    small = jnp.stack(
        [
            pack(
                block(grad_ws, k),
                block(grad_wp, k) * head_owner,
                block(grad_wc, k) * head_owner,
                [block(v, k) for v in vectors],
                block(grad_c1, k),
                [block(grad_bs, k), block(grad_qp, k), block(grad_bp, k) * head_owner],
                grad_bc * head_owner,
            )
            for k in range(fsdp_size)
        ]
    ).astype(bf16)
    middle = reduce_grad(jnp.concatenate([grad_wo.reshape(fsdp_size, part, width), small], axis=1))
    middle = middle.astype(f32)
    done_ws, done_wp, done_wc, done_v, done_c1, done_p, done_bc = unpack(middle[None, part:])
    done_wo = middle[:part]
    late = jnp.concatenate([grad_bq.reshape(fsdp_size, 1, part), grad_bv.reshape(fsdp_size, 1, part)], axis=1)
    late = jnp.pad(late, ((0, 0), (0, 62), (0, width - part))).astype(bf16)
    last = jnp.concatenate(
        [g.reshape(fsdp_size, part, width) for g in (grad_wq, grad_wk, grad_wv)] + [late], axis=1
    )
    last = reduce_grad(last).astype(f32)
    done_wq, done_wk, done_wv = (last[k * part : (k + 1) * part] for k in range(3))
    done_v[0] = last[3 * part, :part]
    done_v[1] = last[3 * part + 1, :part]
    done_w1 = jnp.concatenate(jnp.split(done_w1.astype(f32), ups, axis=0), axis=1)
    return (
        out_b[None],
        logits[None],
        grad_tokens[None],
        done_wq,
        done_v[0],
        done_wk,
        done_wv,
        done_v[1],
        done_wo,
        done_v[2],
        done_v[3],
        done_v[4],
        done_w1,
        done_c1,
        done_w2.astype(f32),
        done_v[5],
        done_v[6],
        done_v[7],
        done_ws,
        done_p[0],
        done_p[1],
        done_wp,
        done_p[2],
        done_wc,
        done_bc,
    )


def solution(mesh):
    in_specs = (
        P("fsdp", "ctx", None),
        P("fsdp", None),
        P("fsdp", None),
        P("fsdp", "ctx", None),
        P("fsdp", None),
        P("fsdp"),
        P("fsdp", None),
        P("fsdp", None),
        P("fsdp"),
        P("fsdp", None),
        P("fsdp"),
        P("fsdp"),
        P("fsdp"),
        P("fsdp", None),
        P("fsdp"),
        P("fsdp", None),
        P("fsdp"),
        P("fsdp"),
        P("fsdp"),
        P("fsdp", None),
        P("fsdp"),
        P("fsdp"),
        P("fsdp", None),
        P("fsdp"),
        P("fsdp", None),
        P(),
    )
    out_specs = (
        P("fsdp", "ctx", None),
        P("fsdp", None, None),
        P("fsdp", "ctx", None),
        P("fsdp", None),
        P("fsdp"),
        P("fsdp", None),
        P("fsdp", None),
        P("fsdp"),
        P("fsdp", None),
        P("fsdp"),
        P("fsdp"),
        P("fsdp"),
        P("fsdp", None),
        P("fsdp"),
        P("fsdp", None),
        P("fsdp"),
        P("fsdp"),
        P("fsdp"),
        P("fsdp", None),
        P("fsdp"),
        P("fsdp"),
        P("fsdp", None),
        P("fsdp"),
        P("fsdp", None),
        P(),
    )
    return jax.shard_map(shards, mesh=mesh, in_specs=in_specs, out_specs=out_specs, check_vma=False)
```

```python
import functools
import math

import jax
import jax.numpy as jnp
from jax import lax
from jax.experimental import pallas as pl
from jax.experimental.pallas import tpu as pltpu
from jax.sharding import PartitionSpec as P

HEADS = 12
HEAD_DIM = 64
POOL_HEADS = 2
CLASSES = 14
NDOC = 4

big_negative = -1e30
norm_eps = 1e-05
f32 = jnp.float32
bf16 = jnp.bfloat16
VMEM_LIMIT = 56 * 1024 * 1024
PLAN = [3, 0, 0, 1, 0, 0, 2, 0, 1, 3, 2, 1, 1, 3, 2, 1, 3, 1, 0, 3, 3, 1, 3, 3]


def doc_of(positions, starts_row):
    return jnp.sum((starts_row[None, :] <= positions[:, None]).astype(jnp.int32), axis=1) - 1


def cross_rows(left_mat, right_mat):
    return lax.dot_general(
        left_mat, right_mat, (((0,), (0,)), ((), ())), preferred_element_type=f32
    )


def back_mul(left_mat, right_mat):
    return lax.dot_general(
        left_mat, right_mat, (((1,), (1,)), ((), ())), preferred_element_type=f32
    )


def _half_mask(shape, axis, half):
    return (lax.broadcasted_iota(jnp.int32, shape, axis) // HEAD_DIM) == half


def _split3(row):
    hi = row.astype(bf16)
    rest = row - hi.astype(f32)
    mid = rest.astype(bf16)
    low = (rest - mid.astype(f32)).astype(bf16)
    return hi.astype(f32), mid.astype(f32), low.astype(f32)


def _extra_rows(docrow, row=None):
    at = lax.broadcasted_iota(jnp.int32, (128, docrow.shape[1]), 0)
    out = jnp.where((at < NDOC) & (at != docrow), big_negative, 0.0)
    if row is not None:
        for k, part in enumerate(_split3(row)):
            out = out + jnp.where(at == NDOC + k, part, 0.0)
    return out.astype(bf16)


def project_kernel(
    me_ref, x_ref, all_ref, vec_ref,
    wq0, wq1, wq2, wq3, wk0, wk1, wk2, wk3, wv0, wv1, wv2, wv3,
    q_ref, k_ref, v_ref, all_t_ref, wq_ref, wk_ref, wv_ref, sems,
):
    @pl.when(pl.program_id(0) == 0)
    def _():
        me = me_ref[0]
        copies = fetch_start((wk0, wk1, wk2, wk3), wk_ref, sems, 0, me)
        copies += fetch_start((wv0, wv1, wv2, wv3), wv_ref, sems, 4, me)
        copies += fetch_start((wq0, wq1, wq2, wq3), wq_ref, sems, 8, me)
        fetch_wait(copies)
        query = jnp.dot(x_ref[...], wq_ref[...], preferred_element_type=f32)
        query = (query + vec_ref[pl.ds(VEC_QUERY, 1), :]).astype(bf16).astype(f32)
        q_ref[...] = (query * (1.0 / math.sqrt(HEAD_DIM))).astype(bf16)

    rows = all_ref[...]
    k_ref[...] = jnp.dot(rows, wk_ref[...], preferred_element_type=f32).astype(bf16)
    value = jnp.dot(rows, wv_ref[...], preferred_element_type=f32)
    v_ref[...] = (value + vec_ref[pl.ds(VEC_VALUE, 1), :]).astype(bf16)
    all_t_ref[...] = rows.T


def project(me, x_in, x_all, vecs, wq, wk, wv):
    tok, width = x_in.shape
    seq = x_all.shape[0]
    rows = 256
    whole = lambda v: pl.BlockSpec(v.shape, lambda i: (0, 0), pipeline_mode=pl.Buffered(1))
    block = pl.BlockSpec((rows, width), lambda i: (i, 0))
    shape = jax.ShapeDtypeStruct
    return pl.pallas_call(
        project_kernel,
        grid=(seq // rows,),
        in_specs=[spec(pltpu.SMEM), whole(x_in), block, whole(vecs)] + [spec(pltpu.HBM)] * 12,
        out_specs=[
            pl.BlockSpec((tok, width), lambda i: (0, 0)),
            block,
            block,
            pl.BlockSpec((width, rows), lambda i: (0, i)),
        ],
        out_shape=[
            shape((tok, width), bf16), shape((seq, width), bf16), shape((seq, width), bf16),
            shape((width, seq), bf16),
        ],
        scratch_shapes=[pltpu.VMEM((width, width), bf16)] * 3 + [pltpu.SemaphoreType.DMA((12,))],
        compiler_params=pltpu.CompilerParams(vmem_limit_bytes=VMEM_LIMIT),
        cost_estimate=NO_COST,
        name="project",
    )(me, x_in, x_all, vecs, *wq, *wk, *wv)


def attend_kernel(chunks, q_ref, k_ref, v_ref, extra_ref, doc_ref, attn_ref, low_ref, low_t_ref, lse_ref, s_ref):
    rows = k_ref.shape[0] // chunks
    q_t = q_ref[...].astype(f32).T
    bias = _extra_rows(doc_ref[...])
    outs = []
    for half in range(2):
        q_aug = jnp.concatenate(
            [jnp.where(_half_mask(q_t.shape, 0, half), q_t, 0.0).astype(bf16), bias], axis=0
        )
        top = None
        for c in range(chunks):
            at = pl.ds(c * rows, rows)
            k_aug = jnp.concatenate([k_ref[at, :], extra_ref[at, :]], axis=1)
            s_now = jnp.dot(k_aug, q_aug, preferred_element_type=f32)
            s_ref[half, at, :] = s_now
            top_now = jnp.max(s_now, axis=0, keepdims=True)
            top = top_now if top is None else jnp.maximum(top, top_now)
        total = jnp.zeros_like(top)
        mixed = jnp.zeros((2 * HEAD_DIM, q_t.shape[1]), f32)
        for c in range(chunks):
            at = pl.ds(c * rows, rows)
            p_now = jnp.exp(s_ref[half, at, :] - top)
            total = total + jnp.sum(p_now, axis=0, keepdims=True)
            mixed = mixed + cross_rows(v_ref[at, :], p_now.astype(bf16))
        lse_ref[0, pl.ds(half, 1), :] = top + jnp.log(total)
        outs.append(mixed[half * HEAD_DIM : (half + 1) * HEAD_DIM] / total)
    out_t = jnp.concatenate(outs, axis=0)
    attn_ref[...] = out_t
    low_ref[...] = out_t.T.astype(bf16)
    low_t_ref[...] = out_t.astype(bf16)


def attend(query, keys, values, extra, docs):
    tok, width = query.shape
    seq = keys.shape[0]
    lanes = 2 * HEAD_DIM
    pairs = width // lanes
    shape = jax.ShapeDtypeStruct
    return pl.pallas_call(
        functools.partial(attend_kernel, 4),
        grid=(pairs,),
        in_specs=[
            pl.BlockSpec((tok, lanes), lambda p: (0, p)),
            pl.BlockSpec((seq, lanes), lambda p: (0, p)),
            pl.BlockSpec((seq, lanes), lambda p: (0, p)),
            pl.BlockSpec((seq, lanes), lambda p: (0, 0)),
            pl.BlockSpec((1, tok), lambda p: (0, 0)),
        ],
        out_specs=[
            pl.BlockSpec((lanes, tok), lambda p: (p, 0)),
            pl.BlockSpec((tok, lanes), lambda p: (0, p)),
            pl.BlockSpec((lanes, tok), lambda p: (p, 0)),
            pl.BlockSpec((1, 2, tok), lambda p: (p, 0, 0)),
        ],
        out_shape=[
            shape((width, tok), f32), shape((tok, width), bf16), shape((width, tok), bf16),
            shape((pairs, 2, tok), f32),
        ],
        scratch_shapes=[pltpu.VMEM((2, seq, tok), f32)],
        compiler_params=pltpu.CompilerParams(vmem_limit_bytes=VMEM_LIMIT),
        cost_estimate=NO_COST,
        name="attend",
    )(query, keys, values, extra, docs)


def attend_back_kernel(
    chunks, q_ref, k_ref, v_ref, extra_ref, doc_ref, attn_ref, lse_ref, g_ref, dq_ref, dk_ref, dv_ref
):
    rows = k_ref.shape[0] // chunks
    q_low = q_ref[...]
    g_low = g_ref[...]
    q_t = q_low.astype(f32).T
    g_t = g_low.astype(f32).T
    prod = attn_ref[...] * g_t
    lanes = 2 * HEAD_DIM
    q_side, g_side, q_rows, g_rows = [], [], [], []
    for half in range(2):
        pick = _half_mask(q_t.shape, 0, half)
        delta = jnp.sum(prod[half * HEAD_DIM : (half + 1) * HEAD_DIM], axis=0, keepdims=True)
        q_side.append(
            jnp.concatenate(
                [
                    jnp.where(pick, q_t, 0.0).astype(bf16),
                    _extra_rows(doc_ref[...], -lse_ref[0, pl.ds(half, 1), :]),
                ],
                axis=0,
            )
        )
        g_side.append(
            jnp.concatenate(
                [
                    jnp.where(pick, g_t, 0.0).astype(bf16),
                    _extra_rows(jnp.full_like(doc_ref[...], -1), -delta)
                    * (lax.broadcasted_iota(jnp.int32, (128, q_t.shape[1]), 0) >= NDOC).astype(bf16),
                ],
                axis=0,
            )
        )
        pick_lane = _half_mask(q_low.shape, 1, half)
        q_rows.append(jnp.where(pick_lane, q_low.astype(f32), 0.0).astype(bf16))
        g_rows.append(jnp.where(pick_lane, g_low.astype(f32), 0.0).astype(bf16))
    q_rows = jnp.concatenate(q_rows, axis=0)
    g_rows = jnp.concatenate(g_rows, axis=0)
    dq_t = [jnp.zeros((lanes, q_t.shape[1]), f32) for half in range(2)]
    for c in range(chunks):
        at = pl.ds(c * rows, rows)
        k_now = k_ref[at, :]
        extra = extra_ref[at, :]
        k_aug = jnp.concatenate([k_now, extra], axis=1)
        v_aug = jnp.concatenate([v_ref[at, :], extra], axis=1)
        p_low, s_low = [], []
        for half in range(2):
            prob = jnp.exp(jnp.dot(k_aug, q_side[half], preferred_element_type=f32))
            slope = jnp.dot(v_aug, g_side[half], preferred_element_type=f32)
            p_low.append(prob.astype(bf16))
            s_low.append((prob * slope).astype(bf16))
            dq_t[half] = dq_t[half] + cross_rows(k_now, s_low[half])
        dk_ref[at, :] = jnp.dot(
            jnp.concatenate(s_low, axis=1), q_rows, preferred_element_type=f32
        ).astype(bf16)
        dv_ref[at, :] = jnp.dot(
            jnp.concatenate(p_low, axis=1), g_rows, preferred_element_type=f32
        ).astype(bf16)
    pick = _half_mask(q_t.shape, 0, 0)
    dq_ref[...] = (jnp.where(pick, dq_t[0], dq_t[1]).T * (1.0 / math.sqrt(HEAD_DIM))).astype(bf16)


def attend_back(query, keys, values, extra, docs, attn_t, lse, grad_attn):
    tok, width = query.shape
    seq = keys.shape[0]
    pairs = width // (2 * HEAD_DIM)
    lanes = 2 * HEAD_DIM
    return pl.pallas_call(
        functools.partial(attend_back_kernel, 4),
        grid=(pairs,),
        in_specs=[
            pl.BlockSpec((tok, lanes), lambda p: (0, p)),
            pl.BlockSpec((seq, lanes), lambda p: (0, p)),
            pl.BlockSpec((seq, lanes), lambda p: (0, p)),
            pl.BlockSpec((seq, lanes), lambda p: (0, 0)),
            pl.BlockSpec((1, tok), lambda p: (0, 0)),
            pl.BlockSpec((lanes, tok), lambda p: (p, 0)),
            pl.BlockSpec((1, 2, tok), lambda p: (p, 0, 0)),
            pl.BlockSpec((tok, lanes), lambda p: (0, p)),
        ],
        out_specs=[
            pl.BlockSpec((tok, lanes), lambda p: (0, p)),
            pl.BlockSpec((seq, lanes), lambda p: (0, p)),
            pl.BlockSpec((seq, lanes), lambda p: (0, p)),
        ],
        out_shape=[
            jax.ShapeDtypeStruct((tok, width), bf16),
            jax.ShapeDtypeStruct((seq, width), bf16),
            jax.ShapeDtypeStruct((seq, width), bf16),
        ],
        compiler_params=pltpu.CompilerParams(vmem_limit_bytes=VMEM_LIMIT),
        cost_estimate=NO_COST,
        name="attend_back",
    )(query, keys, values, extra, docs, attn_t, lse, grad_attn)


VEC_QUERY, VEC_VALUE, VEC_OUT, VEC_GAIN1, VEC_BIAS1, VEC_DOWN, VEC_GAIN2, VEC_BIAS2, VEC_UP = range(9)
VEC_POOL, VEC_CLASS = 12, 15
NO_COST = pl.CostEstimate(flops=0, transcendentals=0, bytes_accessed=0)


def spec(space=pltpu.VMEM):
    return pl.BlockSpec(memory_space=space)


def fetch_start(pieces, target, sems, first, me):
    rows = pieces[0].shape[0]
    copies = []
    for r, piece in enumerate(pieces):
        at = pl.multiple_of((me ^ r) * rows, rows)
        copy = pltpu.make_async_copy(piece, target.at[pl.ds(at, rows), :], sems.at[first + r])
        copy.start()
        copies.append(copy)
    return copies


def fetch_wait(copies):
    for copy in copies:
        copy.wait()


def norm_parts(field):
    centre = field - jnp.mean(field, axis=-1, keepdims=True)
    inv_std = lax.rsqrt(jnp.mean(centre * centre, axis=-1, keepdims=True) + norm_eps)
    return centre * inv_std, inv_std


def norm_back(grad_in, normed, inv_std, gain_row):
    scaled = grad_in * gain_row
    return inv_std * (
        scaled
        - jnp.mean(scaled, axis=-1, keepdims=True)
        - normed * jnp.mean(scaled * normed, axis=-1, keepdims=True)
    )


def column_sum(value):
    return jnp.sum(value.astype(f32), axis=0, keepdims=True)


def student_tables(mats):
    width_part = mats.shape[1] - 64
    ws = jnp.concatenate([mats[k, :width_part] for k in range(mats.shape[0])], axis=0)
    wp = jnp.concatenate([mats[k, width_part : width_part + 32] for k in range(mats.shape[0])], axis=0)
    wc = jnp.concatenate([mats[k, width_part + 32 :] for k in range(mats.shape[0])], axis=0)
    return ws, wp, wc


def halves_sum(value):
    lane = lax.broadcasted_iota(jnp.int32, value.shape, 1)
    half = value.shape[1] // POOL_HEADS
    low = jnp.sum(jnp.where(lane < half, value, 0.0), axis=1, keepdims=True)
    high = jnp.sum(jnp.where(lane < half, 0.0, value), axis=1, keepdims=True)
    return jnp.where(lane < half, low, high)


def of_docs(doc, rows):
    out = jnp.where(doc == 0, rows[0], 0.0)
    for k in range(1, NDOC):
        out = jnp.where(doc == k, rows[k], out)
    return out


def forward_kernel(
    me_ref, attn_ref, x_ref, vec_ref, mats_ref, doc_ref,
    wo0, wo1, wo2, wo3, wu0, wu1, wu2, wu3, wd0, wd1, wd2, wd3,
    hid_t_ref, normed1_ref, inv1_ref, act_ref, slope_ref,
    out_ref, normed2_ref, inv2_ref, student_ref, score_ref, part_ref,
    wo_ref, wu_ref, wd_ref, sems,
):
    me = me_ref[0]
    go_o = fetch_start((wo0, wo1, wo2, wo3), wo_ref, sems, 0, me)
    go_u = fetch_start((wu0, wu1, wu2, wu3), wu_ref, sems, 4, me)
    go_d = fetch_start((wd0, wd1, wd2, wd3), wd_ref, sems, 8, me)
    vec = lambda k: vec_ref[pl.ds(k, 1), :]
    fetch_wait(go_o)
    branch = jnp.dot(attn_ref[...], wo_ref[...], preferred_element_type=f32) + vec(VEC_OUT)
    normed, inv_std = norm_parts(x_ref[...].astype(f32) + branch)
    normed1_ref[...] = normed
    inv1_ref[...] = inv_std
    hidden = normed * vec(VEC_GAIN1) + vec(VEC_BIAS1)
    hid_t_ref[...] = hidden.T.astype(bf16)
    hid_low = hidden.astype(bf16)
    width = hidden.shape[1]
    fetch_wait(go_u)
    down = None
    for j in range(wu_ref.shape[1] // width):
        at = pl.ds(j * width, width)
        pre = jnp.dot(hid_low, wu_ref[:, at], preferred_element_type=f32) + vec(VEC_UP + j)
        cdf = 0.5 * (1.0 + lax.erf(pre * (1.0 / math.sqrt(2.0))))
        pdf = jnp.exp(-0.5 * pre * pre) * (1.0 / math.sqrt(2.0 * math.pi))
        slope_ref[:, at] = (cdf + pre * pdf).astype(bf16)
        act = (pre * cdf).astype(bf16)
        act_ref[:, at] = act
        if j == 0:
            fetch_wait(go_d)
        term = jnp.dot(act, wd_ref[at, :], preferred_element_type=f32)
        down = term if down is None else down + term
    normed, inv_std = norm_parts(hidden + (down + vec(VEC_DOWN)))
    normed2_ref[...] = normed
    inv2_ref[...] = inv_std
    out_low = (normed * vec(VEC_GAIN2) + vec(VEC_BIAS2)).astype(bf16)
    out_ref[...] = out_low
    ws, _, _ = student_tables(mats_ref[...])
    pool = ws.shape[1]
    student = jnp.dot(out_low, ws, preferred_element_type=f32) + vec(VEC_POOL)[:, :pool]
    student_ref[...] = student
    scale = 1.0 / math.sqrt(pool // POOL_HEADS)
    score = halves_sum(student * vec(VEC_POOL + 1)[:, :pool]) * scale
    score_ref[...] = score
    doc = doc_ref[...]
    tops = [
        jnp.max(jnp.where(doc == k, score, big_negative), axis=0, keepdims=True) for k in range(NDOC)
    ]
    weight = jnp.exp(score - of_docs(doc, tops))
    mixed = weight * student
    totals = [jnp.sum(jnp.where(doc == k, weight, 0.0), axis=0, keepdims=True) for k in range(NDOC)]
    sums = [jnp.sum(jnp.where(doc == k, mixed, 0.0), axis=0, keepdims=True) for k in range(NDOC)]
    part_ref[...] = jnp.concatenate(tops + totals + sums + [jnp.zeros((4, pool), f32)], axis=0)


def layer_forward_call(me, attn, x_in, vecs, mats, doc, wo, wu, wd):
    tok, width = x_in.shape
    hidden = wu[0].shape[1]
    pool = mats.shape[2]
    shape = jax.ShapeDtypeStruct
    return pl.pallas_call(
        forward_kernel,
        in_specs=[spec(pltpu.SMEM)] + [spec()] * 5 + [spec(pltpu.HBM)] * 12,
        out_specs=[spec()] * 11,
        out_shape=[
            shape((width, tok), bf16), shape((tok, width), f32), shape((tok, 1), f32),
            shape((tok, hidden), bf16), shape((tok, hidden), bf16),
            shape((tok, width), bf16), shape((tok, width), f32), shape((tok, 1), f32),
            shape((tok, pool), f32), shape((tok, pool), f32), shape((16, pool), f32),
        ],
        scratch_shapes=[
            pltpu.VMEM((width, width), bf16), pltpu.VMEM((width, hidden), bf16),
            pltpu.VMEM((hidden, width), bf16), pltpu.SemaphoreType.DMA((12,)),
        ],
        compiler_params=pltpu.CompilerParams(vmem_limit_bytes=VMEM_LIMIT),
        cost_estimate=NO_COST,
        name="layer_forward",
    )(me, attn, x_in, vecs, mats, doc, *wo, *wu, *wd)


def exact_dot(left, right, dims):
    return lax.dot_general(
        left, right, (dims, ((), ())), precision=lax.Precision.HIGHEST, preferred_element_type=f32
    )


def head_kernel(
    label_ref, owner_ref, parts_ref, vec_ref, mats_ref, doc_ref, student_ref, score_ref, out_ref, cot_ref,
    normed2_ref, inv2_ref,
    down_ref, res2_ref, logits_ref, vec_grad_ref, tables_ref,
):
    vec = lambda k: vec_ref[pl.ds(k, 1), :]
    ws, wp, wc = student_tables(mats_ref[...])
    pool = ws.shape[1]
    wp, wc = wp.astype(f32), wc.astype(f32)
    tops = jnp.max(parts_ref[:, 0:NDOC, :], axis=0)
    factor = jnp.exp(parts_ref[:, 0:NDOC, :] - tops[None])
    totals = jnp.sum(parts_ref[:, NDOC : 2 * NDOC, :] * factor, axis=0)
    pooled = jnp.sum(parts_ref[:, 2 * NDOC : 3 * NDOC, :] * factor, axis=0) / totals
    pooled = jnp.concatenate([pooled, jnp.zeros((8 - NDOC, pool), f32)], axis=0)
    act = jnp.tanh(exact_dot(pooled, wp, ((1,), (0,))) + vec(VEC_POOL + 2)[:, :pool])
    logits = exact_dot(act, wc, ((1,), (0,))) + vec(VEC_CLASS)[:, :pool]
    logits_ref[...] = logits
    lane = lax.broadcasted_iota(jnp.int32, logits.shape, 1)
    row = lax.broadcasted_iota(jnp.int32, logits.shape, 0)
    shown = jnp.where(lane < CLASSES, logits, big_negative)
    shown = jnp.exp(shown - jnp.max(shown, axis=1, keepdims=True))
    grad_logits = shown / jnp.sum(shown, axis=1, keepdims=True)
    for k in range(NDOC):
        grad_logits = grad_logits - jnp.where((row == k) & (lane == label_ref[0, k]), 1.0, 0.0)
    grad_logits = jnp.where(row < NDOC, grad_logits, 0.0)
    owner = (owner_ref[0] == 0).astype(f32)
    grad_wc = exact_dot(act, grad_logits, ((0,), (0,))) * owner
    grad_pre = exact_dot(grad_logits, wc, ((1,), (1,))) * (1.0 - act * act)
    grad_wp = exact_dot(pooled, grad_pre, ((0,), (0,))) * owner
    grad_pooled = exact_dot(grad_pre, wp, ((1,), (1,)))
    doc = doc_ref[...]
    student = student_ref[...]
    each = lambda table: [table[k : k + 1] for k in range(NDOC)]
    weight = jnp.exp(score_ref[...] - of_docs(doc, each(tops))) / of_docs(doc, each(totals))
    tok_grad = of_docs(doc, each(grad_pooled))
    grad_score = weight * halves_sum(tok_grad * (student - of_docs(doc, each(pooled))))
    scale = 1.0 / math.sqrt(pool // POOL_HEADS)
    grad_student = weight * tok_grad + grad_score * vec(VEC_POOL + 1)[:, :pool] * scale
    grad_low = grad_student.astype(bf16)
    out_low = out_ref[...]
    grad_ws = cross_rows(out_low, grad_low)
    blocks, rows = mats_ref.shape[0], mats_ref.shape[1]
    high = rows - 64
    for k in range(blocks):
        tables_ref[k, 0:high, :] = grad_ws[k * high : (k + 1) * high]
        tables_ref[k, high : high + 32, :] = grad_wp[32 * k : 32 * k + 32]
        tables_ref[k, high + 32 : high + 64, :] = grad_wc[32 * k : 32 * k + 32]
    grad_layer = cot_ref[...].astype(f32) + back_mul(grad_low, ws)
    normed = normed2_ref[...]
    grad_res = norm_back(grad_layer, normed, inv2_ref[...], vec(VEC_GAIN2))
    res2_ref[...] = grad_res
    low = grad_res.astype(bf16)
    down_ref[...] = low
    width = normed.shape[1]
    wide = lambda v: jnp.concatenate([v, jnp.zeros((1, width - pool), f32)], axis=1)
    rows = [
        column_sum(low),
        column_sum(grad_layer * normed),
        column_sum(grad_layer),
        wide(column_sum(grad_low)),
        wide(column_sum(grad_score * student) * scale),
        wide(column_sum(grad_pre) * owner),
        wide(column_sum(grad_logits) * owner),
        jnp.zeros((1, width), f32),
    ]
    vec_grad_ref[...] = jnp.concatenate(rows, axis=0)


def head_call(labels, owner, parts, vecs, mats, doc, student, score, out_low, cot, normed2, inv2):
    tok, width = out_low.shape
    shape = jax.ShapeDtypeStruct
    return pl.pallas_call(
        head_kernel,
        in_specs=[spec(pltpu.SMEM)] * 2 + [spec()] * 10,
        out_specs=[spec()] * 5,
        out_shape=[
            shape((tok, width), bf16), shape((tok, width), f32), shape((8, mats.shape[2]), f32),
            shape((8, width), f32), shape(mats.shape, f32),
        ],
        compiler_params=pltpu.CompilerParams(vmem_limit_bytes=VMEM_LIMIT),
        cost_estimate=NO_COST,
        name="head",
    )(labels, owner, parts, vecs, mats, doc, student, score, out_low, cot, normed2, inv2)


def backward_kernel(
    me_ref, low_ref, res2_ref, slope_ref, normed1_ref, inv1_ref, vec_ref,
    wo0, wo1, wo2, wo3, wu0, wu1, wu2, wu3, wd0, wd1, wd2, wd3,
    up_ref, res1_ref, branch_ref, attn_ref, vec_grad_ref,
    wo_ref, wu_ref, wd_ref, sems,
):
    me = me_ref[0]
    go_d = fetch_start((wd0, wd1, wd2, wd3), wd_ref, sems, 8, me)
    go_u = fetch_start((wu0, wu1, wu2, wu3), wu_ref, sems, 4, me)
    go_o = fetch_start((wo0, wo1, wo2, wo3), wo_ref, sems, 0, me)
    low = low_ref[...]
    width = low.shape[1]
    fetch_wait(go_d)
    total = res2_ref[...]
    rows = []
    for j in range(wu_ref.shape[1] // width):
        at = pl.ds(j * width, width)
        up = (back_mul(low, wd_ref[at, :]) * slope_ref[:, at].astype(f32)).astype(bf16)
        up_ref[:, at] = up
        rows.append(column_sum(up))
        if j == 0:
            fetch_wait(go_u)
        total = total + back_mul(up, wu_ref[:, at])
    normed = normed1_ref[...]
    rows += [column_sum(total * normed), column_sum(total)]
    grad_res = norm_back(total, normed, inv1_ref[...], vec_ref[pl.ds(VEC_GAIN1, 1), :])
    res1_ref[...] = grad_res
    branch = grad_res.astype(bf16)
    branch_ref[...] = branch
    rows += [column_sum(branch), jnp.zeros((1, width), f32)]
    vec_grad_ref[...] = jnp.concatenate(rows, axis=0)
    fetch_wait(go_o)
    attn_ref[...] = back_mul(branch, wo_ref[...]).astype(bf16)


def layer_backward_call(me, low, res2, slope, normed1, inv1, vecs, wo, wu, wd):
    tok, width = low.shape
    hidden = wu[0].shape[1]
    shape = jax.ShapeDtypeStruct
    return pl.pallas_call(
        backward_kernel,
        in_specs=[spec(pltpu.SMEM)] + [spec()] * 6 + [spec(pltpu.HBM)] * 12,
        out_specs=[spec()] * 5,
        out_shape=[
            shape((tok, hidden), bf16), shape((tok, width), f32), shape((tok, width), bf16),
            shape((tok, width), bf16), shape((8, width), f32),
        ],
        scratch_shapes=[
            pltpu.VMEM((width, width), bf16), pltpu.VMEM((width, hidden), bf16),
            pltpu.VMEM((hidden, width), bf16), pltpu.SemaphoreType.DMA((12,)),
        ],
        compiler_params=pltpu.CompilerParams(vmem_limit_bytes=VMEM_LIMIT),
        cost_estimate=NO_COST,
        name="layer_backward",
    )(me, low, res2, slope, normed1, inv1, vecs, *wo, *wu, *wd)


def down_grad_kernel(order_ref, act_ref, grad_ref, send_ref, keep_ref):
    term = cross_rows(act_ref[...], grad_ref[...]).astype(bf16)
    half = send_ref.shape[0]

    @pl.when(pl.program_id(0) < pl.num_programs(0) // 2)
    def _():
        send_ref[0] = term

    @pl.when(pl.program_id(0) >= pl.num_programs(0) // 2)
    def _():
        keep_ref[0] = term


def send_keep_specs(block):
    nd = len(block)
    zero = (0,) * (nd - 1)
    return [
        pl.BlockSpec(block, lambda i, s: (jnp.minimum(i, 1),) + zero),
        pl.BlockSpec(block, lambda i, s: (jnp.maximum(i - 2, 0),) + zero),
    ]


def down_grad(blocks, act, grad):
    tok, hidden = act.shape
    width = grad.shape[1]
    part = hidden // 4
    shape = jax.ShapeDtypeStruct((2, part, width), bf16)
    return pl.pallas_call(
        down_grad_kernel,
        grid_spec=pltpu.PrefetchScalarGridSpec(
            num_scalar_prefetch=1,
            grid=(4,),
            in_specs=[
                pl.BlockSpec((tok, part), lambda i, s: (0, s[i])),
                pl.BlockSpec((tok, width), lambda i, s: (0, 0)),
            ],
            out_specs=send_keep_specs((1, part, width)),
        ),
        out_shape=[shape, shape],
        compiler_params=pltpu.CompilerParams(vmem_limit_bytes=VMEM_LIMIT),
        cost_estimate=NO_COST,
        name="down_grad",
    )(blocks, act, grad)


def middle_grad_kernel(order_ref, hid_ref, up_ref, attn_ref, branch_ref, tables_ref, vec_a_ref, vec_b_ref, send_ref, keep_ref):
    part = attn_ref.shape[0]
    width = branch_ref.shape[1]
    pool = tables_ref.shape[2]
    half = width // 2

    def put(out):
        base = 0
        for j in range(up_ref.shape[1] // width):
            out[0, base : base + part, :] = jnp.dot(
                hid_ref[...], up_ref[:, j * width : (j + 1) * width], preferred_element_type=f32
            ).astype(bf16)
            base += part
        out[0, base : base + part, :] = jnp.dot(
            attn_ref[...], branch_ref[...], preferred_element_type=f32
        ).astype(bf16)
        base += part
        high = tables_ref.shape[1] - 64
        step = high * pool // width
        out[0, base : base + step, :] = jnp.concatenate(
            [tables_ref[0, k * step : (k + 1) * step, :] for k in range(width // pool)], axis=1
        ).astype(bf16)
        rows = jnp.concatenate([vec_a_ref[...], vec_b_ref[...]], axis=0)
        rows = jnp.concatenate([rows[:, :half], rows[:, half:]], axis=0)
        out[0, base + step : base + step + 32, :] = jnp.concatenate(
            [
                tables_ref[0, high : high + 32, :],
                tables_ref[0, high + 32 : high + 64, :],
                rows,
                jnp.zeros((32, width - 2 * pool - half), f32),
            ],
            axis=1,
        ).astype(bf16)

    pl.when(pl.program_id(0) < 2)(lambda: put(send_ref))
    pl.when(pl.program_id(0) >= 2)(lambda: put(keep_ref))


def middle_grad(blocks, hid_t, up, attn_t, branch, tables, vec_a, vec_b):
    width, tok = attn_t.shape
    part = width // 4
    hidden = up.shape[1]
    rows = hidden // 4 + part + 64
    shape = jax.ShapeDtypeStruct((2, rows, width), bf16)
    return pl.pallas_call(
        middle_grad_kernel,
        grid_spec=pltpu.PrefetchScalarGridSpec(
            num_scalar_prefetch=1,
            grid=(4,),
            in_specs=[
                pl.BlockSpec((part, tok), lambda i, s: (s[i], 0)),
                pl.BlockSpec((tok, hidden), lambda i, s: (0, 0)),
                pl.BlockSpec((part, tok), lambda i, s: (s[i], 0)),
                pl.BlockSpec((tok, width), lambda i, s: (0, 0)),
                pl.BlockSpec((1,) + tables.shape[1:], lambda i, s: (s[i], 0, 0)),
                pl.BlockSpec(vec_a.shape, lambda i, s: (0, 0)),
                pl.BlockSpec(vec_b.shape, lambda i, s: (0, 0)),
            ],
            out_specs=send_keep_specs((1, rows, width)),
        ),
        out_shape=[shape, shape],
        compiler_params=pltpu.CompilerParams(vmem_limit_bytes=VMEM_LIMIT),
        cost_estimate=NO_COST,
        name="middle_grad",
    )(blocks, hid_t, up, attn_t, branch, tables, vec_a, vec_b)


def last_grad_kernel(order_ref, xt_ref, xt_all_ref, dq_ref, dk_ref, dv_ref, send_ref, keep_ref):
    part = xt_ref.shape[0]

    def put(out):
        for k, (left, right) in enumerate(((xt_ref, dq_ref), (xt_all_ref, dk_ref), (xt_all_ref, dv_ref))):
            out[0, k * part : (k + 1) * part, :] = jnp.dot(
                left[...], right[...], preferred_element_type=f32
            ).astype(bf16)
        width = dq_ref.shape[1]
        rows = jnp.concatenate(
            [column_sum(dq_ref[...]), column_sum(dv_ref[...]), jnp.zeros((62, width), f32)], axis=0
        )
        out[0, 3 * part :, :] = rows.astype(bf16)

    pl.when(pl.program_id(0) < 2)(lambda: put(send_ref))
    pl.when(pl.program_id(0) >= 2)(lambda: put(keep_ref))


def last_grad(blocks, position, x_all_t, dq, dk, dv):
    tok = dq.shape[0]
    width, seq = x_all_t.shape
    part = width // 4
    rows = 3 * part + 64
    shape = jax.ShapeDtypeStruct((2, rows, width), bf16)
    whole = lambda r: pl.BlockSpec((r, width), lambda i, s: (0, 0), pipeline_mode=pl.Buffered(1))
    return pl.pallas_call(
        last_grad_kernel,
        grid_spec=pltpu.PrefetchScalarGridSpec(
            num_scalar_prefetch=1,
            grid=(4,),
            in_specs=[
                pl.BlockSpec((part, tok), lambda i, s: (s[i], s[4])),
                pl.BlockSpec((part, seq), lambda i, s: (s[i], 0)),
                whole(tok),
                whole(seq),
                whole(seq),
            ],
            out_specs=send_keep_specs((1, rows, width)),
        ),
        out_shape=[shape, shape],
        compiler_params=pltpu.CompilerParams(vmem_limit_bytes=VMEM_LIMIT),
        cost_estimate=NO_COST,
        name="last_grad",
    )(jnp.concatenate([blocks, position]), x_all_t, x_all_t, dq, dk, dv)


def others_kernel(
    order_ref, me_ref, dk_ref, dv_ref, wk0, wk1, wk2, wk3, wv0, wv1, wv2, wv3,
    send_ref, keep_ref, wk_ref, wv_ref, sems,
):
    @pl.when(pl.program_id(0) == 0)
    def _():
        copies = fetch_start((wk0, wk1, wk2, wk3), wk_ref, sems, 0, me_ref[0])
        copies += fetch_start((wv0, wv1, wv2, wv3), wv_ref, sems, 4, me_ref[0])
        fetch_wait(copies)

    term = (back_mul(dk_ref[...], wk_ref[...]) + back_mul(dv_ref[...], wv_ref[...])).astype(bf16)
    half = pl.num_programs(0) // 2

    @pl.when(pl.program_id(0) < half)
    def _():
        send_ref[0] = term

    @pl.when(pl.program_id(0) >= half)
    def _():
        keep_ref[0] = term


def others_call(mine, me, dk, dv, wk, wv, rows):
    seq, width = dk.shape
    half = seq // rows // 2
    at = jnp.arange(half, dtype=jnp.int32)
    order = jnp.concatenate([2 * at + 1 - mine, 2 * at + mine]).astype(jnp.int32)
    block = pl.BlockSpec((rows, width), lambda i, s: (s[i], 0))
    shape = jax.ShapeDtypeStruct((half, rows, width), bf16)
    return pl.pallas_call(
        others_kernel,
        grid_spec=pltpu.PrefetchScalarGridSpec(
            num_scalar_prefetch=1,
            grid=(2 * half,),
            in_specs=[spec(pltpu.SMEM), block, block] + [spec(pltpu.HBM)] * 8,
            out_specs=[
                pl.BlockSpec((1, rows, width), lambda i, s: (jnp.minimum(i, half - 1), 0, 0)),
                pl.BlockSpec((1, rows, width), lambda i, s: (jnp.maximum(i - half, 0), 0, 0)),
            ],
            scratch_shapes=[
                pltpu.VMEM((width, width), bf16), pltpu.VMEM((width, width), bf16), pltpu.SemaphoreType.DMA((8,)),
            ],
        ),
        out_shape=[shape, shape],
        compiler_params=pltpu.CompilerParams(vmem_limit_bytes=VMEM_LIMIT),
        cost_estimate=NO_COST,
        name="others",
    )(order, me, dk, dv, *wk, *wv)


def pack_kernel(me_ref, *refs):
    vectors, (up_ref, bs_ref, qp_ref, bp_ref, bc_ref), out_ref = refs[:8], refs[8:13], refs[13]
    part = vectors[0].shape[1]
    small = bs_ref.shape[1]
    width = out_ref.shape[1]
    out_ref[...] = jnp.zeros(out_ref.shape, f32)
    for k in range(width // part):

        @pl.when(me_ref[0] == k)
        def _():
            for row, ref in enumerate(vectors):
                out_ref[row : row + 1, k * part : (k + 1) * part] = ref[...].astype(f32)
            out_ref[VEC_UP + k : VEC_UP + k + 1, :] = up_ref[...].astype(f32)
            for row, ref in enumerate((bs_ref, qp_ref, bp_ref)):
                out_ref[VEC_POOL + row : VEC_POOL + row + 1, k * small : (k + 1) * small] = ref[...].astype(f32)
            if k == 0:
                out_ref[VEC_CLASS : VEC_CLASS + 1, 0:CLASSES] = bc_ref[...].astype(f32)


def pack_call(me, vectors, up, pools, classes, width):
    operands = [v.reshape(1, -1) for v in vectors + [up] + pools + [classes]]
    return pl.pallas_call(
        pack_kernel,
        in_specs=[spec(pltpu.SMEM)] + [spec()] * len(operands),
        out_specs=spec(),
        out_shape=jax.ShapeDtypeStruct((16, width), f32),
        cost_estimate=NO_COST,
        name="pack",
    )(me, *operands)


def swap(value, axis, bit):
    count = lax.axis_size(axis)
    return lax.ppermute(value, axis, [(i, i ^ bit) for i in range(count)])


def join_far(shard):
    return double(shard, "fsdp", 2)


def join_core(column):
    core = lax.axis_index("fsdp") % 2
    across = swap(column, "fsdp", 1)
    full = jnp.where(
        core == 0, jnp.stack([column, across], axis=1), jnp.stack([across, column], axis=1)
    )
    return full.reshape(-1, column.shape[-1])


def bits_of(axis):
    return [1 << k for k in range(lax.axis_size(axis).bit_length() - 1)]


def tie(*values):
    return lax.optimization_barrier(values)


class Box:
    def __init__(self, keep):
        self.keep = keep


class Order:
    def __init__(self, holder):
        self.holder = holder

    def after(self, value):
        value, self.holder.keep = tie(value, self.holder.keep)
        return value

    def pin(self, value):
        box = Box(self.after(value))
        self.holder = box
        return box


class Sum:
    def __init__(self, keep, send, steps):
        self.keep, self.send, self.todo = keep, send, steps

    @staticmethod
    def mine(step):
        index = lax.axis_index(step[1])
        out = 0
        for k, bit in enumerate(step[2]):
            out = out + ((index // bit) % 2) * (1 << k)
        return out

    @staticmethod
    def shift(step, r):
        return sum(bit for k, bit in enumerate(step[2]) if (r >> k) & 1)

    def begin(self):
        step = self.todo[0]
        self.got = [swap(v, step[1], self.shift(step, r + 1)) for r, v in enumerate(self.send)]

    def end(self, order):
        step = self.todo.pop(0)
        got = list(self.got)
        got[-1] = order.after(got[-1])
        order.holder = self
        n = self.keep.shape[-1]
        if step[0] == "gather":
            mine = self.mine(step)
            rows = self.keep.shape[0]
            out = jnp.zeros(((len(got) + 1) * rows, n), bf16)
            for r, v in enumerate([self.keep] + got):
                out = lax.dynamic_update_slice_in_dim(out, v, (mine ^ r) * rows, axis=0)
            self.keep = out
        else:
            parts = [self.keep] + got

            def total(pick):
                out = pick(parts[0]).astype(f32)
                for v in parts[1:]:
                    out = out + pick(v).astype(f32)
                return out.astype(bf16)

            following = self.todo[0] if self.todo else None
            if following is not None and following[0] == "scatter":
                mine = self.mine(following)
                ways, rows = 1 << len(following[2]), following[3]

                def piece(r):
                    return lambda v: lax.dynamic_index_in_dim(
                        v.reshape(-1, ways, rows, n), mine ^ r, 1, keepdims=False
                    )

                self.send = [total(piece(r)) for r in range(1, ways)]
                self.keep = total(piece(0))
                return
            self.keep = total(lambda v: v.reshape(-1, n))
        if self.todo:
            self.send = [self.keep] * ((1 << len(self.todo[0][2])) - 1)

    def step(self, order):
        self.end(order)
        if self.todo:
            self.begin()


def bits_of(axis):
    return [1 << k for k in range(lax.axis_size(axis).bit_length() - 1)]


def double(value, axis, bit):
    mine = (lax.axis_index(axis) // bit) % 2
    got = swap(value, axis, bit)
    return jnp.where(mine == 0, jnp.stack([value, got]), jnp.stack([got, value]))


def rounds_of(axis):
    return [(bit,) for bit in bits_of(axis)]


def grad_steps(rows):
    steps = [("scatter", "fsdp", (1,), rows), ("scatter", "fsdp", (2,), rows)]
    for bits in rounds_of("ctx"):
        rows >>= len(bits)
        steps.append(("scatter", "ctx", bits, rows))
    return steps + [("gather", "ctx", bits, 0) for bits in rounds_of("ctx")[::-1]]


def shards(
    tokens,
    starts,
    labels,
    cotangent,
    w_query,
    b_query,
    w_key,
    w_value,
    b_value,
    w_out,
    b_out,
    norm1_gain,
    norm1_bias,
    w_up,
    b_up,
    w_down,
    b_down,
    norm2_gain,
    norm2_bias,
    w_student,
    b_student,
    pool_query,
    w_pool,
    b_pool,
    w_class,
    b_class,
):
    cycle_size = lax.axis_size("ctx")
    cycle_index = lax.axis_index("ctx")
    fsdp_size = lax.axis_size("fsdp")
    me = lax.axis_index("fsdp")
    me_row = me.reshape(1).astype(jnp.int32)
    tok_rows = tokens.shape[1]
    width = tokens.shape[2]
    part = width // fsdp_size
    hidden_part = b_up.shape[0]
    pool_width = w_pool.shape[1]
    seq_total = tok_rows * cycle_size
    score_scale = 1.0 / math.sqrt(HEAD_DIM)
    starts_row = starts[0]
    x_in = tokens[0]
    x_all = lax.all_gather(x_in, "ctx", axis=0, tiled=True)

    def pieces(shard, far):
        return [shard, swap(shard, "fsdp", 1), far, swap(far, "fsdp", 1)]

    far_wk, far_wv, far_wq = swap(w_key, "fsdp", 2), swap(w_value, "fsdp", 2), swap(w_query, "fsdp", 2)
    mats = jnp.concatenate([w_student, w_pool, jnp.pad(w_class, ((0, 0), (0, pool_width - CLASSES)))], axis=0)
    vectors = [b_query, b_value, b_out, norm1_gain, norm1_bias, b_down, norm2_gain, norm2_bias]
    vecs = pack_call(me_row, vectors, b_up, [b_student, pool_query, b_pool], b_class, width)
    far_vecs, mats = swap(vecs, "fsdp", 2), join_far(mats)
    far_wk, far_wv, far_wq, far_vecs, mats, w_out, w_up = tie(
        far_wk, far_wv, far_wq, far_vecs, mats, w_out, w_up
    )
    vecs = vecs + far_vecs
    vecs = vecs + swap(vecs, "fsdp", 1)
    far_wo, far_w1 = swap(w_out, "fsdp", 2), swap(w_up, "fsdp", 2)
    piece_wk, piece_wv, piece_wq = pieces(w_key, far_wk), pieces(w_value, far_wv), pieces(w_query, far_wq)
    mats = join_core(mats).reshape(fsdp_size, -1, pool_width)
    x_all, far_wo, far_w1, mats, w_down = tie(x_all, far_wo, far_w1, mats, w_down)
    far_w2 = swap(w_down, "fsdp", 2)
    piece_wo, piece_w1 = pieces(w_out, far_wo), pieces(w_up, far_w1)

    local_pos = cycle_index * tok_rows + jnp.arange(tok_rows, dtype=jnp.int32)
    local_doc = doc_of(local_pos, starts_row)
    all_doc = doc_of(jnp.arange(seq_total, dtype=jnp.int32), starts_row)
    at = jnp.arange(128, dtype=jnp.int32)[None, :]
    extra = ((at == all_doc[:, None]) | ((at >= NDOC) & (at < NDOC + 3))).astype(bf16)
    docs = local_doc[None, :]
    doc_column = local_doc[:, None]

    query_s, key_b, value_b, x_all_t = project(me_row, x_in, x_all, vecs, piece_wq, piece_wk, piece_wv)
    attn_t, attn_b, attn_low_t, lse = attend(query_s, key_b, value_b, extra, docs)
    attn_b, far_w2 = tie(attn_b, far_w2)
    piece_w2 = pieces(w_down, far_w2)

    hid_t, normed1, inv1, act, slope, out_b, normed2, inv2, student, score, local = layer_forward_call(
        me_row, attn_b, x_in, vecs, mats, doc_column, piece_wo, piece_w1, piece_w2
    )
    parts = lax.all_to_all(
        jnp.broadcast_to(local[None], (cycle_size,) + local.shape), "ctx", 0, 0, tiled=True
    )
    owner = cycle_index.reshape(1).astype(jnp.int32)
    grad_down_b, grad_res2, logits, vec_a, tables = head_call(
        labels, owner, parts, vecs, mats, doc_column, student, score, out_b, cotangent[0], normed2, inv2
    )
    logits = logits[:NDOC, :CLASSES]

    core = me % 2
    blocks = jnp.stack([1 - core, 3 - core, core, 2 + core]).astype(jnp.int32)

    def grad_sum(pair):
        return Sum(pair[1], [pair[0]], grad_steps(pair[0].shape[1]))

    sum_w2 = grad_sum(down_grad(blocks, act, grad_down_b))
    sum_w2.begin()
    grad_up_b, grad_res1, grad_branch_b, grad_attn_b, vec_b = layer_backward_call(
        me_row, grad_down_b, grad_res2, slope, normed1, inv1, vecs, piece_wo, piece_w1, piece_w2
    )
    order = Order(Box(grad_attn_b))
    attn_box = order.holder
    sum_w2.step(order)
    sum_mid = grad_sum(
        middle_grad(blocks, hid_t, grad_up_b, attn_low_t, grad_branch_b, tables, vec_a, vec_b)
    )
    sum_mid.begin()
    grad_attn_b = order.after(attn_box.keep)
    grad_query_b, grad_key_b, grad_value_b = attend_back(
        query_s, key_b, value_b, extra, docs, attn_t, lse, grad_attn_b
    )
    key_box = order.pin(grad_key_b)
    sum_mid.step(order)
    sum_w2.step(order)
    grad_query_b = order.after(grad_query_b)
    send, keep = last_grad(blocks, cycle_index.reshape(1), x_all_t, grad_query_b, key_box.keep, grad_value_b)
    sum_last = Sum(keep, [send], grad_steps(send.shape[1]))
    sum_last.keep = order.after(sum_last.keep)
    order.holder = sum_last
    sum_last.begin()
    grad_value_b = order.after(grad_value_b)
    send, keep = others_call(
        cycle_index % 2, me_row, key_box.keep, grad_value_b, piece_wk, piece_wv, tok_rows
    )
    sum_others = Sum(keep, [send], [("scatter", "ctx", bits, tok_rows) for bits in rounds_of("ctx")])
    sum_others.keep = order.after(sum_others.keep)
    order.holder = sum_others
    sum_others.begin()
    waves = [sum_w2, sum_mid, sum_others, sum_last]
    plan = PLAN if cycle_size == 8 else []
    for k in plan:
        if waves[k].todo:
            waves[k].step(order)
    while any(w.todo for w in waves):
        for w in waves:
            if w.todo:
                w.step(order)

    near = jnp.concatenate([back_mul(grad_query_b, w)[None] for w in piece_wq])
    near = jnp.concatenate([lax.dynamic_index_in_dim(near, me ^ r, 0, keepdims=False) for r in range(fsdp_size)], axis=1)
    grad_tokens = grad_res1 + near
    grad_tokens = grad_tokens + sum_others.keep.reshape(tok_rows, width).astype(f32)
    middle = sum_mid.keep.astype(f32)
    ups_sum, middle = middle[:hidden_part], middle[hidden_part:]
    last = sum_last.keep.astype(f32)
    done_wo = middle[:part]
    high = part * pool_width // width
    tall = middle[part : part + high]
    done_ws = jnp.concatenate(jnp.split(tall, width // pool_width, axis=1), axis=0)
    rest = middle[part + high :]
    done_wp = rest[:, :pool_width]
    done_wc = rest[:, pool_width : pool_width + CLASSES]
    base = 2 * pool_width
    half = width // 2
    rows = jnp.concatenate([rest[:16, base : base + half], rest[16:, base : base + half]], axis=1)
    own = lax.dynamic_slice_in_dim(rows, me * part, part, axis=1)
    pools = lax.dynamic_slice_in_dim(rows[3:6], me * w_pool.shape[0], w_pool.shape[0], axis=1)
    done_bc = rows[6, :CLASSES]
    done_c1 = lax.dynamic_index_in_dim(rows, 8 + me, 0, keepdims=False)
    late = lax.dynamic_slice_in_dim(last[3 * part : 3 * part + 8], me * part, part, axis=1)
    done_w1 = jnp.concatenate(jnp.split(ups_sum, hidden_part // part, axis=0), axis=1)
    return (
        out_b[None],
        logits[None],
        grad_tokens[None],
        last[:part],
        late[0],
        last[part : 2 * part],
        last[2 * part : 3 * part],
        late[1],
        done_wo,
        own[14],
        own[12],
        own[13],
        done_w1,
        done_c1,
        sum_w2.keep.astype(f32),
        own[0],
        own[1],
        own[2],
        done_ws,
        pools[0],
        pools[1],
        done_wp,
        pools[2],
        done_wc,
        done_bc,
    )


def solution(mesh):
    in_specs = (
        P("fsdp", "ctx", None),
        P("fsdp", None),
        P("fsdp", None),
        P("fsdp", "ctx", None),
        P("fsdp", None),
        P("fsdp"),
        P("fsdp", None),
        P("fsdp", None),
        P("fsdp"),
        P("fsdp", None),
        P("fsdp"),
        P("fsdp"),
        P("fsdp"),
        P("fsdp", None),
        P("fsdp"),
        P("fsdp", None),
        P("fsdp"),
        P("fsdp"),
        P("fsdp"),
        P("fsdp", None),
        P("fsdp"),
        P("fsdp"),
        P("fsdp", None),
        P("fsdp"),
        P("fsdp", None),
        P(),
    )
    out_specs = (
        P("fsdp", "ctx", None),
        P("fsdp", None, None),
        P("fsdp", "ctx", None),
        P("fsdp", None),
        P("fsdp"),
        P("fsdp", None),
        P("fsdp", None),
        P("fsdp"),
        P("fsdp", None),
        P("fsdp"),
        P("fsdp"),
        P("fsdp"),
        P("fsdp", None),
        P("fsdp"),
        P("fsdp", None),
        P("fsdp"),
        P("fsdp"),
        P("fsdp"),
        P("fsdp", None),
        P("fsdp"),
        P("fsdp"),
        P("fsdp", None),
        P("fsdp"),
        P("fsdp", None),
        P(),
    )
    return jax.shard_map(shards, mesh=mesh, in_specs=in_specs, out_specs=out_specs, check_vma=False)
```

```python
import functools
import math

import jax
import jax.numpy as jnp
from jax import lax
from jax.experimental import pallas as pl
from jax.experimental.pallas import tpu as pltpu
from jax.sharding import PartitionSpec as P

HEADS = 12
HEAD_DIM = 64
POOL_HEADS = 2
CLASSES = 14
NDOC = 4

big_negative = -1e30
norm_eps = 1e-05
f32 = jnp.float32
bf16 = jnp.bfloat16
VMEM_LIMIT = 56 * 1024 * 1024
PLAN = [0, 1, 0, 1, 0, 3, 1, 2, 0, 1, 3, 12, 1, 3, 3, 22, 0, 3, 1, 3, 30, 2, 3]


def doc_of(positions, starts_row):
    return jnp.sum((starts_row[None, :] <= positions[:, None]).astype(jnp.int32), axis=1) - 1


def cross_rows(left_mat, right_mat):
    return lax.dot_general(
        left_mat, right_mat, (((0,), (0,)), ((), ())), preferred_element_type=f32
    )


def back_mul(left_mat, right_mat):
    return lax.dot_general(
        left_mat, right_mat, (((1,), (1,)), ((), ())), preferred_element_type=f32
    )


def _half_mask(shape, axis, half):
    return (lax.broadcasted_iota(jnp.int32, shape, axis) // HEAD_DIM) == half


def _split3(row):
    hi = row.astype(bf16)
    rest = row - hi.astype(f32)
    mid = rest.astype(bf16)
    low = (rest - mid.astype(f32)).astype(bf16)
    return hi.astype(f32), mid.astype(f32), low.astype(f32)


def _extra_rows(docrow, row=None):
    at = lax.broadcasted_iota(jnp.int32, (128, docrow.shape[1]), 0)
    out = jnp.where((at < NDOC) & (at != docrow), big_negative, 0.0)
    if row is not None:
        for k, part in enumerate(_split3(row)):
            out = out + jnp.where(at == NDOC + k, part, 0.0)
    return out.astype(bf16)


def project_kernel(
    me_ref, x_ref, all_ref, vec_ref,
    wq0, wq1, wq2, wq3, wk0, wk1, wk2, wk3, wv0, wv1, wv2, wv3,
    q_ref, k_ref, v_ref, all_t_ref, wq_ref, wk_ref, wv_ref, sems,
):
    @pl.when(pl.program_id(0) == 0)
    def _():
        me = me_ref[0]
        copies = fetch_start((wk0, wk1, wk2, wk3), wk_ref, sems, 0, me)
        copies += fetch_start((wv0, wv1, wv2, wv3), wv_ref, sems, 4, me)
        copies += fetch_start((wq0, wq1, wq2, wq3), wq_ref, sems, 8, me)
        fetch_wait(copies)
        query = jnp.dot(x_ref[...], wq_ref[...], preferred_element_type=f32)
        query = (query + vec_ref[pl.ds(VEC_QUERY, 1), :]).astype(bf16).astype(f32)
        q_ref[...] = (query * (1.0 / math.sqrt(HEAD_DIM))).astype(bf16)

    rows = all_ref[...]
    k_ref[...] = jnp.dot(rows, wk_ref[...], preferred_element_type=f32).astype(bf16)
    value = jnp.dot(rows, wv_ref[...], preferred_element_type=f32)
    v_ref[...] = (value + vec_ref[pl.ds(VEC_VALUE, 1), :]).astype(bf16)
    all_t_ref[0] = rows.T


def project(me, x_in, x_all, vecs, wq, wk, wv):
    tok, width = x_in.shape
    seq = x_all.shape[0]
    rows = tok
    whole = lambda v: pl.BlockSpec(v.shape, lambda i: (0, 0), pipeline_mode=pl.Buffered(1))
    block = pl.BlockSpec((rows, width), lambda i: (i, 0))
    shape = jax.ShapeDtypeStruct
    return pl.pallas_call(
        project_kernel,
        grid=(seq // rows,),
        in_specs=[spec(pltpu.SMEM), whole(x_in), block, whole(vecs)] + [spec(pltpu.HBM)] * 12,
        out_specs=[
            pl.BlockSpec((tok, width), lambda i: (0, 0)),
            block,
            block,
            pl.BlockSpec((1, width, rows), lambda i: (i, 0, 0)),
        ],
        out_shape=[
            shape((tok, width), bf16), shape((seq, width), bf16), shape((seq, width), bf16),
            shape((seq // rows, width, rows), bf16),
        ],
        scratch_shapes=[pltpu.VMEM((width, width), bf16)] * 3 + [pltpu.SemaphoreType.DMA((12,))],
        compiler_params=pltpu.CompilerParams(vmem_limit_bytes=VMEM_LIMIT),
        cost_estimate=NO_COST,
        name="project",
    )(me, x_in, x_all, vecs, *wq, *wk, *wv)


def attend_kernel(chunks, q_ref, k_ref, v_ref, extra_ref, doc_ref, attn_ref, low_ref, low_t_ref, lse_ref, s_ref):
    rows = k_ref.shape[0] // chunks
    q_t = q_ref[...].astype(f32).T
    bias = _extra_rows(doc_ref[...])
    outs = []
    for half in range(2):
        q_aug = jnp.concatenate(
            [jnp.where(_half_mask(q_t.shape, 0, half), q_t, 0.0).astype(bf16), bias], axis=0
        )
        top = None
        for c in range(chunks):
            at = pl.ds(c * rows, rows)
            k_aug = jnp.concatenate([k_ref[at, :], extra_ref[at, :]], axis=1)
            s_now = jnp.dot(k_aug, q_aug, preferred_element_type=f32)
            s_ref[half, at, :] = s_now
            top_now = jnp.max(s_now, axis=0, keepdims=True)
            top = top_now if top is None else jnp.maximum(top, top_now)
        total = jnp.zeros_like(top)
        mixed = jnp.zeros((2 * HEAD_DIM, q_t.shape[1]), f32)
        for c in range(chunks):
            at = pl.ds(c * rows, rows)
            p_now = jnp.exp(s_ref[half, at, :] - top)
            total = total + jnp.sum(p_now, axis=0, keepdims=True)
            mixed = mixed + cross_rows(v_ref[at, :], p_now.astype(bf16))
        lse_ref[0, pl.ds(half, 1), :] = top + jnp.log(total)
        outs.append(mixed[half * HEAD_DIM : (half + 1) * HEAD_DIM] / total)
    out_t = jnp.concatenate(outs, axis=0)
    attn_ref[...] = out_t
    low_ref[...] = out_t.T.astype(bf16)
    low_t_ref[...] = out_t.astype(bf16)


def attend(query, keys, values, extra, docs):
    tok, width = query.shape
    seq = keys.shape[0]
    lanes = 2 * HEAD_DIM
    pairs = width // lanes
    shape = jax.ShapeDtypeStruct
    return pl.pallas_call(
        functools.partial(attend_kernel, 4),
        grid=(pairs,),
        in_specs=[
            pl.BlockSpec((tok, lanes), lambda p: (0, p)),
            pl.BlockSpec((seq, lanes), lambda p: (0, p)),
            pl.BlockSpec((seq, lanes), lambda p: (0, p)),
            pl.BlockSpec((seq, lanes), lambda p: (0, 0)),
            pl.BlockSpec((1, tok), lambda p: (0, 0)),
        ],
        out_specs=[
            pl.BlockSpec((lanes, tok), lambda p: (p, 0)),
            pl.BlockSpec((tok, lanes), lambda p: (0, p)),
            pl.BlockSpec((lanes, tok), lambda p: (p, 0)),
            pl.BlockSpec((1, 2, tok), lambda p: (p, 0, 0)),
        ],
        out_shape=[
            shape((width, tok), f32), shape((tok, width), bf16), shape((width, tok), bf16),
            shape((pairs, 2, tok), f32),
        ],
        scratch_shapes=[pltpu.VMEM((2, seq, tok), f32)],
        compiler_params=pltpu.CompilerParams(vmem_limit_bytes=VMEM_LIMIT),
        cost_estimate=NO_COST,
        name="attend",
    )(query, keys, values, extra, docs)


def attend_back_kernel(
    chunks, q_ref, k_ref, v_ref, extra_ref, doc_ref, attn_ref, lse_ref, g_ref, *more
):
    dq_ref, dk_ref, dv_ref = more[-3:]
    rows = k_ref.shape[0] // chunks
    q_low = q_ref[...]
    g_low = g_ref[...]
    q_t = q_low.astype(f32).T
    g_t = g_low.astype(f32).T
    prod = attn_ref[...] * g_t
    lanes = 2 * HEAD_DIM
    q_side, g_side, q_rows, g_rows = [], [], [], []
    for half in range(2):
        pick = _half_mask(q_t.shape, 0, half)
        delta = jnp.sum(prod[half * HEAD_DIM : (half + 1) * HEAD_DIM], axis=0, keepdims=True)
        q_side.append(
            jnp.concatenate(
                [
                    jnp.where(pick, q_t, 0.0).astype(bf16),
                    _extra_rows(doc_ref[...], -lse_ref[0, pl.ds(half, 1), :]),
                ],
                axis=0,
            )
        )
        g_side.append(
            jnp.concatenate(
                [
                    jnp.where(pick, g_t, 0.0).astype(bf16),
                    _extra_rows(jnp.full_like(doc_ref[...], -1), -delta)
                    * (lax.broadcasted_iota(jnp.int32, (128, q_t.shape[1]), 0) >= NDOC).astype(bf16),
                ],
                axis=0,
            )
        )
        pick_lane = _half_mask(q_low.shape, 1, half)
        q_rows.append(jnp.where(pick_lane, q_low.astype(f32), 0.0).astype(bf16))
        g_rows.append(jnp.where(pick_lane, g_low.astype(f32), 0.0).astype(bf16))
    q_rows = jnp.concatenate(q_rows, axis=0)
    g_rows = jnp.concatenate(g_rows, axis=0)
    dq_t = [jnp.zeros((lanes, q_t.shape[1]), f32) for half in range(2)]
    for c in range(chunks):
        at = pl.ds(c * rows, rows)
        k_now = k_ref[at, :]
        extra = extra_ref[at, :]
        k_aug = jnp.concatenate([k_now, extra], axis=1)
        v_aug = jnp.concatenate([v_ref[at, :], extra], axis=1)
        p_low, s_low = [], []
        for half in range(2):
            prob = jnp.exp(jnp.dot(k_aug, q_side[half], preferred_element_type=f32))
            slope = jnp.dot(v_aug, g_side[half], preferred_element_type=f32)
            p_low.append(prob.astype(bf16))
            s_low.append((prob * slope).astype(bf16))
            dq_t[half] = dq_t[half] + cross_rows(k_now, s_low[half])
        dk_ref[at, :] = jnp.dot(
            jnp.concatenate(s_low, axis=1), q_rows, preferred_element_type=f32
        ).astype(bf16)
        dv_ref[at, :] = jnp.dot(
            jnp.concatenate(p_low, axis=1), g_rows, preferred_element_type=f32
        ).astype(bf16)
    pick = _half_mask(q_t.shape, 0, 0)
    dq_ref[...] = (jnp.where(pick, dq_t[0], dq_t[1]).T * (1.0 / math.sqrt(HEAD_DIM))).astype(bf16)


def attend_back(first, pairs, so_far, query, keys, values, extra, docs, attn_t, lse, grad_attn):
    tok, width = query.shape
    seq = keys.shape[0]
    lanes = 2 * HEAD_DIM
    columns = lambda rows: pl.BlockSpec((rows, lanes), lambda p: (0, p + first))
    shape = lambda rows: jax.ShapeDtypeStruct((rows, width), bf16)
    return pl.pallas_call(
        functools.partial(attend_back_kernel, 4),
        grid=(pairs,),
        in_specs=[
            columns(tok),
            columns(seq),
            columns(seq),
            pl.BlockSpec((seq, lanes), lambda p: (0, 0)),
            pl.BlockSpec((1, tok), lambda p: (0, 0)),
            pl.BlockSpec((lanes, tok), lambda p: (p + first, 0)),
            pl.BlockSpec((1, 2, tok), lambda p: (p + first, 0, 0)),
            columns(tok),
        ]
        + [spec(pltpu.HBM)] * len(so_far),
        out_specs=[columns(tok), columns(seq), columns(seq)],
        out_shape=[shape(tok), shape(seq), shape(seq)],
        input_output_aliases={8 + k: k for k in range(len(so_far))},
        compiler_params=pltpu.CompilerParams(vmem_limit_bytes=VMEM_LIMIT),
        cost_estimate=NO_COST,
        name="attend_back",
    )(query, keys, values, extra, docs, attn_t, lse, grad_attn, *so_far)


VEC_QUERY, VEC_VALUE, VEC_OUT, VEC_GAIN1, VEC_BIAS1, VEC_DOWN, VEC_GAIN2, VEC_BIAS2, VEC_UP = range(9)
VEC_POOL, VEC_CLASS = 12, 15
NO_COST = pl.CostEstimate(flops=0, transcendentals=0, bytes_accessed=0)


def spec(space=pltpu.VMEM):
    return pl.BlockSpec(memory_space=space)


def fetch_start(pieces, target, sems, first, me):
    rows = pieces[0].shape[0]
    copies = []
    for r, piece in enumerate(pieces):
        at = pl.multiple_of((me ^ r) * rows, rows)
        copy = pltpu.make_async_copy(piece, target.at[pl.ds(at, rows), :], sems.at[first + r])
        copy.start()
        copies.append(copy)
    return copies


def fetch_wait(copies):
    for copy in copies:
        copy.wait()


def norm_parts(field):
    centre = field - jnp.mean(field, axis=-1, keepdims=True)
    inv_std = lax.rsqrt(jnp.mean(centre * centre, axis=-1, keepdims=True) + norm_eps)
    return centre * inv_std, inv_std


def norm_back(grad_in, normed, inv_std, gain_row):
    scaled = grad_in * gain_row
    return inv_std * (
        scaled
        - jnp.mean(scaled, axis=-1, keepdims=True)
        - normed * jnp.mean(scaled * normed, axis=-1, keepdims=True)
    )


def column_sum(value):
    return jnp.sum(value.astype(f32), axis=0, keepdims=True)


def student_tables(mats):
    width_part = mats.shape[1] - 64
    ws = jnp.concatenate([mats[k, :width_part] for k in range(mats.shape[0])], axis=0)
    wp = jnp.concatenate([mats[k, width_part : width_part + 32] for k in range(mats.shape[0])], axis=0)
    wc = jnp.concatenate([mats[k, width_part + 32 :] for k in range(mats.shape[0])], axis=0)
    return ws, wp, wc


def halves_sum(value):
    lane = lax.broadcasted_iota(jnp.int32, value.shape, 1)
    half = value.shape[1] // POOL_HEADS
    low = jnp.sum(jnp.where(lane < half, value, 0.0), axis=1, keepdims=True)
    high = jnp.sum(jnp.where(lane < half, 0.0, value), axis=1, keepdims=True)
    return jnp.where(lane < half, low, high)


def of_docs(doc, rows):
    out = jnp.where(doc == 0, rows[0], 0.0)
    for k in range(1, NDOC):
        out = jnp.where(doc == k, rows[k], out)
    return out


def forward_kernel(
    me_ref, attn_ref, x_ref, vec_ref, mats_ref, doc_ref,
    wo0, wo1, wo2, wo3, wu0, wu1, wu2, wu3, wd0, wd1, wd2, wd3,
    hid_t_ref, normed1_ref, inv1_ref, act_ref, slope_ref,
    out_ref, normed2_ref, inv2_ref, student_ref, score_ref, part_ref,
    wo_ref, wu_ref, wd_ref, sems,
):
    me = me_ref[0]
    go_o = fetch_start((wo0, wo1, wo2, wo3), wo_ref, sems, 0, me)
    go_u = fetch_start((wu0, wu1, wu2, wu3), wu_ref, sems, 4, me)
    go_d = fetch_start((wd0, wd1, wd2, wd3), wd_ref, sems, 8, me)
    vec = lambda k: vec_ref[pl.ds(k, 1), :]
    fetch_wait(go_o)
    branch = jnp.dot(attn_ref[...], wo_ref[...], preferred_element_type=f32) + vec(VEC_OUT)
    normed, inv_std = norm_parts(x_ref[...].astype(f32) + branch)
    normed1_ref[...] = normed
    inv1_ref[...] = inv_std
    hidden = normed * vec(VEC_GAIN1) + vec(VEC_BIAS1)
    hid_t_ref[...] = hidden.T.astype(bf16)
    hid_low = hidden.astype(bf16)
    width = hidden.shape[1]
    fetch_wait(go_u)
    down = None
    for j in range(wu_ref.shape[1] // width):
        at = pl.ds(j * width, width)
        pre = jnp.dot(hid_low, wu_ref[:, at], preferred_element_type=f32) + vec(VEC_UP + j)
        cdf = 0.5 * (1.0 + lax.erf(pre * (1.0 / math.sqrt(2.0))))
        pdf = jnp.exp(-0.5 * pre * pre) * (1.0 / math.sqrt(2.0 * math.pi))
        slope_ref[:, at] = (cdf + pre * pdf).astype(bf16)
        act = (pre * cdf).astype(bf16)
        act_ref[:, at] = act
        if j == 0:
            fetch_wait(go_d)
        term = jnp.dot(act, wd_ref[at, :], preferred_element_type=f32)
        down = term if down is None else down + term
    normed, inv_std = norm_parts(hidden + (down + vec(VEC_DOWN)))
    normed2_ref[...] = normed
    inv2_ref[...] = inv_std
    out_low = (normed * vec(VEC_GAIN2) + vec(VEC_BIAS2)).astype(bf16)
    out_ref[...] = out_low
    ws, _, _ = student_tables(mats_ref[...])
    pool = ws.shape[1]
    student = jnp.dot(out_low, ws, preferred_element_type=f32) + vec(VEC_POOL)[:, :pool]
    student_ref[...] = student
    scale = 1.0 / math.sqrt(pool // POOL_HEADS)
    score = halves_sum(student * vec(VEC_POOL + 1)[:, :pool]) * scale
    score_ref[...] = score
    doc = doc_ref[...]
    tops = [
        jnp.max(jnp.where(doc == k, score, big_negative), axis=0, keepdims=True) for k in range(NDOC)
    ]
    weight = jnp.exp(score - of_docs(doc, tops))
    mixed = weight * student
    totals = [jnp.sum(jnp.where(doc == k, weight, 0.0), axis=0, keepdims=True) for k in range(NDOC)]
    sums = [jnp.sum(jnp.where(doc == k, mixed, 0.0), axis=0, keepdims=True) for k in range(NDOC)]
    part_ref[...] = jnp.concatenate(tops + totals + sums + [jnp.zeros((4, pool), f32)], axis=0)


def layer_forward_call(me, attn, x_in, vecs, mats, doc, wo, wu, wd):
    tok, width = x_in.shape
    hidden = wu[0].shape[1]
    pool = mats.shape[2]
    shape = jax.ShapeDtypeStruct
    return pl.pallas_call(
        forward_kernel,
        in_specs=[spec(pltpu.SMEM)] + [spec()] * 5 + [spec(pltpu.HBM)] * 12,
        out_specs=[spec()] * 11,
        out_shape=[
            shape((width, tok), bf16), shape((tok, width), f32), shape((tok, 1), f32),
            shape((tok, hidden), bf16), shape((tok, hidden), bf16),
            shape((tok, width), bf16), shape((tok, width), f32), shape((tok, 1), f32),
            shape((tok, pool), f32), shape((tok, pool), f32), shape((16, pool), f32),
        ],
        scratch_shapes=[
            pltpu.VMEM((width, width), bf16), pltpu.VMEM((width, hidden), bf16),
            pltpu.VMEM((hidden, width), bf16), pltpu.SemaphoreType.DMA((12,)),
        ],
        compiler_params=pltpu.CompilerParams(vmem_limit_bytes=VMEM_LIMIT),
        cost_estimate=NO_COST,
        name="layer_forward",
    )(me, attn, x_in, vecs, mats, doc, *wo, *wu, *wd)


def exact_dot(left, right, dims):
    return lax.dot_general(
        left, right, (dims, ((), ())), precision=lax.Precision.HIGHEST, preferred_element_type=f32
    )


def head_kernel(
    label_ref, owner_ref, parts_ref, vec_ref, mats_ref, doc_ref, student_ref, score_ref, out_ref, cot_ref,
    normed2_ref, inv2_ref,
    down_ref, res2_ref, logits_ref, vec_grad_ref, tables_ref,
):
    vec = lambda k: vec_ref[pl.ds(k, 1), :]
    ws, wp, wc = student_tables(mats_ref[...])
    pool = ws.shape[1]
    wp, wc = wp.astype(f32), wc.astype(f32)
    tops = jnp.max(parts_ref[:, 0:NDOC, :], axis=0)
    factor = jnp.exp(parts_ref[:, 0:NDOC, :] - tops[None])
    totals = jnp.sum(parts_ref[:, NDOC : 2 * NDOC, :] * factor, axis=0)
    pooled = jnp.sum(parts_ref[:, 2 * NDOC : 3 * NDOC, :] * factor, axis=0) / totals
    pooled = jnp.concatenate([pooled, jnp.zeros((8 - NDOC, pool), f32)], axis=0)
    act = jnp.tanh(exact_dot(pooled, wp, ((1,), (0,))) + vec(VEC_POOL + 2)[:, :pool])
    logits = exact_dot(act, wc, ((1,), (0,))) + vec(VEC_CLASS)[:, :pool]
    logits_ref[...] = logits
    lane = lax.broadcasted_iota(jnp.int32, logits.shape, 1)
    row = lax.broadcasted_iota(jnp.int32, logits.shape, 0)
    shown = jnp.where(lane < CLASSES, logits, big_negative)
    shown = jnp.exp(shown - jnp.max(shown, axis=1, keepdims=True))
    grad_logits = shown / jnp.sum(shown, axis=1, keepdims=True)
    for k in range(NDOC):
        grad_logits = grad_logits - jnp.where((row == k) & (lane == label_ref[0, k]), 1.0, 0.0)
    grad_logits = jnp.where(row < NDOC, grad_logits, 0.0)
    owner = (owner_ref[0] == 0).astype(f32)
    grad_wc = exact_dot(act, grad_logits, ((0,), (0,))) * owner
    grad_pre = exact_dot(grad_logits, wc, ((1,), (1,))) * (1.0 - act * act)
    grad_wp = exact_dot(pooled, grad_pre, ((0,), (0,))) * owner
    grad_pooled = exact_dot(grad_pre, wp, ((1,), (1,)))
    doc = doc_ref[...]
    student = student_ref[...]
    each = lambda table: [table[k : k + 1] for k in range(NDOC)]
    weight = jnp.exp(score_ref[...] - of_docs(doc, each(tops))) / of_docs(doc, each(totals))
    tok_grad = of_docs(doc, each(grad_pooled))
    grad_score = weight * halves_sum(tok_grad * (student - of_docs(doc, each(pooled))))
    scale = 1.0 / math.sqrt(pool // POOL_HEADS)
    grad_student = weight * tok_grad + grad_score * vec(VEC_POOL + 1)[:, :pool] * scale
    grad_low = grad_student.astype(bf16)
    out_low = out_ref[...]
    grad_ws = cross_rows(out_low, grad_low)
    blocks, rows = mats_ref.shape[0], mats_ref.shape[1]
    high = rows - 64
    for k in range(blocks):
        tables_ref[k, 0:high, :] = grad_ws[k * high : (k + 1) * high]
        tables_ref[k, high : high + 32, :] = grad_wp[32 * k : 32 * k + 32]
        tables_ref[k, high + 32 : high + 64, :] = grad_wc[32 * k : 32 * k + 32]
    grad_layer = cot_ref[...].astype(f32) + back_mul(grad_low, ws)
    normed = normed2_ref[...]
    grad_res = norm_back(grad_layer, normed, inv2_ref[...], vec(VEC_GAIN2))
    res2_ref[...] = grad_res
    low = grad_res.astype(bf16)
    down_ref[...] = low
    width = normed.shape[1]
    wide = lambda v: jnp.concatenate([v, jnp.zeros((1, width - pool), f32)], axis=1)
    rows = [
        column_sum(low),
        column_sum(grad_layer * normed),
        column_sum(grad_layer),
        wide(column_sum(grad_low)),
        wide(column_sum(grad_score * student) * scale),
        wide(column_sum(grad_pre) * owner),
        wide(column_sum(grad_logits) * owner),
        jnp.zeros((1, width), f32),
    ]
    vec_grad_ref[...] = jnp.concatenate(rows, axis=0)


def head_call(labels, owner, parts, vecs, mats, doc, student, score, out_low, cot, normed2, inv2):
    tok, width = out_low.shape
    shape = jax.ShapeDtypeStruct
    return pl.pallas_call(
        head_kernel,
        in_specs=[spec(pltpu.SMEM)] * 2 + [spec()] * 10,
        out_specs=[spec()] * 5,
        out_shape=[
            shape((tok, width), bf16), shape((tok, width), f32), shape((8, mats.shape[2]), f32),
            shape((8, width), f32), shape(mats.shape, f32),
        ],
        compiler_params=pltpu.CompilerParams(vmem_limit_bytes=VMEM_LIMIT),
        cost_estimate=NO_COST,
        name="head",
    )(labels, owner, parts, vecs, mats, doc, student, score, out_low, cot, normed2, inv2)


def backward_kernel(
    me_ref, low_ref, res2_ref, slope_ref, normed1_ref, inv1_ref, vec_ref,
    wo0, wo1, wo2, wo3, wu0, wu1, wu2, wu3, wd0, wd1, wd2, wd3,
    up_ref, res1_ref, branch_ref, attn_ref, vec_grad_ref,
    wo_ref, wu_ref, wd_ref, sems,
):
    me = me_ref[0]
    go_d = fetch_start((wd0, wd1, wd2, wd3), wd_ref, sems, 8, me)
    go_u = fetch_start((wu0, wu1, wu2, wu3), wu_ref, sems, 4, me)
    go_o = fetch_start((wo0, wo1, wo2, wo3), wo_ref, sems, 0, me)
    low = low_ref[...]
    width = low.shape[1]
    fetch_wait(go_d)
    total = res2_ref[...]
    rows = []
    for j in range(wu_ref.shape[1] // width):
        at = pl.ds(j * width, width)
        up = (back_mul(low, wd_ref[at, :]) * slope_ref[:, at].astype(f32)).astype(bf16)
        up_ref[:, at] = up
        rows.append(column_sum(up))
        if j == 0:
            fetch_wait(go_u)
        total = total + back_mul(up, wu_ref[:, at])
    normed = normed1_ref[...]
    rows += [column_sum(total * normed), column_sum(total)]
    grad_res = norm_back(total, normed, inv1_ref[...], vec_ref[pl.ds(VEC_GAIN1, 1), :])
    res1_ref[...] = grad_res
    branch = grad_res.astype(bf16)
    branch_ref[...] = branch
    rows += [column_sum(branch), jnp.zeros((1, width), f32)]
    vec_grad_ref[...] = jnp.concatenate(rows, axis=0)
    fetch_wait(go_o)
    attn_ref[...] = back_mul(branch, wo_ref[...]).astype(bf16)


def layer_backward_call(me, low, res2, slope, normed1, inv1, vecs, wo, wu, wd):
    tok, width = low.shape
    hidden = wu[0].shape[1]
    shape = jax.ShapeDtypeStruct
    return pl.pallas_call(
        backward_kernel,
        in_specs=[spec(pltpu.SMEM)] + [spec()] * 6 + [spec(pltpu.HBM)] * 12,
        out_specs=[spec()] * 5,
        out_shape=[
            shape((tok, hidden), bf16), shape((tok, width), f32), shape((tok, width), bf16),
            shape((tok, width), bf16), shape((8, width), f32),
        ],
        scratch_shapes=[
            pltpu.VMEM((width, width), bf16), pltpu.VMEM((width, hidden), bf16),
            pltpu.VMEM((hidden, width), bf16), pltpu.SemaphoreType.DMA((12,)),
        ],
        compiler_params=pltpu.CompilerParams(vmem_limit_bytes=VMEM_LIMIT),
        cost_estimate=NO_COST,
        name="layer_backward",
    )(me, low, res2, slope, normed1, inv1, vecs, *wo, *wu, *wd)


def down_grad_kernel(order_ref, act_ref, grad_ref, send_ref, keep_ref):
    term = cross_rows(act_ref[...], grad_ref[...]).astype(bf16)
    half = send_ref.shape[0]

    @pl.when(pl.program_id(0) < pl.num_programs(0) // 2)
    def _():
        send_ref[0] = term

    @pl.when(pl.program_id(0) >= pl.num_programs(0) // 2)
    def _():
        keep_ref[0] = term


def send_keep_specs(block):
    nd = len(block)
    zero = (0,) * (nd - 1)
    return [
        pl.BlockSpec(block, lambda i, s: (jnp.minimum(i, 1),) + zero),
        pl.BlockSpec(block, lambda i, s: (jnp.maximum(i - 2, 0),) + zero),
    ]


def down_grad(blocks, act, grad):
    tok, hidden = act.shape
    width = grad.shape[1]
    part = hidden // 4
    shape = jax.ShapeDtypeStruct((2, part, width), bf16)
    return pl.pallas_call(
        down_grad_kernel,
        grid_spec=pltpu.PrefetchScalarGridSpec(
            num_scalar_prefetch=1,
            grid=(4,),
            in_specs=[
                pl.BlockSpec((tok, part), lambda i, s: (0, s[i])),
                pl.BlockSpec((tok, width), lambda i, s: (0, 0)),
            ],
            out_specs=send_keep_specs((1, part, width)),
        ),
        out_shape=[shape, shape],
        compiler_params=pltpu.CompilerParams(vmem_limit_bytes=VMEM_LIMIT),
        cost_estimate=NO_COST,
        name="down_grad",
    )(blocks, act, grad)


def middle_grad_kernel(order_ref, hid_ref, up_ref, attn_ref, branch_ref, tables_ref, vec_a_ref, vec_b_ref, send_ref, keep_ref):
    part = attn_ref.shape[0]
    width = branch_ref.shape[1]
    pool = tables_ref.shape[2]
    half = width // 2

    def put(out):
        base = 0
        for j in range(up_ref.shape[1] // width):
            out[0, base : base + part, :] = jnp.dot(
                hid_ref[...], up_ref[:, j * width : (j + 1) * width], preferred_element_type=f32
            ).astype(bf16)
            base += part
        out[0, base : base + part, :] = jnp.dot(
            attn_ref[...], branch_ref[...], preferred_element_type=f32
        ).astype(bf16)
        base += part
        high = tables_ref.shape[1] - 64
        step = high * pool // width
        out[0, base : base + step, :] = jnp.concatenate(
            [tables_ref[0, k * step : (k + 1) * step, :] for k in range(width // pool)], axis=1
        ).astype(bf16)
        rows = jnp.concatenate([vec_a_ref[...], vec_b_ref[...]], axis=0)
        rows = jnp.concatenate([rows[:, :half], rows[:, half:]], axis=0)
        out[0, base + step : base + step + 32, :] = jnp.concatenate(
            [
                tables_ref[0, high : high + 32, :],
                tables_ref[0, high + 32 : high + 64, :],
                rows,
                jnp.zeros((32, width - 2 * pool - half), f32),
            ],
            axis=1,
        ).astype(bf16)

    pl.when(pl.program_id(0) < 2)(lambda: put(send_ref))
    pl.when(pl.program_id(0) >= 2)(lambda: put(keep_ref))


def middle_grad(blocks, hid_t, up, attn_t, branch, tables, vec_a, vec_b):
    width, tok = attn_t.shape
    part = width // 4
    hidden = up.shape[1]
    rows = hidden // 4 + part + 64
    shape = jax.ShapeDtypeStruct((2, rows, width), bf16)
    return pl.pallas_call(
        middle_grad_kernel,
        grid_spec=pltpu.PrefetchScalarGridSpec(
            num_scalar_prefetch=1,
            grid=(4,),
            in_specs=[
                pl.BlockSpec((part, tok), lambda i, s: (s[i], 0)),
                pl.BlockSpec((tok, hidden), lambda i, s: (0, 0)),
                pl.BlockSpec((part, tok), lambda i, s: (s[i], 0)),
                pl.BlockSpec((tok, width), lambda i, s: (0, 0)),
                pl.BlockSpec((1,) + tables.shape[1:], lambda i, s: (s[i], 0, 0)),
                pl.BlockSpec(vec_a.shape, lambda i, s: (0, 0)),
                pl.BlockSpec(vec_b.shape, lambda i, s: (0, 0)),
            ],
            out_specs=send_keep_specs((1, rows, width)),
        ),
        out_shape=[shape, shape],
        compiler_params=pltpu.CompilerParams(vmem_limit_bytes=VMEM_LIMIT),
        cost_estimate=NO_COST,
        name="middle_grad",
    )(blocks, hid_t, up, attn_t, branch, tables, vec_a, vec_b)


def last_grad_kernel(order_ref, xt_ref, xt_all_ref, dq_ref, dk_ref, dv_ref, send_ref, keep_ref):
    part = xt_ref.shape[0]

    def put(out):
        for k, (left, right) in enumerate(((xt_ref, dq_ref), (xt_all_ref, dk_ref), (xt_all_ref, dv_ref))):
            out[0, k * part : (k + 1) * part, :] = jnp.dot(
                left[...], right[...], preferred_element_type=f32
            ).astype(bf16)
        width = dq_ref.shape[1]
        rows = jnp.concatenate(
            [column_sum(dq_ref[...]), column_sum(dv_ref[...]), jnp.zeros((62, width), f32)], axis=0
        )
        out[0, 3 * part :, :] = rows.astype(bf16)

    pl.when(pl.program_id(0) < 2)(lambda: put(send_ref))
    pl.when(pl.program_id(0) >= 2)(lambda: put(keep_ref))


def last_grad(blocks, position, x_all_t, dq, dk, dv):
    tok, width = dq.shape
    seq = dk.shape[0]
    x_all_t = x_all_t.transpose(1, 0, 2).reshape(width, seq)
    part = width // 4
    rows = 3 * part + 64
    shape = jax.ShapeDtypeStruct((2, rows, width), bf16)
    whole = lambda r: pl.BlockSpec((r, width), lambda i, s: (0, 0), pipeline_mode=pl.Buffered(1))
    return pl.pallas_call(
        last_grad_kernel,
        grid_spec=pltpu.PrefetchScalarGridSpec(
            num_scalar_prefetch=1,
            grid=(4,),
            in_specs=[
                pl.BlockSpec((part, tok), lambda i, s: (s[i], s[4])),
                pl.BlockSpec((part, seq), lambda i, s: (s[i], 0)),
                whole(tok),
                whole(seq),
                whole(seq),
            ],
            out_specs=send_keep_specs((1, rows, width)),
        ),
        out_shape=[shape, shape],
        compiler_params=pltpu.CompilerParams(vmem_limit_bytes=VMEM_LIMIT),
        cost_estimate=NO_COST,
        name="last_grad",
    )(jnp.concatenate([blocks, position]), x_all_t, x_all_t, dq, dk, dv)


def others_kernel(
    order_ref, me_ref, q_ref, res_ref, k_ref, v_ref,
    wk0, wk1, wk2, wk3, wv0, wv1, wv2, wv3, wq0, wq1, wq2, wq3,
    send_ref, keep_ref, near_ref, wk_ref, wv_ref, wq_ref, sems,
):
    step = pl.program_id(0)
    half = pl.num_programs(0) // 2
    start = lambda pieces, target, first: fetch_start(pieces, target, sems, first, me_ref[0])

    @pl.when(step == 0)
    def _():
        copies = start((wk0, wk1, wk2, wk3), wk_ref, 0) + start((wv0, wv1, wv2, wv3), wv_ref, 4)
        query = start((wq0, wq1, wq2, wq3), wq_ref, 8)
        fetch_wait(query)
        near_ref[...] = res_ref[...] + back_mul(q_ref[...], wq_ref[...])
        fetch_wait(copies)

    flat = lambda ref: ref[...].reshape(-1, ref.shape[-1])
    term = back_mul(flat(k_ref), wk_ref[...]) + back_mul(flat(v_ref), wv_ref[...])
    term = term.astype(bf16).reshape(send_ref.shape)

    @pl.when(step < half)
    def _():
        send_ref[...] = term

    @pl.when(step >= half)
    def _():
        keep_ref[...] = term


def others_call(order, me, dq, res, dk, dv, wk, wv, wq, rows):
    seq, width = dk.shape
    tok = res.shape[0]
    half = seq // rows // 2
    group = 2 if half % 2 == 0 else 1
    n = half // group
    block = pl.BlockSpec((group, 1, rows, width), lambda i, s: (i % n, s[i // n], 0, 0))
    whole = lambda v: pl.BlockSpec(v.shape, lambda i, s: (0, 0), pipeline_mode=pl.Buffered(1))
    shape = jax.ShapeDtypeStruct((half, rows, width), bf16)
    cut = lambda v: v.reshape(half, 2, rows, width)
    return pl.pallas_call(
        others_kernel,
        grid_spec=pltpu.PrefetchScalarGridSpec(
            num_scalar_prefetch=1,
            grid=(2 * n,),
            in_specs=[spec(pltpu.SMEM), whole(dq), whole(res), block, block] + [spec(pltpu.HBM)] * 12,
            out_specs=[
                pl.BlockSpec((group, rows, width), lambda i, s: (jnp.minimum(i, n - 1), 0, 0)),
                pl.BlockSpec((group, rows, width), lambda i, s: (jnp.maximum(i - n, 0), 0, 0)),
                pl.BlockSpec((tok, width), lambda i, s: (0, 0)),
            ],
            scratch_shapes=[pltpu.VMEM((width, width), bf16)] * 3 + [pltpu.SemaphoreType.DMA((12,))],
        ),
        out_shape=[shape, shape, jax.ShapeDtypeStruct((tok, width), f32)],
        compiler_params=pltpu.CompilerParams(vmem_limit_bytes=VMEM_LIMIT),
        cost_estimate=NO_COST,
        name="others",
    )(order, me, dq, res, cut(dk), cut(dv), *wk, *wv, *wq)


def finish_kernel(
    core_ref, me_ref, q_hbm, k_hbm, v_hbm, x_hbm, res_ref,
    wk0, wk1, wk2, wk3, wv0, wv1, wv2, wv3, wq0, wq1, wq2, wq3,
    send_ref, keep_ref, far_ref, own_ref, near_ref,
    q_ref, x_ref, k_ref, v_ref, wk_ref, wv_ref, wq_ref, term_ref, sems, block_sems,
):
    core, mine = core_ref[0], core_ref[1] % 2
    count, rows = x_hbm.shape[0], q_ref.shape[0]
    half = count // 2
    me = me_ref[0]
    query = pltpu.make_async_copy(q_hbm, q_ref, sems.at[16])
    query.start()
    token = pltpu.make_async_copy(x_hbm.at[core_ref[1]], x_ref.at[2 * half], sems.at[17])
    token.start()
    tokens = [
        pltpu.make_async_copy(
            x_hbm.at[2 * (n % half) + jnp.where(n < half, 1 - mine, mine)], x_ref.at[n], block_sems.at[n]
        )
        for n in range(count)
    ]
    for copy in tokens:
        copy.start()

    def sorted_copies(src, dst, first):
        return [
            pltpu.make_async_copy(
                src.at[:, 1 - mine if n == 0 else mine], dst.at[n], sems.at[first + n]
            )
            for n in range(2)
        ]

    keys = sorted_copies(k_hbm, k_ref, 12)
    values = sorted_copies(v_hbm, v_ref, 14)
    for copy in keys + values:
        copy.start()
    weights = fetch_start((wk0, wk1, wk2, wk3), wk_ref, sems, 0, me)
    weights += fetch_start((wv0, wv1, wv2, wv3), wv_ref, sems, 4, me)
    weights += fetch_start((wq0, wq1, wq2, wq3), wq_ref, sems, 8, me)
    part = wq_ref.shape[0] // 4
    width = wq_ref.shape[1]

    def put(row, term):
        term_ref[0:width, :] = term
        for out, c in ((send_ref, 1 - core), (keep_ref, core)):
            for far in range(2):
                at = pl.multiple_of((2 * far + c) * part, part)
                out[far, row * part : (row + 1) * part, :] = term_ref[pl.ds(at, part), :].astype(bf16)

    query.wait()
    token.wait()
    put(0, jnp.dot(x_ref[2 * half], q_ref[...], preferred_element_type=f32))
    for copy in tokens:
        copy.wait()
    left = jnp.concatenate([x_ref[n] for n in range(count)], axis=1)
    for row, ref, copies in ((1, k_ref, keys), (2, v_ref, values)):
        for copy in copies:
            copy.wait()
        put(row, jnp.dot(left, ref[...].reshape(count * rows, width), preferred_element_type=f32))
    sums = column_sum(v_ref[...].reshape(count * rows, width))
    last = jnp.concatenate([column_sum(q_ref[...]), sums, jnp.zeros((62, width), f32)], axis=0).astype(bf16)
    for out in (send_ref, keep_ref):
        for far in range(2):
            out[far, 3 * part :, :] = last
    fetch_wait(weights)
    near_ref[...] = res_ref[...] + back_mul(q_ref[...], wq_ref[...])
    for n, out in ((0, far_ref), (1, own_ref)):
        term = back_mul(k_ref[n].reshape(half * rows, width), wk_ref[...])
        term = term + back_mul(v_ref[n].reshape(half * rows, width), wv_ref[...])
        out[...] = term.astype(bf16).reshape(half, rows, width)


def finish(core_position, me, dq, dk, dv, x_all_t, res, wk, wv, wq):
    count, width, rows = x_all_t.shape
    half = count // 2
    part = width // 4
    shape = jax.ShapeDtypeStruct
    grads = shape((2, 3 * part + 64, width), bf16)
    others = shape((half, rows, width), bf16)
    cut = lambda v: v.reshape(half, 2, rows, width)
    hbm = spec(pltpu.HBM)
    vmem = lambda *dims: pltpu.VMEM(dims, bf16)
    return pl.pallas_call(
        finish_kernel,
        in_specs=[spec(pltpu.SMEM)] * 2 + [hbm] * 4 + [spec()] + [hbm] * 12,
        out_specs=[spec()] * 5,
        out_shape=[grads, grads, others, others, shape((rows, width), f32)],
        scratch_shapes=[
            vmem(rows, width), vmem(count + 1, width, rows), vmem(2, half, rows, width), vmem(2, half, rows, width),
            vmem(width, width), vmem(width, width), vmem(width, width),
            pltpu.VMEM((width, width), f32), pltpu.SemaphoreType.DMA((18,)), pltpu.SemaphoreType.DMA((count,)),
        ],
        compiler_params=pltpu.CompilerParams(vmem_limit_bytes=VMEM_LIMIT),
        cost_estimate=NO_COST,
        name="finish",
    )(core_position, me, dq, cut(dk), cut(dv), x_all_t, res, *wk, *wv, *wq)


def pack_kernel(me_ref, *refs):
    vectors, (up_ref, bs_ref, qp_ref, bp_ref, bc_ref), out_ref = refs[:8], refs[8:13], refs[13]
    part = vectors[0].shape[1]
    small = bs_ref.shape[1]
    width = out_ref.shape[1]
    out_ref[...] = jnp.zeros(out_ref.shape, f32)
    for k in range(width // part):

        @pl.when(me_ref[0] == k)
        def _():
            for row, ref in enumerate(vectors):
                out_ref[row : row + 1, k * part : (k + 1) * part] = ref[...].astype(f32)
            out_ref[VEC_UP + k : VEC_UP + k + 1, :] = up_ref[...].astype(f32)
            for row, ref in enumerate((bs_ref, qp_ref, bp_ref)):
                out_ref[VEC_POOL + row : VEC_POOL + row + 1, k * small : (k + 1) * small] = ref[...].astype(f32)
            if k == 0:
                out_ref[VEC_CLASS : VEC_CLASS + 1, 0:CLASSES] = bc_ref[...].astype(f32)


def pack_call(me, vectors, up, pools, classes, width):
    operands = [v.reshape(1, -1) for v in vectors + [up] + pools + [classes]]
    return pl.pallas_call(
        pack_kernel,
        in_specs=[spec(pltpu.SMEM)] + [spec()] * len(operands),
        out_specs=spec(),
        out_shape=jax.ShapeDtypeStruct((16, width), f32),
        cost_estimate=NO_COST,
        name="pack",
    )(me, *operands)


def swap(value, axis, bit):
    count = lax.axis_size(axis)
    return lax.ppermute(value, axis, [(i, i ^ bit) for i in range(count)])


def join_far(shard):
    return double(shard, "fsdp", 2)


def join_core(column):
    core = lax.axis_index("fsdp") % 2
    across = swap(column, "fsdp", 1)
    full = jnp.where(
        core == 0, jnp.stack([column, across], axis=1), jnp.stack([across, column], axis=1)
    )
    return full.reshape(-1, column.shape[-1])


def bits_of(axis):
    return [1 << k for k in range(lax.axis_size(axis).bit_length() - 1)]


def tie(*values):
    return lax.optimization_barrier(values)


def merge_kernel(pick_ref, keep_ref, got_ref, send_ref, kept_ref):
    mine = pick_ref[0]
    for out, at in ((send_ref, 1 - mine), (kept_ref, mine)):
        out[0] = (keep_ref[0, at].astype(f32) + got_ref[0, at].astype(f32)).astype(bf16)


def merge(keep, got, mine, rows):
    n = keep.shape[-1]
    keep, got = keep.reshape(-1, 2, rows, n), got.reshape(-1, 2, rows, n)
    a = keep.shape[0]
    cuts = 1
    while rows // cuts > 256 and rows % (32 * cuts) == 0:
        cuts *= 2
    both = pl.BlockSpec((1, 2, rows // cuts, n), lambda i, j, s: (i, 0, j, 0))
    half = pl.BlockSpec((1, rows // cuts, n), lambda i, j, s: (i, j, 0))
    shape = jax.ShapeDtypeStruct((a, rows, n), bf16)
    return pl.pallas_call(
        merge_kernel,
        grid_spec=pltpu.PrefetchScalarGridSpec(
            num_scalar_prefetch=1, grid=(a, cuts), in_specs=[both, both], out_specs=[half, half]
        ),
        out_shape=[shape, shape],
        cost_estimate=NO_COST,
        compiler_params=pltpu.CompilerParams(vmem_limit_bytes=VMEM_LIMIT),
        name="merge",
    )(mine, keep, got)


def merge_cut_kernel(pick_ref, keep_ref, got_ref, first_ref, second_ref, kept_ref):
    mine = pick_ref[0]
    half = pl.num_programs(0) // 2
    total = lambda at: (keep_ref[at].astype(f32) + got_ref[at].astype(f32)).astype(bf16)
    kept_ref[...] = total(mine)

    @pl.when(pl.program_id(0) < half)
    def _():
        first_ref[...] = total(1 - mine)

    @pl.when(pl.program_id(0) >= half)
    def _():
        second_ref[...] = total(1 - mine)


def merge_cut(keep, got, mine):
    _, rows, n = keep.shape
    cuts = 4
    step = rows // cuts
    both = pl.BlockSpec((2, step, n), lambda j, s: (0, j, 0))
    part = jax.ShapeDtypeStruct((rows // 2, n), bf16)
    return pl.pallas_call(
        merge_cut_kernel,
        grid_spec=pltpu.PrefetchScalarGridSpec(
            num_scalar_prefetch=1,
            grid=(cuts,),
            in_specs=[both, both],
            out_specs=[
                pl.BlockSpec((step, n), lambda j, s: (jnp.minimum(j, cuts // 2 - 1), 0)),
                pl.BlockSpec((step, n), lambda j, s: (jnp.maximum(j - cuts // 2, 0), 0)),
                pl.BlockSpec((step, n), lambda j, s: (j, 0)),
            ],
        ),
        out_shape=[part, part, jax.ShapeDtypeStruct((rows, n), bf16)],
        cost_estimate=NO_COST,
        compiler_params=pltpu.CompilerParams(vmem_limit_bytes=VMEM_LIMIT),
        name="merge_cut",
    )(mine, keep, got)


def merge_parts_kernel(pick_ref, keep_ref, first_ref, second_ref, send_ref, kept_ref):
    def put(low_ref, high_ref):
        low_ref[...] = (keep_ref[0].astype(f32) + first_ref[...].astype(f32)).astype(bf16)
        high_ref[...] = (keep_ref[1].astype(f32) + second_ref[...].astype(f32)).astype(bf16)

    pl.when(pick_ref[0] == 0)(lambda: put(kept_ref, send_ref))
    pl.when(pick_ref[0] != 0)(lambda: put(send_ref, kept_ref))


def merge_parts(keep, first, second, mine):
    rows, n = first.shape
    shape = jax.ShapeDtypeStruct((rows, n), bf16)
    step = rows // 2
    block = pl.BlockSpec((step, n), lambda j, s: (j, 0))
    return pl.pallas_call(
        merge_parts_kernel,
        grid_spec=pltpu.PrefetchScalarGridSpec(
            num_scalar_prefetch=1,
            grid=(2,),
            in_specs=[pl.BlockSpec((2, step, n), lambda j, s: (0, j, 0)), block, block],
            out_specs=[block, block],
        ),
        out_shape=[shape, shape],
        cost_estimate=NO_COST,
        compiler_params=pltpu.CompilerParams(vmem_limit_bytes=VMEM_LIMIT),
        name="merge_parts",
    )(mine, keep.reshape(2, rows, n), first, second)


class Box:
    def __init__(self, keep):
        self.keep = keep


class Order:
    def __init__(self, holder):
        self.holder = holder
        self.results = None

    def after(self, value):
        if self.results is not None and self.results[0]:
            value, self.holder.keep, *done = tie(value, self.holder.keep, *self.results[1])
            self.results = (False, done)
        else:
            value, self.holder.keep = tie(value, self.holder.keep)
        return value

    def pin(self, value):
        box = Box(self.after(value))
        self.holder = box
        return box


class Sum:
    def __init__(self, keep, send, steps):
        self.keep, self.send, self.todo = keep, send, steps

    @staticmethod
    def mine(step):
        return (lax.axis_index(step[1]) // step[2][0]) % 2

    @staticmethod
    def shift(step, r):
        return sum(bit for k, bit in enumerate(step[2]) if (r >> k) & 1)

    def begin(self):
        step = self.todo[0]
        self.got = [swap(v, step[1], self.shift(step, r + 1)) for r, v in enumerate(self.send)]

    def end(self, order, pick=None):
        step = self.todo.pop(0)
        got = list(self.got)
        got[-1] = order.after(got[-1])
        order.holder = self
        n = self.keep.shape[-1]
        if step[0] == "gather":
            mine = self.mine(step)
            rows = self.keep.shape[0]
            out = jnp.zeros(((len(got) + 1) * rows, n), bf16)
            for r, v in enumerate([self.keep] + got):
                out = lax.dynamic_update_slice_in_dim(out, v, (mine ^ r) * rows, axis=0)
            self.keep = out
        else:
            parts = [self.keep] + got

            def total(pick):
                out = pick(parts[0]).astype(f32)
                for v in parts[1:]:
                    out = out + pick(v).astype(f32)
                return out.astype(bf16)

            following = self.todo[0] if self.todo else None
            if following is not None and following[0] == "scatter":
                mine = self.mine(following)
                ways, rows = 1 << len(following[2]), following[3]
                if pick is not None:
                    send, self.keep = merge(self.keep, got[0], pick, rows)
                    self.send = [send]
                    return

                def piece(r):
                    return lambda v: lax.dynamic_index_in_dim(
                        v.reshape(-1, ways, rows, n), mine ^ r, 1, keepdims=False
                    )

                self.send = [total(piece(r)) for r in range(1, ways)]
                self.keep = total(piece(0))
                return
            self.keep = total(lambda v: v.reshape(-1, n))
        if self.todo:
            self.send = [self.keep] * ((1 << len(self.todo[0][2])) - 1)

    def step(self, order, pick=None):
        self.end(order, pick)
        if self.todo:
            self.begin()


def bits_of(axis):
    return [1 << k for k in range(lax.axis_size(axis).bit_length() - 1)]


def double(value, axis, bit):
    mine = (lax.axis_index(axis) // bit) % 2
    got = swap(value, axis, bit)
    return jnp.where(mine == 0, jnp.stack([value, got]), jnp.stack([got, value]))


def rounds_of(axis):
    return [(bit,) for bit in bits_of(axis)]


def grad_steps(rows, far_second=False):
    steps = [("scatter", "fsdp", (1,), rows)]
    far = ("scatter", "fsdp", (2,))
    if not far_second:
        steps.append(far + (rows,))
    for k, bits in enumerate(rounds_of("ctx")):
        rows //= 2
        steps.append(("scatter", "ctx", bits, rows))
        if far_second and k == 0:
            steps.append(far + (rows,))
    return steps + [("gather", "ctx", bits, 0) for bits in rounds_of("ctx")[::-1]]


def shards(
    tokens,
    starts,
    labels,
    cotangent,
    w_query,
    b_query,
    w_key,
    w_value,
    b_value,
    w_out,
    b_out,
    norm1_gain,
    norm1_bias,
    w_up,
    b_up,
    w_down,
    b_down,
    norm2_gain,
    norm2_bias,
    w_student,
    b_student,
    pool_query,
    w_pool,
    b_pool,
    w_class,
    b_class,
):
    cycle_size = lax.axis_size("ctx")
    cycle_index = lax.axis_index("ctx")
    fsdp_size = lax.axis_size("fsdp")
    me = lax.axis_index("fsdp")
    core, far = me % 2, me // 2
    number = lambda *v: jnp.stack(v).astype(jnp.int32)
    me_row, owner, pick_far, pick_near = number(me), number(cycle_index), number(far), number(cycle_index % 2)
    blocks = number(1 - core, 3 - core, core, 2 + core)
    core_position = number(core, cycle_index)
    near_order = number(1 - cycle_index % 2, cycle_index % 2)
    tok_rows = tokens.shape[1]
    width = tokens.shape[2]
    part = width // fsdp_size
    hidden_part = b_up.shape[0]
    pool_width = w_pool.shape[1]
    seq_total = tok_rows * cycle_size
    score_scale = 1.0 / math.sqrt(HEAD_DIM)
    starts_row = starts[0]
    x_in = tokens[0]
    x_all = lax.all_gather(x_in, "ctx", axis=0, tiled=True)

    def pieces(shard, far):
        return [shard, swap(shard, "fsdp", 1), far, swap(far, "fsdp", 1)]

    far_wk, far_wv, far_wq = swap(w_key, "fsdp", 2), swap(w_value, "fsdp", 2), swap(w_query, "fsdp", 2)
    mats = jnp.concatenate([w_student, w_pool, jnp.pad(w_class, ((0, 0), (0, pool_width - CLASSES)))], axis=0)
    vectors = [b_query, b_value, b_out, norm1_gain, norm1_bias, b_down, norm2_gain, norm2_bias]
    vecs = pack_call(me_row, vectors, b_up, [b_student, pool_query, b_pool], b_class, width)
    far_vecs, mats = swap(vecs, "fsdp", 2), join_far(mats)
    far_wk, far_wv, far_wq, far_vecs, mats, w_out, w_up = tie(
        far_wk, far_wv, far_wq, far_vecs, mats, w_out, w_up
    )
    vecs = vecs + far_vecs
    vecs = vecs + swap(vecs, "fsdp", 1)
    vecs, owner, pick_far, pick_near, blocks, core_position, near_order = tie(
        vecs, owner, pick_far, pick_near, blocks, core_position, near_order
    )
    far_wo, far_w1 = swap(w_out, "fsdp", 2), swap(w_up, "fsdp", 2)
    piece_wk, piece_wv, piece_wq = pieces(w_key, far_wk), pieces(w_value, far_wv), pieces(w_query, far_wq)
    mats = join_core(mats).reshape(fsdp_size, -1, pool_width)
    x_all, far_wo, far_w1, mats, w_down = tie(x_all, far_wo, far_w1, mats, w_down)
    far_w2 = swap(w_down, "fsdp", 2)
    piece_wo, piece_w1 = pieces(w_out, far_wo), pieces(w_up, far_w1)

    local_pos = cycle_index * tok_rows + jnp.arange(tok_rows, dtype=jnp.int32)
    local_doc = doc_of(local_pos, starts_row)
    all_doc = doc_of(jnp.arange(seq_total, dtype=jnp.int32), starts_row)
    at = jnp.arange(128, dtype=jnp.int32)[None, :]
    extra = ((at == all_doc[:, None]) | ((at >= NDOC) & (at < NDOC + 3))).astype(bf16)
    docs = local_doc[None, :]
    doc_column = local_doc[:, None]

    query_s, key_b, value_b, x_all_t = project(me_row, x_in, x_all, vecs, piece_wq, piece_wk, piece_wv)
    attn_t, attn_b, attn_low_t, lse = attend(query_s, key_b, value_b, extra, docs)
    attn_b, far_w2 = tie(attn_b, far_w2)
    piece_w2 = pieces(w_down, far_w2)

    hid_t, normed1, inv1, act, slope, out_b, normed2, inv2, student, score, local = layer_forward_call(
        me_row, attn_b, x_in, vecs, mats, doc_column, piece_wo, piece_w1, piece_w2
    )
    parts = lax.all_to_all(
        jnp.broadcast_to(local[None], (cycle_size,) + local.shape), "ctx", 0, 0, tiled=True
    )
    grad_down_b, grad_res2, logits, vec_a, tables = head_call(
        labels, owner, parts, vecs, mats, doc_column, student, score, out_b, cotangent[0], normed2, inv2
    )
    logits = logits[:NDOC, :CLASSES]


    def grad_sum(pair, far_second=False):
        return Sum(pair[1], [pair[0]], grad_steps(pair[0].shape[1], far_second))

    sum_w2 = grad_sum(down_grad(blocks, act, grad_down_b))
    sum_w2.begin()
    grad_up_b, grad_res1, grad_branch_b, grad_attn_b, vec_b = layer_backward_call(
        me_row, grad_down_b, grad_res2, slope, normed1, inv1, vecs, piece_wo, piece_w1, piece_w2
    )
    order = Order(Box(grad_attn_b))
    attn_box = order.holder
    first, second, sum_w2.keep = merge_cut(sum_w2.keep, order.after(sum_w2.got[0]), pick_far)
    sum_w2.todo = sum_w2.todo[2:]
    order.holder = sum_w2
    first, second = swap(first, "fsdp", 2), swap(second, "fsdp", 2)
    grad_up_b = order.after(grad_up_b)
    sum_mid = grad_sum(
        middle_grad(blocks, hid_t, grad_up_b, attn_low_t, grad_branch_b, tables, vec_a, vec_b), True
    )
    sum_mid.keep = order.after(sum_mid.keep)
    order.holder = sum_mid
    sum_mid.begin()
    pairs = width // (2 * HEAD_DIM)
    some = (pairs + 1) // 2
    given = (query_s, key_b, value_b, extra, docs, attn_t, lse)
    grad_attn_b = order.after(attn_box.keep)
    dq, dk, dv = attend_back(0, some, (), *given, grad_attn_b)
    box = order.pin(dq)
    first = order.after(first)
    sum_mid.step(order, pick_near)
    grad_attn_b, first = tie(order.after(grad_attn_b), first)
    dq, dk, dv = attend_back(some, pairs - some, (box.keep, dk, dv), *given, grad_attn_b)
    box = order.pin(dq)
    send, sum_w2.keep = merge_parts(sum_w2.keep, first, order.after(second), pick_near)
    sum_w2.send = [send]
    order.holder = sum_w2
    sum_w2.begin()
    dq = order.after(box.keep)
    if seq_total <= 4096:
        send, keep, others_send, others_keep, near = finish(
            core_position, me_row, dq, dk, dv, x_all_t, grad_res1, piece_wk, piece_wv, piece_wq
        )
    else:
        send, keep = last_grad(blocks, core_position[1:], x_all_t, dq, dk, dv)
        others_send, others_keep, near = others_call(
            near_order, me_row, dq, grad_res1, dk, dv, piece_wk, piece_wv, piece_wq, tok_rows
        )
    near = order.after(near)
    sum_mid.step(order)
    sum_last = grad_sum((order.after(send), keep))
    sum_last.begin()
    sum_last.step(order, pick_far)
    sum_others = Sum(
        others_keep, [order.after(others_send)], [("scatter", "ctx", bits, tok_rows) for bits in rounds_of("ctx")]
    )
    sum_others.begin()
    sum_w2.step(order)

    def early_results():
        middle = sum_mid.keep.astype(f32)
        ups_sum, middle = middle[:hidden_part], middle[hidden_part:]
        high = part * pool_width // width
        tall = middle[part : part + high]
        done_ws = jnp.concatenate(jnp.split(tall, width // pool_width, axis=1), axis=0)
        rest = middle[part + high :]
        base, half = 2 * pool_width, width // 2
        rows = jnp.concatenate([rest[:16, base : base + half], rest[16:, base : base + half]], axis=1)
        return (
            middle[:part],
            done_ws,
            rest[:, :pool_width],
            rest[:, pool_width : pool_width + CLASSES],
            lax.dynamic_slice_in_dim(rows, me * part, part, axis=1),
            lax.dynamic_slice_in_dim(rows[3:6], me * w_pool.shape[0], w_pool.shape[0], axis=1),
            rows[6, :CLASSES],
            lax.dynamic_index_in_dim(rows, 8 + me, 0, keepdims=False),
            jnp.concatenate(jnp.split(ups_sum, hidden_part // part, axis=0), axis=1),
            sum_w2.keep.astype(f32),
        )

    waves = [sum_w2, sum_mid, sum_others, sum_last]
    plan = PLAN if cycle_size == 8 else []
    for k in plan:
        if k == 30:
            order.results = (True, early_results())
            continue
        wave = waves[k % 10]
        if k < 20 and wave.todo:
            wave.end(order)
        if k >= 20:
            wave.send = [order.after(wave.send[0])]
        if k // 10 != 1 and wave.todo:
            wave.begin()
    while any(w.todo for w in waves):
        for w in waves:
            if w.todo:
                w.step(order)
    if order.results is None:
        order.results = (False, early_results())

    grad_tokens = near + sum_others.keep.reshape(tok_rows, width).astype(f32)
    (
        done_wo, done_ws, done_wp, done_wc, own, pools, done_bc, done_c1, done_w1, done_w2,
    ) = order.results[1]
    last = sum_last.keep.astype(f32)
    late = lax.dynamic_slice_in_dim(last[3 * part : 3 * part + 8], me * part, part, axis=1)
    return (
        out_b[None],
        logits[None],
        grad_tokens[None],
        last[:part],
        late[0],
        last[part : 2 * part],
        last[2 * part : 3 * part],
        late[1],
        done_wo,
        own[14],
        own[12],
        own[13],
        done_w1,
        done_c1,
        done_w2,
        own[0],
        own[1],
        own[2],
        done_ws,
        pools[0],
        pools[1],
        done_wp,
        pools[2],
        done_wc,
        done_bc,
    )


def solution(mesh):
    in_specs = (
        P("fsdp", "ctx", None),
        P("fsdp", None),
        P("fsdp", None),
        P("fsdp", "ctx", None),
        P("fsdp", None),
        P("fsdp"),
        P("fsdp", None),
        P("fsdp", None),
        P("fsdp"),
        P("fsdp", None),
        P("fsdp"),
        P("fsdp"),
        P("fsdp"),
        P("fsdp", None),
        P("fsdp"),
        P("fsdp", None),
        P("fsdp"),
        P("fsdp"),
        P("fsdp"),
        P("fsdp", None),
        P("fsdp"),
        P("fsdp"),
        P("fsdp", None),
        P("fsdp"),
        P("fsdp", None),
        P(),
    )
    out_specs = (
        P("fsdp", "ctx", None),
        P("fsdp", None, None),
        P("fsdp", "ctx", None),
        P("fsdp", None),
        P("fsdp"),
        P("fsdp", None),
        P("fsdp", None),
        P("fsdp"),
        P("fsdp", None),
        P("fsdp"),
        P("fsdp"),
        P("fsdp"),
        P("fsdp", None),
        P("fsdp"),
        P("fsdp", None),
        P("fsdp"),
        P("fsdp"),
        P("fsdp"),
        P("fsdp", None),
        P("fsdp"),
        P("fsdp"),
        P("fsdp", None),
        P("fsdp"),
        P("fsdp", None),
        P(),
    )
    return jax.shard_map(shards, mesh=mesh, in_specs=in_specs, out_specs=out_specs, check_vma=False)
```

```python
import functools
import math

import jax
import jax.numpy as jnp
from jax import lax
from jax.experimental import pallas as pl
from jax.experimental.pallas import tpu as pltpu
from jax.sharding import PartitionSpec as P

HEADS = 12
HEAD_DIM = 64
POOL_HEADS = 2
CLASSES = 14
NDOC = 4

big_negative = -1e30
norm_eps = 1e-05
f32 = jnp.float32
bf16 = jnp.bfloat16
VMEM_LIMIT = 56 * 1024 * 1024
PLAN = [0, 1, 0, 1, 0, 3, 1, 2, 0, 1, 3, 12, 1, 3, 3, 22, 0, 3, 1, 3, 30, 2, 3]


def doc_of(positions, starts_row):
    return jnp.sum((starts_row[None, :] <= positions[:, None]).astype(jnp.int32), axis=1) - 1


def cross_rows(left_mat, right_mat):
    return lax.dot_general(
        left_mat, right_mat, (((0,), (0,)), ((), ())), preferred_element_type=f32
    )


def back_mul(left_mat, right_mat):
    return lax.dot_general(
        left_mat, right_mat, (((1,), (1,)), ((), ())), preferred_element_type=f32
    )


def _half_mask(shape, axis, half):
    return (lax.broadcasted_iota(jnp.int32, shape, axis) // HEAD_DIM) == half


def _split3(row):
    hi = row.astype(bf16)
    rest = row - hi.astype(f32)
    mid = rest.astype(bf16)
    low = (rest - mid.astype(f32)).astype(bf16)
    return hi.astype(f32), mid.astype(f32), low.astype(f32)


def _extra_rows(docrow, row=None):
    at = lax.broadcasted_iota(jnp.int32, (128, docrow.shape[1]), 0)
    out = jnp.where((at < NDOC) & (at != docrow), big_negative, 0.0)
    if row is not None:
        for k, part in enumerate(_split3(row)):
            out = out + jnp.where(at == NDOC + k, part, 0.0)
    return out.astype(bf16)


def project_kernel(
    me_ref, x_ref, all_ref, vec_ref,
    wq0, wq1, wq2, wq3, wk0, wk1, wk2, wk3, wv0, wv1, wv2, wv3,
    q_ref, k_ref, v_ref, all_t_ref, wq_ref, wk_ref, wv_ref, sems,
):
    @pl.when(pl.program_id(0) == 0)
    def _():
        me = me_ref[0]
        copies = fetch_start((wk0, wk1, wk2, wk3), wk_ref, sems, 0, me)
        copies += fetch_start((wv0, wv1, wv2, wv3), wv_ref, sems, 4, me)
        copies += fetch_start((wq0, wq1, wq2, wq3), wq_ref, sems, 8, me)
        fetch_wait(copies)
        query = jnp.dot(x_ref[...], wq_ref[...], preferred_element_type=f32)
        query = (query + vec_ref[pl.ds(VEC_QUERY, 1), :]).astype(bf16).astype(f32)
        q_ref[...] = (query * (1.0 / math.sqrt(HEAD_DIM))).astype(bf16)

    rows = all_ref[...]
    k_ref[...] = jnp.dot(rows, wk_ref[...], preferred_element_type=f32).astype(bf16)
    value = jnp.dot(rows, wv_ref[...], preferred_element_type=f32)
    v_ref[...] = (value + vec_ref[pl.ds(VEC_VALUE, 1), :]).astype(bf16)
    all_t_ref[0] = rows.T


def project(me, x_in, x_all, vecs, wq, wk, wv):
    tok, width = x_in.shape
    seq = x_all.shape[0]
    rows = tok
    whole = lambda v: pl.BlockSpec(v.shape, lambda i: (0, 0), pipeline_mode=pl.Buffered(1))
    block = pl.BlockSpec((rows, width), lambda i: (i, 0))
    shape = jax.ShapeDtypeStruct
    return pl.pallas_call(
        project_kernel,
        grid=(seq // rows,),
        in_specs=[spec(pltpu.SMEM), whole(x_in), block, whole(vecs)] + [spec(pltpu.HBM)] * 12,
        out_specs=[
            pl.BlockSpec((tok, width), lambda i: (0, 0)),
            block,
            block,
            pl.BlockSpec((1, width, rows), lambda i: (i, 0, 0)),
        ],
        out_shape=[
            shape((tok, width), bf16), shape((seq, width), bf16), shape((seq, width), bf16),
            shape((seq // rows, width, rows), bf16),
        ],
        scratch_shapes=[pltpu.VMEM((width, width), bf16)] * 3 + [pltpu.SemaphoreType.DMA((12,))],
        compiler_params=pltpu.CompilerParams(vmem_limit_bytes=VMEM_LIMIT),
        cost_estimate=NO_COST,
        name="project",
    )(me, x_in, x_all, vecs, *wq, *wk, *wv)


def attend_kernel(chunks, q_ref, k_ref, v_ref, extra_ref, doc_ref, attn_ref, low_ref, low_t_ref, lse_ref, s_ref):
    rows = k_ref.shape[0] // chunks
    q_t = q_ref[...].astype(f32).T
    bias = _extra_rows(doc_ref[...])
    outs = []
    for half in range(2):
        q_aug = jnp.concatenate(
            [jnp.where(_half_mask(q_t.shape, 0, half), q_t, 0.0).astype(bf16), bias], axis=0
        )
        top = None
        for c in range(chunks):
            at = pl.ds(c * rows, rows)
            k_aug = jnp.concatenate([k_ref[at, :], extra_ref[at, :]], axis=1)
            s_now = jnp.dot(k_aug, q_aug, preferred_element_type=f32)
            s_ref[half, at, :] = s_now
            top_now = jnp.max(s_now, axis=0, keepdims=True)
            top = top_now if top is None else jnp.maximum(top, top_now)
        total = jnp.zeros_like(top)
        mixed = jnp.zeros((2 * HEAD_DIM, q_t.shape[1]), f32)
        for c in range(chunks):
            at = pl.ds(c * rows, rows)
            p_now = jnp.exp(s_ref[half, at, :] - top)
            total = total + jnp.sum(p_now, axis=0, keepdims=True)
            mixed = mixed + cross_rows(v_ref[at, :], p_now.astype(bf16))
        lse_ref[0, pl.ds(half, 1), :] = top + jnp.log(total)
        outs.append(mixed[half * HEAD_DIM : (half + 1) * HEAD_DIM] / total)
    out_t = jnp.concatenate(outs, axis=0)
    attn_ref[...] = out_t
    low_ref[...] = out_t.T.astype(bf16)
    low_t_ref[...] = out_t.astype(bf16)


def attend(query, keys, values, extra, docs):
    tok, width = query.shape
    seq = keys.shape[0]
    lanes = 2 * HEAD_DIM
    pairs = width // lanes
    shape = jax.ShapeDtypeStruct
    return pl.pallas_call(
        functools.partial(attend_kernel, 4),
        grid=(pairs,),
        in_specs=[
            pl.BlockSpec((tok, lanes), lambda p: (0, p)),
            pl.BlockSpec((seq, lanes), lambda p: (0, p)),
            pl.BlockSpec((seq, lanes), lambda p: (0, p)),
            pl.BlockSpec((seq, lanes), lambda p: (0, 0)),
            pl.BlockSpec((1, tok), lambda p: (0, 0)),
        ],
        out_specs=[
            pl.BlockSpec((lanes, tok), lambda p: (p, 0)),
            pl.BlockSpec((tok, lanes), lambda p: (0, p)),
            pl.BlockSpec((lanes, tok), lambda p: (p, 0)),
            pl.BlockSpec((1, 2, tok), lambda p: (p, 0, 0)),
        ],
        out_shape=[
            shape((width, tok), f32), shape((tok, width), bf16), shape((width, tok), bf16),
            shape((pairs, 2, tok), f32),
        ],
        scratch_shapes=[pltpu.VMEM((2, seq, tok), f32)],
        compiler_params=pltpu.CompilerParams(vmem_limit_bytes=VMEM_LIMIT),
        cost_estimate=NO_COST,
        name="attend",
    )(query, keys, values, extra, docs)


def attend_back_kernel(
    chunks, q_ref, k_ref, v_ref, extra_ref, doc_ref, attn_ref, lse_ref, g_ref, *more
):
    dq_ref, dk_ref, dv_ref = more[-3:]
    rows = k_ref.shape[0] // chunks
    q_low = q_ref[...]
    g_low = g_ref[...]
    q_t = q_low.astype(f32).T
    g_t = g_low.astype(f32).T
    prod = attn_ref[...] * g_t
    lanes = 2 * HEAD_DIM
    q_side, g_side, q_rows, g_rows = [], [], [], []
    for half in range(2):
        pick = _half_mask(q_t.shape, 0, half)
        delta = jnp.sum(prod[half * HEAD_DIM : (half + 1) * HEAD_DIM], axis=0, keepdims=True)
        q_side.append(
            jnp.concatenate(
                [
                    jnp.where(pick, q_t, 0.0).astype(bf16),
                    _extra_rows(doc_ref[...], -lse_ref[0, pl.ds(half, 1), :]),
                ],
                axis=0,
            )
        )
        g_side.append(
            jnp.concatenate(
                [
                    jnp.where(pick, g_t, 0.0).astype(bf16),
                    _extra_rows(jnp.full_like(doc_ref[...], -1), -delta)
                    * (lax.broadcasted_iota(jnp.int32, (128, q_t.shape[1]), 0) >= NDOC).astype(bf16),
                ],
                axis=0,
            )
        )
        pick_lane = _half_mask(q_low.shape, 1, half)
        q_rows.append(jnp.where(pick_lane, q_low.astype(f32), 0.0).astype(bf16))
        g_rows.append(jnp.where(pick_lane, g_low.astype(f32), 0.0).astype(bf16))
    q_rows = jnp.concatenate(q_rows, axis=0)
    g_rows = jnp.concatenate(g_rows, axis=0)
    dq_t = [jnp.zeros((lanes, q_t.shape[1]), f32) for half in range(2)]
    for c in range(chunks):
        at = pl.ds(c * rows, rows)
        k_now = k_ref[at, :]
        extra = extra_ref[at, :]
        k_aug = jnp.concatenate([k_now, extra], axis=1)
        v_aug = jnp.concatenate([v_ref[at, :], extra], axis=1)
        p_low, s_low = [], []
        for half in range(2):
            prob = jnp.exp(jnp.dot(k_aug, q_side[half], preferred_element_type=f32))
            slope = jnp.dot(v_aug, g_side[half], preferred_element_type=f32)
            p_low.append(prob.astype(bf16))
            s_low.append((prob * slope).astype(bf16))
            dq_t[half] = dq_t[half] + cross_rows(k_now, s_low[half])
        dk_ref[at, :] = jnp.dot(
            jnp.concatenate(s_low, axis=1), q_rows, preferred_element_type=f32
        ).astype(bf16)
        dv_ref[at, :] = jnp.dot(
            jnp.concatenate(p_low, axis=1), g_rows, preferred_element_type=f32
        ).astype(bf16)
    pick = _half_mask(q_t.shape, 0, 0)
    dq_ref[...] = (jnp.where(pick, dq_t[0], dq_t[1]).T * (1.0 / math.sqrt(HEAD_DIM))).astype(bf16)


def attend_back(first, pairs, so_far, query, keys, values, extra, docs, attn_t, lse, grad_attn):
    tok, width = query.shape
    seq = keys.shape[0]
    lanes = 2 * HEAD_DIM
    columns = lambda rows: pl.BlockSpec((rows, lanes), lambda p: (0, p + first))
    shape = lambda rows: jax.ShapeDtypeStruct((rows, width), bf16)
    return pl.pallas_call(
        functools.partial(attend_back_kernel, 4),
        grid=(pairs,),
        in_specs=[
            columns(tok),
            columns(seq),
            columns(seq),
            pl.BlockSpec((seq, lanes), lambda p: (0, 0)),
            pl.BlockSpec((1, tok), lambda p: (0, 0)),
            pl.BlockSpec((lanes, tok), lambda p: (p + first, 0)),
            pl.BlockSpec((1, 2, tok), lambda p: (p + first, 0, 0)),
            columns(tok),
        ]
        + [spec(pltpu.HBM)] * len(so_far),
        out_specs=[columns(tok), columns(seq), columns(seq)],
        out_shape=[shape(tok), shape(seq), shape(seq)],
        input_output_aliases={8 + k: k for k in range(len(so_far))},
        compiler_params=pltpu.CompilerParams(vmem_limit_bytes=VMEM_LIMIT),
        cost_estimate=NO_COST,
        name="attend_back",
    )(query, keys, values, extra, docs, attn_t, lse, grad_attn, *so_far)


VEC_QUERY, VEC_VALUE, VEC_OUT, VEC_GAIN1, VEC_BIAS1, VEC_DOWN, VEC_GAIN2, VEC_BIAS2, VEC_UP = range(9)
VEC_POOL, VEC_CLASS = 12, 15
NO_COST = pl.CostEstimate(flops=0, transcendentals=0, bytes_accessed=0)


def spec(space=pltpu.VMEM):
    return pl.BlockSpec(memory_space=space)


def fetch_start(pieces, target, sems, first, me):
    rows = pieces[0].shape[0]
    copies = []
    for r, piece in enumerate(pieces):
        at = pl.multiple_of((me ^ r) * rows, rows)
        copy = pltpu.make_async_copy(piece, target.at[pl.ds(at, rows), :], sems.at[first + r])
        copy.start()
        copies.append(copy)
    return copies


def fetch_wait(copies):
    for copy in copies:
        copy.wait()


def norm_parts(field):
    centre = field - jnp.mean(field, axis=-1, keepdims=True)
    inv_std = lax.rsqrt(jnp.mean(centre * centre, axis=-1, keepdims=True) + norm_eps)
    return centre * inv_std, inv_std


def norm_back(grad_in, normed, inv_std, gain_row):
    scaled = grad_in * gain_row
    return inv_std * (
        scaled
        - jnp.mean(scaled, axis=-1, keepdims=True)
        - normed * jnp.mean(scaled * normed, axis=-1, keepdims=True)
    )


def column_sum(value):
    return jnp.sum(value.astype(f32), axis=0, keepdims=True)


def student_tables(mats):
    width_part = mats.shape[1] - 64
    ws = jnp.concatenate([mats[k, :width_part] for k in range(mats.shape[0])], axis=0)
    wp = jnp.concatenate([mats[k, width_part : width_part + 32] for k in range(mats.shape[0])], axis=0)
    wc = jnp.concatenate([mats[k, width_part + 32 :] for k in range(mats.shape[0])], axis=0)
    return ws, wp, wc


def halves_sum(value):
    lane = lax.broadcasted_iota(jnp.int32, value.shape, 1)
    half = value.shape[1] // POOL_HEADS
    low = jnp.sum(jnp.where(lane < half, value, 0.0), axis=1, keepdims=True)
    high = jnp.sum(jnp.where(lane < half, 0.0, value), axis=1, keepdims=True)
    return jnp.where(lane < half, low, high)


def of_docs(doc, rows):
    out = jnp.where(doc == 0, rows[0], 0.0)
    for k in range(1, NDOC):
        out = jnp.where(doc == k, rows[k], out)
    return out


def forward_kernel(
    me_ref, attn_ref, x_ref, vec_ref, mats_ref, doc_ref,
    wo0, wo1, wo2, wo3, wu0, wu1, wu2, wu3, wd0, wd1, wd2, wd3,
    hid_t_ref, normed1_ref, inv1_ref, act_ref, slope_ref,
    out_ref, normed2_ref, inv2_ref, student_ref, score_ref, part_ref,
    wo_ref, wu_ref, wd_ref, sems,
):
    me = me_ref[0]
    go_o = fetch_start((wo0, wo1, wo2, wo3), wo_ref, sems, 0, me)
    go_u = fetch_start((wu0, wu1, wu2, wu3), wu_ref, sems, 4, me)
    go_d = fetch_start((wd0, wd1, wd2, wd3), wd_ref, sems, 8, me)
    vec = lambda k: vec_ref[pl.ds(k, 1), :]
    fetch_wait(go_o)
    branch = jnp.dot(attn_ref[...], wo_ref[...], preferred_element_type=f32) + vec(VEC_OUT)
    normed, inv_std = norm_parts(x_ref[...].astype(f32) + branch)
    normed1_ref[...] = normed
    inv1_ref[...] = inv_std
    hidden = normed * vec(VEC_GAIN1) + vec(VEC_BIAS1)
    hid_t_ref[...] = hidden.T.astype(bf16)
    hid_low = hidden.astype(bf16)
    width = hidden.shape[1]
    fetch_wait(go_u)
    down = None
    for j in range(wu_ref.shape[1] // width):
        at = pl.ds(j * width, width)
        pre = jnp.dot(hid_low, wu_ref[:, at], preferred_element_type=f32) + vec(VEC_UP + j)
        cdf = 0.5 * (1.0 + lax.erf(pre * (1.0 / math.sqrt(2.0))))
        pdf = jnp.exp(-0.5 * pre * pre) * (1.0 / math.sqrt(2.0 * math.pi))
        slope_ref[:, at] = (cdf + pre * pdf).astype(bf16)
        act = (pre * cdf).astype(bf16)
        act_ref[:, at] = act
        if j == 0:
            fetch_wait(go_d)
        term = jnp.dot(act, wd_ref[at, :], preferred_element_type=f32)
        down = term if down is None else down + term
    normed, inv_std = norm_parts(hidden + (down + vec(VEC_DOWN)))
    normed2_ref[...] = normed
    inv2_ref[...] = inv_std
    out_low = (normed * vec(VEC_GAIN2) + vec(VEC_BIAS2)).astype(bf16)
    out_ref[...] = out_low
    ws, _, _ = student_tables(mats_ref[...])
    pool = ws.shape[1]
    student = jnp.dot(out_low, ws, preferred_element_type=f32) + vec(VEC_POOL)[:, :pool]
    student_ref[...] = student
    scale = 1.0 / math.sqrt(pool // POOL_HEADS)
    score = halves_sum(student * vec(VEC_POOL + 1)[:, :pool]) * scale
    score_ref[...] = score
    doc = doc_ref[...]
    tops = [
        jnp.max(jnp.where(doc == k, score, big_negative), axis=0, keepdims=True) for k in range(NDOC)
    ]
    weight = jnp.exp(score - of_docs(doc, tops))
    mixed = weight * student
    totals = [jnp.sum(jnp.where(doc == k, weight, 0.0), axis=0, keepdims=True) for k in range(NDOC)]
    sums = [jnp.sum(jnp.where(doc == k, mixed, 0.0), axis=0, keepdims=True) for k in range(NDOC)]
    part_ref[...] = jnp.concatenate(tops + totals + sums + [jnp.zeros((4, pool), f32)], axis=0)


def layer_forward_call(me, attn, x_in, vecs, mats, doc, wo, wu, wd):
    tok, width = x_in.shape
    hidden = wu[0].shape[1]
    pool = mats.shape[2]
    shape = jax.ShapeDtypeStruct
    return pl.pallas_call(
        forward_kernel,
        in_specs=[spec(pltpu.SMEM)] + [spec()] * 5 + [spec(pltpu.HBM)] * 12,
        out_specs=[spec()] * 11,
        out_shape=[
            shape((width, tok), bf16), shape((tok, width), f32), shape((tok, 1), f32),
            shape((tok, hidden), bf16), shape((tok, hidden), bf16),
            shape((tok, width), bf16), shape((tok, width), f32), shape((tok, 1), f32),
            shape((tok, pool), f32), shape((tok, pool), f32), shape((16, pool), f32),
        ],
        scratch_shapes=[
            pltpu.VMEM((width, width), bf16), pltpu.VMEM((width, hidden), bf16),
            pltpu.VMEM((hidden, width), bf16), pltpu.SemaphoreType.DMA((12,)),
        ],
        compiler_params=pltpu.CompilerParams(vmem_limit_bytes=VMEM_LIMIT),
        cost_estimate=NO_COST,
        name="layer_forward",
    )(me, attn, x_in, vecs, mats, doc, *wo, *wu, *wd)


def exact_dot(left, right, dims):
    return lax.dot_general(
        left, right, (dims, ((), ())), precision=lax.Precision.HIGHEST, preferred_element_type=f32
    )


def head_kernel(
    label_ref, owner_ref, parts_ref, vec_ref, mats_ref, doc_ref, student_ref, score_ref, out_ref, cot_ref,
    normed2_ref, inv2_ref,
    down_ref, res2_ref, logits_ref, vec_grad_ref, tables_ref,
):
    vec = lambda k: vec_ref[pl.ds(k, 1), :]
    ws, wp, wc = student_tables(mats_ref[...])
    pool = ws.shape[1]
    wp, wc = wp.astype(f32), wc.astype(f32)
    tops = jnp.max(parts_ref[:, 0:NDOC, :], axis=0)
    factor = jnp.exp(parts_ref[:, 0:NDOC, :] - tops[None])
    totals = jnp.sum(parts_ref[:, NDOC : 2 * NDOC, :] * factor, axis=0)
    pooled = jnp.sum(parts_ref[:, 2 * NDOC : 3 * NDOC, :] * factor, axis=0) / totals
    pooled = jnp.concatenate([pooled, jnp.zeros((8 - NDOC, pool), f32)], axis=0)
    act = jnp.tanh(exact_dot(pooled, wp, ((1,), (0,))) + vec(VEC_POOL + 2)[:, :pool])
    logits = exact_dot(act, wc, ((1,), (0,))) + vec(VEC_CLASS)[:, :pool]
    logits_ref[...] = logits
    lane = lax.broadcasted_iota(jnp.int32, logits.shape, 1)
    row = lax.broadcasted_iota(jnp.int32, logits.shape, 0)
    shown = jnp.where(lane < CLASSES, logits, big_negative)
    shown = jnp.exp(shown - jnp.max(shown, axis=1, keepdims=True))
    grad_logits = shown / jnp.sum(shown, axis=1, keepdims=True)
    for k in range(NDOC):
        grad_logits = grad_logits - jnp.where((row == k) & (lane == label_ref[0, k]), 1.0, 0.0)
    grad_logits = jnp.where(row < NDOC, grad_logits, 0.0)
    owner = (owner_ref[0] == 0).astype(f32)
    grad_wc = exact_dot(act, grad_logits, ((0,), (0,))) * owner
    grad_pre = exact_dot(grad_logits, wc, ((1,), (1,))) * (1.0 - act * act)
    grad_wp = exact_dot(pooled, grad_pre, ((0,), (0,))) * owner
    grad_pooled = exact_dot(grad_pre, wp, ((1,), (1,)))
    doc = doc_ref[...]
    student = student_ref[...]
    each = lambda table: [table[k : k + 1] for k in range(NDOC)]
    weight = jnp.exp(score_ref[...] - of_docs(doc, each(tops))) / of_docs(doc, each(totals))
    tok_grad = of_docs(doc, each(grad_pooled))
    grad_score = weight * halves_sum(tok_grad * (student - of_docs(doc, each(pooled))))
    scale = 1.0 / math.sqrt(pool // POOL_HEADS)
    grad_student = weight * tok_grad + grad_score * vec(VEC_POOL + 1)[:, :pool] * scale
    grad_low = grad_student.astype(bf16)
    out_low = out_ref[...]
    grad_ws = cross_rows(out_low, grad_low)
    blocks, rows = mats_ref.shape[0], mats_ref.shape[1]
    high = rows - 64
    for k in range(blocks):
        tables_ref[k, 0:high, :] = grad_ws[k * high : (k + 1) * high]
        tables_ref[k, high : high + 32, :] = grad_wp[32 * k : 32 * k + 32]
        tables_ref[k, high + 32 : high + 64, :] = grad_wc[32 * k : 32 * k + 32]
    grad_layer = cot_ref[...].astype(f32) + back_mul(grad_low, ws)
    normed = normed2_ref[...]
    grad_res = norm_back(grad_layer, normed, inv2_ref[...], vec(VEC_GAIN2))
    res2_ref[...] = grad_res
    low = grad_res.astype(bf16)
    down_ref[...] = low
    width = normed.shape[1]
    wide = lambda v: jnp.concatenate([v, jnp.zeros((1, width - pool), f32)], axis=1)
    rows = [
        column_sum(low),
        column_sum(grad_layer * normed),
        column_sum(grad_layer),
        wide(column_sum(grad_low)),
        wide(column_sum(grad_score * student) * scale),
        wide(column_sum(grad_pre) * owner),
        wide(column_sum(grad_logits) * owner),
        jnp.zeros((1, width), f32),
    ]
    vec_grad_ref[...] = jnp.concatenate(rows, axis=0)


def head_call(labels, owner, parts, vecs, mats, doc, student, score, out_low, cot, normed2, inv2):
    tok, width = out_low.shape
    shape = jax.ShapeDtypeStruct
    return pl.pallas_call(
        head_kernel,
        in_specs=[spec(pltpu.SMEM)] * 2 + [spec()] * 10,
        out_specs=[spec()] * 5,
        out_shape=[
            shape((tok, width), bf16), shape((tok, width), f32), shape((8, mats.shape[2]), f32),
            shape((8, width), f32), shape(mats.shape, f32),
        ],
        compiler_params=pltpu.CompilerParams(vmem_limit_bytes=VMEM_LIMIT),
        cost_estimate=NO_COST,
        name="head",
    )(labels, owner, parts, vecs, mats, doc, student, score, out_low, cot, normed2, inv2)


def backward_kernel(
    me_ref, low_ref, res2_ref, slope_ref, normed1_ref, inv1_ref, vec_ref,
    wo0, wo1, wo2, wo3, wu0, wu1, wu2, wu3, wd0, wd1, wd2, wd3,
    up_ref, res1_ref, branch_ref, attn_ref, vec_grad_ref,
    wo_ref, wu_ref, wd_ref, sems,
):
    me = me_ref[0]
    go_d = fetch_start((wd0, wd1, wd2, wd3), wd_ref, sems, 8, me)
    go_u = fetch_start((wu0, wu1, wu2, wu3), wu_ref, sems, 4, me)
    go_o = fetch_start((wo0, wo1, wo2, wo3), wo_ref, sems, 0, me)
    low = low_ref[...]
    width = low.shape[1]
    fetch_wait(go_d)
    total = res2_ref[...]
    rows = []
    for j in range(wu_ref.shape[1] // width):
        at = pl.ds(j * width, width)
        up = (back_mul(low, wd_ref[at, :]) * slope_ref[:, at].astype(f32)).astype(bf16)
        up_ref[:, at] = up
        rows.append(column_sum(up))
        if j == 0:
            fetch_wait(go_u)
        total = total + back_mul(up, wu_ref[:, at])
    normed = normed1_ref[...]
    rows += [column_sum(total * normed), column_sum(total)]
    grad_res = norm_back(total, normed, inv1_ref[...], vec_ref[pl.ds(VEC_GAIN1, 1), :])
    res1_ref[...] = grad_res
    branch = grad_res.astype(bf16)
    branch_ref[...] = branch
    rows += [column_sum(branch), jnp.zeros((1, width), f32)]
    vec_grad_ref[...] = jnp.concatenate(rows, axis=0)
    fetch_wait(go_o)
    attn_ref[...] = back_mul(branch, wo_ref[...]).astype(bf16)


def layer_backward_call(me, low, res2, slope, normed1, inv1, vecs, wo, wu, wd):
    tok, width = low.shape
    hidden = wu[0].shape[1]
    shape = jax.ShapeDtypeStruct
    return pl.pallas_call(
        backward_kernel,
        in_specs=[spec(pltpu.SMEM)] + [spec()] * 6 + [spec(pltpu.HBM)] * 12,
        out_specs=[spec()] * 5,
        out_shape=[
            shape((tok, hidden), bf16), shape((tok, width), f32), shape((tok, width), bf16),
            shape((tok, width), bf16), shape((8, width), f32),
        ],
        scratch_shapes=[
            pltpu.VMEM((width, width), bf16), pltpu.VMEM((width, hidden), bf16),
            pltpu.VMEM((hidden, width), bf16), pltpu.SemaphoreType.DMA((12,)),
        ],
        compiler_params=pltpu.CompilerParams(vmem_limit_bytes=VMEM_LIMIT),
        cost_estimate=NO_COST,
        name="layer_backward",
    )(me, low, res2, slope, normed1, inv1, vecs, *wo, *wu, *wd)


def down_grad_kernel(order_ref, act_ref, grad_ref, send_ref, keep_ref):
    term = cross_rows(act_ref[...], grad_ref[...]).astype(bf16)
    half = send_ref.shape[0]

    @pl.when(pl.program_id(0) < pl.num_programs(0) // 2)
    def _():
        send_ref[0] = term

    @pl.when(pl.program_id(0) >= pl.num_programs(0) // 2)
    def _():
        keep_ref[0] = term


def send_keep_specs(block):
    nd = len(block)
    zero = (0,) * (nd - 1)
    return [
        pl.BlockSpec(block, lambda i, s: (jnp.minimum(i, 1),) + zero),
        pl.BlockSpec(block, lambda i, s: (jnp.maximum(i - 2, 0),) + zero),
    ]


def down_grad(blocks, act, grad):
    tok, hidden = act.shape
    width = grad.shape[1]
    part = hidden // 4
    shape = jax.ShapeDtypeStruct((2, part, width), bf16)
    return pl.pallas_call(
        down_grad_kernel,
        grid_spec=pltpu.PrefetchScalarGridSpec(
            num_scalar_prefetch=1,
            grid=(4,),
            in_specs=[
                pl.BlockSpec((tok, part), lambda i, s: (0, s[i])),
                pl.BlockSpec((tok, width), lambda i, s: (0, 0)),
            ],
            out_specs=send_keep_specs((1, part, width)),
        ),
        out_shape=[shape, shape],
        compiler_params=pltpu.CompilerParams(vmem_limit_bytes=VMEM_LIMIT),
        cost_estimate=NO_COST,
        name="down_grad",
    )(blocks, act, grad)


def middle_grad_kernel(order_ref, hid_ref, up_ref, attn_ref, branch_ref, tables_ref, vec_a_ref, vec_b_ref, send_ref, keep_ref):
    part = attn_ref.shape[0]
    width = branch_ref.shape[1]
    pool = tables_ref.shape[2]
    half = width // 2

    def put(out):
        base = 0
        for j in range(up_ref.shape[1] // width):
            out[0, base : base + part, :] = jnp.dot(
                hid_ref[...], up_ref[:, j * width : (j + 1) * width], preferred_element_type=f32
            ).astype(bf16)
            base += part
        out[0, base : base + part, :] = jnp.dot(
            attn_ref[...], branch_ref[...], preferred_element_type=f32
        ).astype(bf16)
        base += part
        high = tables_ref.shape[1] - 64
        step = high * pool // width
        out[0, base : base + step, :] = jnp.concatenate(
            [tables_ref[0, k * step : (k + 1) * step, :] for k in range(width // pool)], axis=1
        ).astype(bf16)
        rows = jnp.concatenate([vec_a_ref[...], vec_b_ref[...]], axis=0)
        rows = jnp.concatenate([rows[:, :half], rows[:, half:]], axis=0)
        out[0, base + step : base + step + 32, :] = jnp.concatenate(
            [
                tables_ref[0, high : high + 32, :],
                tables_ref[0, high + 32 : high + 64, :],
                rows,
                jnp.zeros((32, width - 2 * pool - half), f32),
            ],
            axis=1,
        ).astype(bf16)

    pl.when(pl.program_id(0) < 2)(lambda: put(send_ref))
    pl.when(pl.program_id(0) >= 2)(lambda: put(keep_ref))


def middle_grad(blocks, hid_t, up, attn_t, branch, tables, vec_a, vec_b):
    width, tok = attn_t.shape
    part = width // 4
    hidden = up.shape[1]
    rows = hidden // 4 + part + 64
    shape = jax.ShapeDtypeStruct((2, rows, width), bf16)
    return pl.pallas_call(
        middle_grad_kernel,
        grid_spec=pltpu.PrefetchScalarGridSpec(
            num_scalar_prefetch=1,
            grid=(4,),
            in_specs=[
                pl.BlockSpec((part, tok), lambda i, s: (s[i], 0)),
                pl.BlockSpec((tok, hidden), lambda i, s: (0, 0)),
                pl.BlockSpec((part, tok), lambda i, s: (s[i], 0)),
                pl.BlockSpec((tok, width), lambda i, s: (0, 0)),
                pl.BlockSpec((1,) + tables.shape[1:], lambda i, s: (s[i], 0, 0)),
                pl.BlockSpec(vec_a.shape, lambda i, s: (0, 0)),
                pl.BlockSpec(vec_b.shape, lambda i, s: (0, 0)),
            ],
            out_specs=send_keep_specs((1, rows, width)),
        ),
        out_shape=[shape, shape],
        compiler_params=pltpu.CompilerParams(vmem_limit_bytes=VMEM_LIMIT),
        cost_estimate=NO_COST,
        name="middle_grad",
    )(blocks, hid_t, up, attn_t, branch, tables, vec_a, vec_b)


def last_grad_kernel(order_ref, xt_ref, xt_all_ref, dq_ref, dk_ref, dv_ref, send_ref, keep_ref):
    part = xt_ref.shape[0]

    def put(out):
        for k, (left, right) in enumerate(((xt_ref, dq_ref), (xt_all_ref, dk_ref), (xt_all_ref, dv_ref))):
            out[0, k * part : (k + 1) * part, :] = jnp.dot(
                left[...], right[...], preferred_element_type=f32
            ).astype(bf16)
        width = dq_ref.shape[1]
        rows = jnp.concatenate(
            [column_sum(dq_ref[...]), column_sum(dv_ref[...]), jnp.zeros((62, width), f32)], axis=0
        )
        out[0, 3 * part :, :] = rows.astype(bf16)

    pl.when(pl.program_id(0) < 2)(lambda: put(send_ref))
    pl.when(pl.program_id(0) >= 2)(lambda: put(keep_ref))


def last_grad(blocks, position, x_all_t, dq, dk, dv):
    tok, width = dq.shape
    seq = dk.shape[0]
    x_all_t = x_all_t.transpose(1, 0, 2).reshape(width, seq)
    part = width // 4
    rows = 3 * part + 64
    shape = jax.ShapeDtypeStruct((2, rows, width), bf16)
    whole = lambda r: pl.BlockSpec((r, width), lambda i, s: (0, 0), pipeline_mode=pl.Buffered(1))
    return pl.pallas_call(
        last_grad_kernel,
        grid_spec=pltpu.PrefetchScalarGridSpec(
            num_scalar_prefetch=1,
            grid=(4,),
            in_specs=[
                pl.BlockSpec((part, tok), lambda i, s: (s[i], s[4])),
                pl.BlockSpec((part, seq), lambda i, s: (s[i], 0)),
                whole(tok),
                whole(seq),
                whole(seq),
            ],
            out_specs=send_keep_specs((1, rows, width)),
        ),
        out_shape=[shape, shape],
        compiler_params=pltpu.CompilerParams(vmem_limit_bytes=VMEM_LIMIT),
        cost_estimate=NO_COST,
        name="last_grad",
    )(jnp.concatenate([blocks, position]), x_all_t, x_all_t, dq, dk, dv)


def others_kernel(
    order_ref, me_ref, q_ref, res_ref, k_ref, v_ref,
    wk0, wk1, wk2, wk3, wv0, wv1, wv2, wv3, wq0, wq1, wq2, wq3,
    send_ref, keep_ref, near_ref, wk_ref, wv_ref, wq_ref, sems,
):
    step = pl.program_id(0)
    half = pl.num_programs(0) // 2
    start = lambda pieces, target, first: fetch_start(pieces, target, sems, first, me_ref[0])

    @pl.when(step == 0)
    def _():
        copies = start((wk0, wk1, wk2, wk3), wk_ref, 0) + start((wv0, wv1, wv2, wv3), wv_ref, 4)
        query = start((wq0, wq1, wq2, wq3), wq_ref, 8)
        fetch_wait(query)
        near_ref[...] = res_ref[...] + back_mul(q_ref[...], wq_ref[...])
        fetch_wait(copies)

    flat = lambda ref: ref[...].reshape(-1, ref.shape[-1])
    term = back_mul(flat(k_ref), wk_ref[...]) + back_mul(flat(v_ref), wv_ref[...])
    term = term.astype(bf16).reshape(send_ref.shape)

    @pl.when(step < half)
    def _():
        send_ref[...] = term

    @pl.when(step >= half)
    def _():
        keep_ref[...] = term


def others_call(order, me, dq, res, dk, dv, wk, wv, wq, rows):
    seq, width = dk.shape
    tok = res.shape[0]
    half = seq // rows // 2
    group = 2 if half % 2 == 0 else 1
    n = half // group
    block = pl.BlockSpec((group, 1, rows, width), lambda i, s: (i % n, s[i // n], 0, 0))
    whole = lambda v: pl.BlockSpec(v.shape, lambda i, s: (0, 0), pipeline_mode=pl.Buffered(1))
    shape = jax.ShapeDtypeStruct((half, rows, width), bf16)
    cut = lambda v: v.reshape(half, 2, rows, width)
    return pl.pallas_call(
        others_kernel,
        grid_spec=pltpu.PrefetchScalarGridSpec(
            num_scalar_prefetch=1,
            grid=(2 * n,),
            in_specs=[spec(pltpu.SMEM), whole(dq), whole(res), block, block] + [spec(pltpu.HBM)] * 12,
            out_specs=[
                pl.BlockSpec((group, rows, width), lambda i, s: (jnp.minimum(i, n - 1), 0, 0)),
                pl.BlockSpec((group, rows, width), lambda i, s: (jnp.maximum(i - n, 0), 0, 0)),
                pl.BlockSpec((tok, width), lambda i, s: (0, 0)),
            ],
            scratch_shapes=[pltpu.VMEM((width, width), bf16)] * 3 + [pltpu.SemaphoreType.DMA((12,))],
        ),
        out_shape=[shape, shape, jax.ShapeDtypeStruct((tok, width), f32)],
        compiler_params=pltpu.CompilerParams(vmem_limit_bytes=VMEM_LIMIT),
        cost_estimate=NO_COST,
        name="others",
    )(order, me, dq, res, cut(dk), cut(dv), *wk, *wv, *wq)


def finish_kernel(
    core_ref, me_ref, q_hbm, k_hbm, v_hbm, x_hbm, res_ref,
    wk0, wk1, wk2, wk3, wv0, wv1, wv2, wv3, wq0, wq1, wq2, wq3,
    send_ref, keep_ref, far_ref, own_ref, near_ref,
    q_ref, x_ref, k_ref, v_ref, wk_ref, wv_ref, wq_ref, term_ref, sems, block_sems,
):
    core, mine = core_ref[0], core_ref[1] % 2
    count, rows = x_hbm.shape[0], q_ref.shape[0]
    half = count // 2
    me = me_ref[0]
    query = pltpu.make_async_copy(q_hbm, q_ref, sems.at[16])
    query.start()
    token = pltpu.make_async_copy(x_hbm.at[core_ref[1]], x_ref.at[2 * half], sems.at[17])
    token.start()
    tokens = [
        pltpu.make_async_copy(
            x_hbm.at[2 * (n % half) + jnp.where(n < half, 1 - mine, mine)], x_ref.at[n], block_sems.at[n]
        )
        for n in range(count)
    ]
    for copy in tokens:
        copy.start()

    def sorted_copies(src, dst, first):
        return [
            pltpu.make_async_copy(
                src.at[:, 1 - mine if n == 0 else mine], dst.at[n], sems.at[first + n]
            )
            for n in range(2)
        ]

    keys = sorted_copies(k_hbm, k_ref, 12)
    values = sorted_copies(v_hbm, v_ref, 14)
    for copy in keys + values:
        copy.start()
    weights = fetch_start((wk0, wk1, wk2, wk3), wk_ref, sems, 0, me)
    weights += fetch_start((wv0, wv1, wv2, wv3), wv_ref, sems, 4, me)
    weights += fetch_start((wq0, wq1, wq2, wq3), wq_ref, sems, 8, me)
    part = wq_ref.shape[0] // 4
    width = wq_ref.shape[1]

    def put(row, term):
        term_ref[0:width, :] = term
        for out, c in ((send_ref, 1 - core), (keep_ref, core)):
            for far in range(2):
                at = pl.multiple_of((2 * far + c) * part, part)
                out[far, row * part : (row + 1) * part, :] = term_ref[pl.ds(at, part), :].astype(bf16)

    query.wait()
    token.wait()
    put(0, jnp.dot(x_ref[2 * half], q_ref[...], preferred_element_type=f32))
    for copy in tokens:
        copy.wait()
    left = jnp.concatenate([x_ref[n] for n in range(count)], axis=1)
    for row, ref, copies in ((1, k_ref, keys), (2, v_ref, values)):
        for copy in copies:
            copy.wait()
        put(row, jnp.dot(left, ref[...].reshape(count * rows, width), preferred_element_type=f32))
    sums = column_sum(v_ref[...].reshape(count * rows, width))
    last = jnp.concatenate([column_sum(q_ref[...]), sums, jnp.zeros((62, width), f32)], axis=0).astype(bf16)
    for out in (send_ref, keep_ref):
        for far in range(2):
            out[far, 3 * part :, :] = last
    fetch_wait(weights)
    near_ref[...] = res_ref[...] + back_mul(q_ref[...], wq_ref[...])
    for n, out in ((0, far_ref), (1, own_ref)):
        term = back_mul(k_ref[n].reshape(half * rows, width), wk_ref[...])
        term = term + back_mul(v_ref[n].reshape(half * rows, width), wv_ref[...])
        out[...] = term.astype(bf16).reshape(half, rows, width)


def finish(core_position, me, dq, dk, dv, x_all_t, res, wk, wv, wq):
    count, width, rows = x_all_t.shape
    half = count // 2
    part = width // 4
    shape = jax.ShapeDtypeStruct
    grads = shape((2, 3 * part + 64, width), bf16)
    others = shape((half, rows, width), bf16)
    cut = lambda v: v.reshape(half, 2, rows, width)
    hbm = spec(pltpu.HBM)
    vmem = lambda *dims: pltpu.VMEM(dims, bf16)
    return pl.pallas_call(
        finish_kernel,
        in_specs=[spec(pltpu.SMEM)] * 2 + [hbm] * 4 + [spec()] + [hbm] * 12,
        out_specs=[spec()] * 5,
        out_shape=[grads, grads, others, others, shape((rows, width), f32)],
        scratch_shapes=[
            vmem(rows, width), vmem(count + 1, width, rows), vmem(2, half, rows, width), vmem(2, half, rows, width),
            vmem(width, width), vmem(width, width), vmem(width, width),
            pltpu.VMEM((width, width), f32), pltpu.SemaphoreType.DMA((18,)), pltpu.SemaphoreType.DMA((count,)),
        ],
        compiler_params=pltpu.CompilerParams(vmem_limit_bytes=VMEM_LIMIT),
        cost_estimate=NO_COST,
        name="finish",
    )(core_position, me, dq, cut(dk), cut(dv), x_all_t, res, *wk, *wv, *wq)


def pack_kernel(me_ref, *refs):
    vectors, (up_ref, bs_ref, qp_ref, bp_ref, bc_ref), out_ref = refs[:8], refs[8:13], refs[13]
    part = vectors[0].shape[1]
    small = bs_ref.shape[1]
    width = out_ref.shape[1]
    out_ref[...] = jnp.zeros(out_ref.shape, f32)
    for k in range(width // part):

        @pl.when(me_ref[0] == k)
        def _():
            for row, ref in enumerate(vectors):
                out_ref[row : row + 1, k * part : (k + 1) * part] = ref[...].astype(f32)
            out_ref[VEC_UP + k : VEC_UP + k + 1, :] = up_ref[...].astype(f32)
            for row, ref in enumerate((bs_ref, qp_ref, bp_ref)):
                out_ref[VEC_POOL + row : VEC_POOL + row + 1, k * small : (k + 1) * small] = ref[...].astype(f32)
            if k == 0:
                out_ref[VEC_CLASS : VEC_CLASS + 1, 0:CLASSES] = bc_ref[...].astype(f32)


def pack_call(me, vectors, up, pools, classes, width):
    operands = [v.reshape(1, -1) for v in vectors + [up] + pools + [classes]]
    return pl.pallas_call(
        pack_kernel,
        in_specs=[spec(pltpu.SMEM)] + [spec()] * len(operands),
        out_specs=spec(),
        out_shape=jax.ShapeDtypeStruct((16, width), f32),
        cost_estimate=NO_COST,
        name="pack",
    )(me, *operands)


def swap(value, axis, bit):
    count = lax.axis_size(axis)
    return lax.ppermute(value, axis, [(i, i ^ bit) for i in range(count)])


def join_far(shard):
    return double(shard, "fsdp", 2)


def join_core(column):
    core = lax.axis_index("fsdp") % 2
    across = swap(column, "fsdp", 1)
    full = jnp.where(
        core == 0, jnp.stack([column, across], axis=1), jnp.stack([across, column], axis=1)
    )
    return full.reshape(-1, column.shape[-1])


def bits_of(axis):
    return [1 << k for k in range(lax.axis_size(axis).bit_length() - 1)]


def tie(*values):
    return lax.optimization_barrier(values)


def merge_kernel(pick_ref, keep_ref, got_ref, send_ref, kept_ref):
    mine = pick_ref[0]
    for out, at in ((send_ref, 1 - mine), (kept_ref, mine)):
        out[0] = (keep_ref[0, at].astype(f32) + got_ref[0, at].astype(f32)).astype(bf16)


def merge(keep, got, mine, rows):
    n = keep.shape[-1]
    keep, got = keep.reshape(-1, 2, rows, n), got.reshape(-1, 2, rows, n)
    a = keep.shape[0]
    cuts = 1
    while rows // cuts > 256 and rows % (32 * cuts) == 0:
        cuts *= 2
    both = pl.BlockSpec((1, 2, rows // cuts, n), lambda i, j, s: (i, 0, j, 0))
    half = pl.BlockSpec((1, rows // cuts, n), lambda i, j, s: (i, j, 0))
    shape = jax.ShapeDtypeStruct((a, rows, n), bf16)
    return pl.pallas_call(
        merge_kernel,
        grid_spec=pltpu.PrefetchScalarGridSpec(
            num_scalar_prefetch=1, grid=(a, cuts), in_specs=[both, both], out_specs=[half, half]
        ),
        out_shape=[shape, shape],
        cost_estimate=NO_COST,
        compiler_params=pltpu.CompilerParams(vmem_limit_bytes=VMEM_LIMIT),
        name="merge",
    )(mine, keep, got)


def merge_cut_kernel(pick_ref, keep_ref, got_ref, first_ref, second_ref, kept_ref):
    mine = pick_ref[0]
    half = pl.num_programs(0) // 2
    total = lambda at: (keep_ref[at].astype(f32) + got_ref[at].astype(f32)).astype(bf16)
    kept_ref[...] = total(mine)

    @pl.when(pl.program_id(0) < half)
    def _():
        first_ref[...] = total(1 - mine)

    @pl.when(pl.program_id(0) >= half)
    def _():
        second_ref[...] = total(1 - mine)


def merge_cut(keep, got, mine):
    _, rows, n = keep.shape
    cuts = 4
    step = rows // cuts
    both = pl.BlockSpec((2, step, n), lambda j, s: (0, j, 0))
    part = jax.ShapeDtypeStruct((rows // 2, n), bf16)
    return pl.pallas_call(
        merge_cut_kernel,
        grid_spec=pltpu.PrefetchScalarGridSpec(
            num_scalar_prefetch=1,
            grid=(cuts,),
            in_specs=[both, both],
            out_specs=[
                pl.BlockSpec((step, n), lambda j, s: (jnp.minimum(j, cuts // 2 - 1), 0)),
                pl.BlockSpec((step, n), lambda j, s: (jnp.maximum(j - cuts // 2, 0), 0)),
                pl.BlockSpec((step, n), lambda j, s: (j, 0)),
            ],
        ),
        out_shape=[part, part, jax.ShapeDtypeStruct((rows, n), bf16)],
        cost_estimate=NO_COST,
        compiler_params=pltpu.CompilerParams(vmem_limit_bytes=VMEM_LIMIT),
        name="merge_cut",
    )(mine, keep, got)


def merge_parts_kernel(pick_ref, keep_ref, first_ref, second_ref, send_ref, kept_ref):
    def put(low_ref, high_ref):
        low_ref[...] = (keep_ref[0].astype(f32) + first_ref[...].astype(f32)).astype(bf16)
        high_ref[...] = (keep_ref[1].astype(f32) + second_ref[...].astype(f32)).astype(bf16)

    pl.when(pick_ref[0] == 0)(lambda: put(kept_ref, send_ref))
    pl.when(pick_ref[0] != 0)(lambda: put(send_ref, kept_ref))


def merge_parts(keep, first, second, mine):
    rows, n = first.shape
    shape = jax.ShapeDtypeStruct((rows, n), bf16)
    step = rows // 2
    block = pl.BlockSpec((step, n), lambda j, s: (j, 0))
    return pl.pallas_call(
        merge_parts_kernel,
        grid_spec=pltpu.PrefetchScalarGridSpec(
            num_scalar_prefetch=1,
            grid=(2,),
            in_specs=[pl.BlockSpec((2, step, n), lambda j, s: (0, j, 0)), block, block],
            out_specs=[block, block],
        ),
        out_shape=[shape, shape],
        cost_estimate=NO_COST,
        compiler_params=pltpu.CompilerParams(vmem_limit_bytes=VMEM_LIMIT),
        name="merge_parts",
    )(mine, keep.reshape(2, rows, n), first, second)


class Box:
    def __init__(self, keep):
        self.keep = keep


class Order:
    def __init__(self, holder):
        self.holder = holder
        self.results = None

    def after(self, value):
        if self.results is not None and self.results[0]:
            value, self.holder.keep, *done = tie(value, self.holder.keep, *self.results[1])
            self.results = (False, done)
        else:
            value, self.holder.keep = tie(value, self.holder.keep)
        return value

    def pin(self, value):
        box = Box(self.after(value))
        self.holder = box
        return box


class Sum:
    def __init__(self, keep, send, steps):
        self.keep, self.send, self.todo = keep, send, steps

    @staticmethod
    def mine(step):
        return (lax.axis_index(step[1]) // step[2][0]) % 2

    @staticmethod
    def shift(step, r):
        return sum(bit for k, bit in enumerate(step[2]) if (r >> k) & 1)

    def begin(self):
        step = self.todo[0]
        self.got = [swap(v, step[1], self.shift(step, r + 1)) for r, v in enumerate(self.send)]

    def end(self, order, pick=None):
        step = self.todo.pop(0)
        got = list(self.got)
        got[-1] = order.after(got[-1])
        order.holder = self
        n = self.keep.shape[-1]
        if step[0] == "gather":
            mine = self.mine(step)
            rows = self.keep.shape[0]
            out = jnp.zeros(((len(got) + 1) * rows, n), bf16)
            for r, v in enumerate([self.keep] + got):
                out = lax.dynamic_update_slice_in_dim(out, v, (mine ^ r) * rows, axis=0)
            self.keep = out
        else:
            parts = [self.keep] + got

            def total(pick):
                out = pick(parts[0]).astype(f32)
                for v in parts[1:]:
                    out = out + pick(v).astype(f32)
                return out.astype(bf16)

            following = self.todo[0] if self.todo else None
            if following is not None and following[0] == "scatter":
                mine = self.mine(following)
                ways, rows = 1 << len(following[2]), following[3]
                if pick is not None:
                    send, self.keep = merge(self.keep, got[0], pick, rows)
                    self.send = [send]
                    return

                def piece(r):
                    return lambda v: lax.dynamic_index_in_dim(
                        v.reshape(-1, ways, rows, n), mine ^ r, 1, keepdims=False
                    )

                self.send = [total(piece(r)) for r in range(1, ways)]
                self.keep = total(piece(0))
                return
            self.keep = total(lambda v: v.reshape(-1, n))
        if self.todo:
            self.send = [self.keep] * ((1 << len(self.todo[0][2])) - 1)

    def step(self, order, pick=None):
        self.end(order, pick)
        if self.todo:
            self.begin()


def bits_of(axis):
    return [1 << k for k in range(lax.axis_size(axis).bit_length() - 1)]


def double(value, axis, bit):
    mine = (lax.axis_index(axis) // bit) % 2
    got = swap(value, axis, bit)
    return jnp.where(mine == 0, jnp.stack([value, got]), jnp.stack([got, value]))


def rounds_of(axis):
    return [(bit,) for bit in bits_of(axis)]


def grad_steps(rows, far_second=False):
    steps = [("scatter", "fsdp", (1,), rows)]
    far = ("scatter", "fsdp", (2,))
    if not far_second:
        steps.append(far + (rows,))
    for k, bits in enumerate(rounds_of("ctx")):
        rows //= 2
        steps.append(("scatter", "ctx", bits, rows))
        if far_second and k == 0:
            steps.append(far + (rows,))
    return steps + [("gather", "ctx", bits, 0) for bits in rounds_of("ctx")[::-1]]


def shards(
    tokens,
    starts,
    labels,
    cotangent,
    w_query,
    b_query,
    w_key,
    w_value,
    b_value,
    w_out,
    b_out,
    norm1_gain,
    norm1_bias,
    w_up,
    b_up,
    w_down,
    b_down,
    norm2_gain,
    norm2_bias,
    w_student,
    b_student,
    pool_query,
    w_pool,
    b_pool,
    w_class,
    b_class,
):
    cycle_size = lax.axis_size("ctx")
    cycle_index = lax.axis_index("ctx")
    fsdp_size = lax.axis_size("fsdp")
    me = lax.axis_index("fsdp")
    core, far = me % 2, me // 2
    number = lambda *v: jnp.stack(v).astype(jnp.int32)
    me_row, owner, pick_far, pick_near = number(me), number(cycle_index), number(far), number(cycle_index % 2)
    blocks = number(1 - core, 3 - core, core, 2 + core)
    core_position = number(core, cycle_index)
    near_order = number(1 - cycle_index % 2, cycle_index % 2)
    tok_rows = tokens.shape[1]
    width = tokens.shape[2]
    part = width // fsdp_size
    hidden_part = b_up.shape[0]
    pool_width = w_pool.shape[1]
    seq_total = tok_rows * cycle_size
    score_scale = 1.0 / math.sqrt(HEAD_DIM)
    starts_row = starts[0]
    x_in = tokens[0]
    x_all = lax.all_gather(x_in, "ctx", axis=0, tiled=True)

    def pieces(shard, far):
        return [shard, swap(shard, "fsdp", 1), far, swap(far, "fsdp", 1)]

    far_wk, far_wv, far_wq = swap(w_key, "fsdp", 2), swap(w_value, "fsdp", 2), swap(w_query, "fsdp", 2)
    mats = jnp.concatenate([w_student, w_pool, jnp.pad(w_class, ((0, 0), (0, pool_width - CLASSES)))], axis=0)
    vectors = [b_query, b_value, b_out, norm1_gain, norm1_bias, b_down, norm2_gain, norm2_bias]
    vecs = pack_call(me_row, vectors, b_up, [b_student, pool_query, b_pool], b_class, width)
    far_vecs, mats = swap(vecs, "fsdp", 2), join_far(mats)
    far_wk, far_wv, far_wq, far_vecs, mats, w_out, w_up = tie(
        far_wk, far_wv, far_wq, far_vecs, mats, w_out, w_up
    )
    vecs = vecs + far_vecs
    vecs = vecs + swap(vecs, "fsdp", 1)
    vecs, owner, pick_far, pick_near, blocks, core_position, near_order = tie(
        vecs, owner, pick_far, pick_near, blocks, core_position, near_order
    )
    far_wo, far_w1 = swap(w_out, "fsdp", 2), swap(w_up, "fsdp", 2)
    piece_wk, piece_wv, piece_wq = pieces(w_key, far_wk), pieces(w_value, far_wv), pieces(w_query, far_wq)
    mats = join_core(mats).reshape(fsdp_size, -1, pool_width)
    far_wo, far_w1, mats, w_down, vecs, *near = tie(
        far_wo, far_w1, mats, w_down, vecs, piece_wk[3], piece_wv[3], piece_wq[3]
    )
    piece_wk[3], piece_wv[3], piece_wq[3] = near
    far_w2 = swap(w_down, "fsdp", 2)
    piece_wo, piece_w1 = pieces(w_out, far_wo), pieces(w_up, far_w1)

    local_pos = cycle_index * tok_rows + jnp.arange(tok_rows, dtype=jnp.int32)
    local_doc = doc_of(local_pos, starts_row)
    all_doc = doc_of(jnp.arange(seq_total, dtype=jnp.int32), starts_row)
    at = jnp.arange(128, dtype=jnp.int32)[None, :]
    extra = ((at == all_doc[:, None]) | ((at >= NDOC) & (at < NDOC + 3))).astype(bf16)
    docs = local_doc[None, :]
    doc_column = local_doc[:, None]

    query_s, key_b, value_b, x_all_t = project(me_row, x_in, x_all, vecs, piece_wq, piece_wk, piece_wv)
    attn_t, attn_b, attn_low_t, lse = attend(query_s, key_b, value_b, extra, docs)
    attn_b, far_w2 = tie(attn_b, far_w2)
    piece_w2 = pieces(w_down, far_w2)

    hid_t, normed1, inv1, act, slope, out_b, normed2, inv2, student, score, local = layer_forward_call(
        me_row, attn_b, x_in, vecs, mats, doc_column, piece_wo, piece_w1, piece_w2
    )
    parts = lax.all_to_all(
        jnp.broadcast_to(local[None], (cycle_size,) + local.shape), "ctx", 0, 0, tiled=True
    )
    grad_down_b, grad_res2, logits, vec_a, tables = head_call(
        labels, owner, parts, vecs, mats, doc_column, student, score, out_b, cotangent[0], normed2, inv2
    )
    logits = logits[:NDOC, :CLASSES]


    def grad_sum(pair, far_second=False):
        return Sum(pair[1], [pair[0]], grad_steps(pair[0].shape[1], far_second))

    sum_w2 = grad_sum(down_grad(blocks, act, grad_down_b))
    sum_w2.begin()
    grad_up_b, grad_res1, grad_branch_b, grad_attn_b, vec_b = layer_backward_call(
        me_row, grad_down_b, grad_res2, slope, normed1, inv1, vecs, piece_wo, piece_w1, piece_w2
    )
    order = Order(Box(grad_attn_b))
    attn_box = order.holder
    first, second, sum_w2.keep = merge_cut(sum_w2.keep, order.after(sum_w2.got[0]), pick_far)
    sum_w2.todo = sum_w2.todo[2:]
    order.holder = sum_w2
    first, second = swap(first, "fsdp", 2), swap(second, "fsdp", 2)
    grad_up_b = order.after(grad_up_b)
    sum_mid = grad_sum(
        middle_grad(blocks, hid_t, grad_up_b, attn_low_t, grad_branch_b, tables, vec_a, vec_b), True
    )
    sum_mid.keep = order.after(sum_mid.keep)
    order.holder = sum_mid
    sum_mid.begin()
    pairs = width // (2 * HEAD_DIM)
    some = (pairs + 1) // 2
    given = (query_s, key_b, value_b, extra, docs, attn_t, lse)
    grad_attn_b = order.after(attn_box.keep)
    dq, dk, dv = attend_back(0, some, (), *given, grad_attn_b)
    box = order.pin(dq)
    first = order.after(first)
    sum_mid.step(order, pick_near)
    grad_attn_b, first = tie(order.after(grad_attn_b), first)
    dq, dk, dv = attend_back(some, pairs - some, (box.keep, dk, dv), *given, grad_attn_b)
    box = order.pin(dq)
    send, sum_w2.keep = merge_parts(sum_w2.keep, first, order.after(second), pick_near)
    sum_w2.send = [send]
    order.holder = sum_w2
    sum_w2.begin()
    dq = order.after(box.keep)
    if seq_total <= 4096:
        send, keep, others_send, others_keep, near = finish(
            core_position, me_row, dq, dk, dv, x_all_t, grad_res1, piece_wk, piece_wv, piece_wq
        )
    else:
        send, keep = last_grad(blocks, core_position[1:], x_all_t, dq, dk, dv)
        others_send, others_keep, near = others_call(
            near_order, me_row, dq, grad_res1, dk, dv, piece_wk, piece_wv, piece_wq, tok_rows
        )
    near = order.after(near)
    sum_mid.step(order)
    sum_last = grad_sum((order.after(send), keep))
    sum_last.begin()
    sum_last.step(order, pick_far)
    sum_others = Sum(
        others_keep, [order.after(others_send)], [("scatter", "ctx", bits, tok_rows) for bits in rounds_of("ctx")]
    )
    sum_others.begin()
    sum_w2.step(order)

    def early_results():
        middle = sum_mid.keep.astype(f32)
        ups_sum, middle = middle[:hidden_part], middle[hidden_part:]
        high = part * pool_width // width
        tall = middle[part : part + high]
        done_ws = jnp.concatenate(jnp.split(tall, width // pool_width, axis=1), axis=0)
        rest = middle[part + high :]
        base, half = 2 * pool_width, width // 2
        rows = jnp.concatenate([rest[:16, base : base + half], rest[16:, base : base + half]], axis=1)
        return (
            middle[:part],
            done_ws,
            rest[:, :pool_width],
            rest[:, pool_width : pool_width + CLASSES],
            lax.dynamic_slice_in_dim(rows, me * part, part, axis=1),
            lax.dynamic_slice_in_dim(rows[3:6], me * w_pool.shape[0], w_pool.shape[0], axis=1),
            rows[6, :CLASSES],
            lax.dynamic_index_in_dim(rows, 8 + me, 0, keepdims=False),
            jnp.concatenate(jnp.split(ups_sum, hidden_part // part, axis=0), axis=1),
            sum_w2.keep.astype(f32),
        )

    waves = [sum_w2, sum_mid, sum_others, sum_last]
    plan = PLAN if cycle_size == 8 else []
    for k in plan:
        if k == 30:
            order.results = (True, early_results())
            continue
        wave = waves[k % 10]
        if k < 20 and wave.todo:
            wave.end(order)
        if k >= 20:
            wave.send = [order.after(wave.send[0])]
        if k // 10 != 1 and wave.todo:
            wave.begin()
    while any(w.todo for w in waves):
        for w in waves:
            if w.todo:
                w.step(order)
    if order.results is None:
        order.results = (False, early_results())

    grad_tokens = near + sum_others.keep.reshape(tok_rows, width).astype(f32)
    (
        done_wo, done_ws, done_wp, done_wc, own, pools, done_bc, done_c1, done_w1, done_w2,
    ) = order.results[1]
    last = sum_last.keep.astype(f32)
    late = lax.dynamic_slice_in_dim(last[3 * part : 3 * part + 8], me * part, part, axis=1)
    return (
        out_b[None],
        logits[None],
        grad_tokens[None],
        last[:part],
        late[0],
        last[part : 2 * part],
        last[2 * part : 3 * part],
        late[1],
        done_wo,
        own[14],
        own[12],
        own[13],
        done_w1,
        done_c1,
        done_w2,
        own[0],
        own[1],
        own[2],
        done_ws,
        pools[0],
        pools[1],
        done_wp,
        pools[2],
        done_wc,
        done_bc,
    )


def solution(mesh):
    in_specs = (
        P("fsdp", "ctx", None),
        P("fsdp", None),
        P("fsdp", None),
        P("fsdp", "ctx", None),
        P("fsdp", None),
        P("fsdp"),
        P("fsdp", None),
        P("fsdp", None),
        P("fsdp"),
        P("fsdp", None),
        P("fsdp"),
        P("fsdp"),
        P("fsdp"),
        P("fsdp", None),
        P("fsdp"),
        P("fsdp", None),
        P("fsdp"),
        P("fsdp"),
        P("fsdp"),
        P("fsdp", None),
        P("fsdp"),
        P("fsdp"),
        P("fsdp", None),
        P("fsdp"),
        P("fsdp", None),
        P(),
    )
    out_specs = (
        P("fsdp", "ctx", None),
        P("fsdp", None, None),
        P("fsdp", "ctx", None),
        P("fsdp", None),
        P("fsdp"),
        P("fsdp", None),
        P("fsdp", None),
        P("fsdp"),
        P("fsdp", None),
        P("fsdp"),
        P("fsdp"),
        P("fsdp"),
        P("fsdp", None),
        P("fsdp"),
        P("fsdp", None),
        P("fsdp"),
        P("fsdp"),
        P("fsdp"),
        P("fsdp", None),
        P("fsdp"),
        P("fsdp"),
        P("fsdp", None),
        P("fsdp"),
        P("fsdp", None),
        P(),
    )
    return jax.shard_map(shards, mesh=mesh, in_specs=in_specs, out_specs=out_specs, check_vma=False)
```

```python
import functools
import math

import jax
import jax.numpy as jnp
from jax import lax
from jax.experimental import pallas as pl
from jax.experimental.pallas import tpu as pltpu
from jax.sharding import PartitionSpec as P

HEADS = 12
HEAD_DIM = 64
POOL_HEADS = 2
CLASSES = 14
NDOC = 4

big_negative = -1e30
norm_eps = 1e-05
f32 = jnp.float32
bf16 = jnp.bfloat16
VMEM_LIMIT = 56 * 1024 * 1024
PLAN = [0, 1, 0, 1, 0, 3, 2, 1, 0, 1, 3, 12, 1, 3, 3, 22, 0, 3, 3, 1, 30, 2, 3]


def doc_of(positions, starts_row):
    return jnp.sum((starts_row[None, :] <= positions[:, None]).astype(jnp.int32), axis=1) - 1


def cross_rows(left_mat, right_mat):
    return lax.dot_general(
        left_mat, right_mat, (((0,), (0,)), ((), ())), preferred_element_type=f32
    )


def back_mul(left_mat, right_mat):
    return lax.dot_general(
        left_mat, right_mat, (((1,), (1,)), ((), ())), preferred_element_type=f32
    )


def _half_mask(shape, axis, half):
    return (lax.broadcasted_iota(jnp.int32, shape, axis) // HEAD_DIM) == half


def _split3(row):
    hi = row.astype(bf16)
    rest = row - hi.astype(f32)
    mid = rest.astype(bf16)
    low = (rest - mid.astype(f32)).astype(bf16)
    return hi.astype(f32), mid.astype(f32), low.astype(f32)


def _extra_rows(docrow, row=None):
    at = lax.broadcasted_iota(jnp.int32, (128, docrow.shape[1]), 0)
    out = jnp.where((at < NDOC) & (at != docrow), big_negative, 0.0)
    if row is not None:
        for k, part in enumerate(_split3(row)):
            out = out + jnp.where(at == NDOC + k, part, 0.0)
    return out.astype(bf16)


def project_kernel(
    me_ref, x_ref, all_ref, vec_ref,
    wq0, wq1, wq2, wq3, wk0, wk1, wk2, wk3, wv0, wv1, wv2, wv3,
    q_ref, k_ref, v_ref, all_t_ref, wq_ref, wk_ref, wv_ref, sems,
):
    @pl.when(pl.program_id(0) == 0)
    def _():
        me = me_ref[0]
        copies = fetch_start((wk0, wk1, wk2, wk3), wk_ref, sems, 0, me)
        copies += fetch_start((wv0, wv1, wv2, wv3), wv_ref, sems, 4, me)
        copies += fetch_start((wq0, wq1, wq2, wq3), wq_ref, sems, 8, me)
        fetch_wait(copies)
        query = jnp.dot(x_ref[...], wq_ref[...], preferred_element_type=f32)
        query = (query + vec_ref[pl.ds(VEC_QUERY, 1), :]).astype(bf16).astype(f32)
        q_ref[...] = (query * (1.0 / math.sqrt(HEAD_DIM))).astype(bf16)

    rows = all_ref[...]
    k_ref[...] = jnp.dot(rows, wk_ref[...], preferred_element_type=f32).astype(bf16)
    value = jnp.dot(rows, wv_ref[...], preferred_element_type=f32)
    v_ref[...] = (value + vec_ref[pl.ds(VEC_VALUE, 1), :]).astype(bf16)
    all_t_ref[0] = rows.T


def project(me, x_in, x_all, vecs, wq, wk, wv):
    tok, width = x_in.shape
    seq = x_all.shape[0]
    rows = tok
    whole = lambda v: pl.BlockSpec(v.shape, lambda i: (0, 0), pipeline_mode=pl.Buffered(1))
    block = pl.BlockSpec((rows, width), lambda i: (i, 0))
    shape = jax.ShapeDtypeStruct
    return pl.pallas_call(
        project_kernel,
        grid=(seq // rows,),
        in_specs=[spec(pltpu.SMEM), whole(x_in), block, whole(vecs)] + [spec(pltpu.HBM)] * 12,
        out_specs=[
            pl.BlockSpec((tok, width), lambda i: (0, 0)),
            block,
            block,
            pl.BlockSpec((1, width, rows), lambda i: (i, 0, 0)),
        ],
        out_shape=[
            shape((tok, width), bf16), shape((seq, width), bf16), shape((seq, width), bf16),
            shape((seq // rows, width, rows), bf16),
        ],
        scratch_shapes=[pltpu.VMEM((width, width), bf16)] * 3 + [pltpu.SemaphoreType.DMA((12,))],
        compiler_params=pltpu.CompilerParams(vmem_limit_bytes=VMEM_LIMIT),
        cost_estimate=NO_COST,
        name="project",
    )(me, x_in, x_all, vecs, *wq, *wk, *wv)


def attend_kernel(chunks, q_ref, k_ref, v_ref, extra_ref, doc_ref, attn_ref, low_ref, low_t_ref, lse_ref, s_ref):
    rows = k_ref.shape[0] // chunks
    q_t = q_ref[...].astype(f32).T
    bias = _extra_rows(doc_ref[...])
    outs = []
    for half in range(2):
        q_aug = jnp.concatenate(
            [jnp.where(_half_mask(q_t.shape, 0, half), q_t, 0.0).astype(bf16), bias], axis=0
        )
        top = None
        for c in range(chunks):
            at = pl.ds(c * rows, rows)
            k_aug = jnp.concatenate([k_ref[at, :], extra_ref[at, :]], axis=1)
            s_now = jnp.dot(k_aug, q_aug, preferred_element_type=f32)
            s_ref[half, at, :] = s_now
            top_now = jnp.max(s_now, axis=0, keepdims=True)
            top = top_now if top is None else jnp.maximum(top, top_now)
        total = jnp.zeros_like(top)
        mixed = jnp.zeros((2 * HEAD_DIM, q_t.shape[1]), f32)
        for c in range(chunks):
            at = pl.ds(c * rows, rows)
            p_now = jnp.exp(s_ref[half, at, :] - top)
            total = total + jnp.sum(p_now, axis=0, keepdims=True)
            mixed = mixed + cross_rows(v_ref[at, :], p_now.astype(bf16))
        lse_ref[0, pl.ds(half, 1), :] = top + jnp.log(total)
        outs.append(mixed[half * HEAD_DIM : (half + 1) * HEAD_DIM] / total)
    out_t = jnp.concatenate(outs, axis=0)
    attn_ref[...] = out_t
    low_ref[...] = out_t.T.astype(bf16)
    low_t_ref[...] = out_t.astype(bf16)


def attend(query, keys, values, extra, docs):
    tok, width = query.shape
    seq = keys.shape[0]
    lanes = 2 * HEAD_DIM
    pairs = width // lanes
    shape = jax.ShapeDtypeStruct
    return pl.pallas_call(
        functools.partial(attend_kernel, 4),
        grid=(pairs,),
        in_specs=[
            pl.BlockSpec((tok, lanes), lambda p: (0, p)),
            pl.BlockSpec((seq, lanes), lambda p: (0, p)),
            pl.BlockSpec((seq, lanes), lambda p: (0, p)),
            pl.BlockSpec((seq, lanes), lambda p: (0, 0)),
            pl.BlockSpec((1, tok), lambda p: (0, 0)),
        ],
        out_specs=[
            pl.BlockSpec((lanes, tok), lambda p: (p, 0)),
            pl.BlockSpec((tok, lanes), lambda p: (0, p)),
            pl.BlockSpec((lanes, tok), lambda p: (p, 0)),
            pl.BlockSpec((1, 2, tok), lambda p: (p, 0, 0)),
        ],
        out_shape=[
            shape((width, tok), f32), shape((tok, width), bf16), shape((width, tok), bf16),
            shape((pairs, 2, tok), f32),
        ],
        scratch_shapes=[pltpu.VMEM((2, seq, tok), f32)],
        compiler_params=pltpu.CompilerParams(vmem_limit_bytes=VMEM_LIMIT),
        cost_estimate=NO_COST,
        name="attend",
    )(query, keys, values, extra, docs)


def attend_back_kernel(
    chunks, q_ref, k_ref, v_ref, extra_ref, doc_ref, attn_ref, lse_ref, g_ref, *more
):
    dq_ref, dk_ref, dv_ref = more[-3:]
    rows = k_ref.shape[0] // chunks
    q_low = q_ref[...]
    g_low = g_ref[...]
    q_t = q_low.astype(f32).T
    g_t = g_low.astype(f32).T
    prod = attn_ref[...] * g_t
    lanes = 2 * HEAD_DIM
    q_side, g_side, q_rows, g_rows = [], [], [], []
    for half in range(2):
        pick = _half_mask(q_t.shape, 0, half)
        delta = jnp.sum(prod[half * HEAD_DIM : (half + 1) * HEAD_DIM], axis=0, keepdims=True)
        q_side.append(
            jnp.concatenate(
                [
                    jnp.where(pick, q_t, 0.0).astype(bf16),
                    _extra_rows(doc_ref[...], -lse_ref[0, pl.ds(half, 1), :]),
                ],
                axis=0,
            )
        )
        g_side.append(
            jnp.concatenate(
                [
                    jnp.where(pick, g_t, 0.0).astype(bf16),
                    _extra_rows(jnp.full_like(doc_ref[...], -1), -delta)
                    * (lax.broadcasted_iota(jnp.int32, (128, q_t.shape[1]), 0) >= NDOC).astype(bf16),
                ],
                axis=0,
            )
        )
        pick_lane = _half_mask(q_low.shape, 1, half)
        q_rows.append(jnp.where(pick_lane, q_low.astype(f32), 0.0).astype(bf16))
        g_rows.append(jnp.where(pick_lane, g_low.astype(f32), 0.0).astype(bf16))
    q_rows = jnp.concatenate(q_rows, axis=0)
    g_rows = jnp.concatenate(g_rows, axis=0)
    dq_t = [jnp.zeros((lanes, q_t.shape[1]), f32) for half in range(2)]
    for c in range(chunks):
        at = pl.ds(c * rows, rows)
        k_now = k_ref[at, :]
        extra = extra_ref[at, :]
        k_aug = jnp.concatenate([k_now, extra], axis=1)
        v_aug = jnp.concatenate([v_ref[at, :], extra], axis=1)
        p_low, s_low = [], []
        for half in range(2):
            prob = jnp.exp(jnp.dot(k_aug, q_side[half], preferred_element_type=f32))
            slope = jnp.dot(v_aug, g_side[half], preferred_element_type=f32)
            p_low.append(prob.astype(bf16))
            s_low.append((prob * slope).astype(bf16))
            dq_t[half] = dq_t[half] + cross_rows(k_now, s_low[half])
        dk_ref[at, :] = jnp.dot(
            jnp.concatenate(s_low, axis=1), q_rows, preferred_element_type=f32
        ).astype(bf16)
        dv_ref[at, :] = jnp.dot(
            jnp.concatenate(p_low, axis=1), g_rows, preferred_element_type=f32
        ).astype(bf16)
    pick = _half_mask(q_t.shape, 0, 0)
    dq_ref[...] = (jnp.where(pick, dq_t[0], dq_t[1]).T * (1.0 / math.sqrt(HEAD_DIM))).astype(bf16)


def attend_back(first, pairs, so_far, query, keys, values, extra, docs, attn_t, lse, grad_attn):
    tok, width = query.shape
    seq = keys.shape[0]
    lanes = 2 * HEAD_DIM
    columns = lambda rows: pl.BlockSpec((rows, lanes), lambda p: (0, p + first))
    shape = lambda rows: jax.ShapeDtypeStruct((rows, width), bf16)
    return pl.pallas_call(
        functools.partial(attend_back_kernel, max(2, seq // 1024)),
        grid=(pairs,),
        in_specs=[
            columns(tok),
            columns(seq),
            columns(seq),
            pl.BlockSpec((seq, lanes), lambda p: (0, 0)),
            pl.BlockSpec((1, tok), lambda p: (0, 0)),
            pl.BlockSpec((lanes, tok), lambda p: (p + first, 0)),
            pl.BlockSpec((1, 2, tok), lambda p: (p + first, 0, 0)),
            columns(tok),
        ]
        + [spec(pltpu.HBM)] * len(so_far),
        out_specs=[columns(tok), columns(seq), columns(seq)],
        out_shape=[shape(tok), shape(seq), shape(seq)],
        input_output_aliases={8 + k: k for k in range(len(so_far))},
        compiler_params=pltpu.CompilerParams(vmem_limit_bytes=VMEM_LIMIT),
        cost_estimate=NO_COST,
        name="attend_back",
    )(query, keys, values, extra, docs, attn_t, lse, grad_attn, *so_far)


VEC_QUERY, VEC_VALUE, VEC_OUT, VEC_GAIN1, VEC_BIAS1, VEC_DOWN, VEC_GAIN2, VEC_BIAS2, VEC_UP = range(9)
VEC_POOL, VEC_CLASS = 12, 15
NO_COST = pl.CostEstimate(flops=0, transcendentals=0, bytes_accessed=0)


def spec(space=pltpu.VMEM):
    return pl.BlockSpec(memory_space=space)


def fetch_start(pieces, target, sems, first, me):
    rows = pieces[0].shape[0]
    copies = []
    for r, piece in enumerate(pieces):
        at = pl.multiple_of((me ^ r) * rows, rows)
        copy = pltpu.make_async_copy(piece, target.at[pl.ds(at, rows), :], sems.at[first + r])
        copy.start()
        copies.append(copy)
    return copies


def fetch_wait(copies):
    for copy in copies:
        copy.wait()


def norm_parts(field):
    centre = field - jnp.mean(field, axis=-1, keepdims=True)
    inv_std = lax.rsqrt(jnp.mean(centre * centre, axis=-1, keepdims=True) + norm_eps)
    return centre * inv_std, inv_std


def norm_back(grad_in, normed, inv_std, gain_row):
    scaled = grad_in * gain_row
    return inv_std * (
        scaled
        - jnp.mean(scaled, axis=-1, keepdims=True)
        - normed * jnp.mean(scaled * normed, axis=-1, keepdims=True)
    )


def column_sum(value):
    return jnp.sum(value.astype(f32), axis=0, keepdims=True)


def student_tables(mats):
    width_part = mats.shape[1] - 64
    ws = jnp.concatenate([mats[k, :width_part] for k in range(mats.shape[0])], axis=0)
    wp = jnp.concatenate([mats[k, width_part : width_part + 32] for k in range(mats.shape[0])], axis=0)
    wc = jnp.concatenate([mats[k, width_part + 32 :] for k in range(mats.shape[0])], axis=0)
    return ws, wp, wc


def halves_sum(value):
    lane = lax.broadcasted_iota(jnp.int32, value.shape, 1)
    half = value.shape[1] // POOL_HEADS
    low = jnp.sum(jnp.where(lane < half, value, 0.0), axis=1, keepdims=True)
    high = jnp.sum(jnp.where(lane < half, 0.0, value), axis=1, keepdims=True)
    return jnp.where(lane < half, low, high)


def of_docs(doc, rows):
    out = jnp.where(doc == 0, rows[0], 0.0)
    for k in range(1, NDOC):
        out = jnp.where(doc == k, rows[k], out)
    return out


def forward_kernel(
    me_ref, attn_ref, x_ref, vec_ref, mats_ref, doc_ref,
    wo0, wo1, wo2, wo3, wu0, wu1, wu2, wu3, wd0, wd1, wd2, wd3,
    hid_t_ref, normed1_ref, inv1_ref, act_ref, slope_ref,
    out_ref, normed2_ref, inv2_ref, student_ref, score_ref, part_ref,
    wo_ref, wu_ref, wd_ref, sems,
):
    me = me_ref[0]
    go_o = fetch_start((wo0, wo1, wo2, wo3), wo_ref, sems, 0, me)
    go_u = fetch_start((wu0, wu1, wu2, wu3), wu_ref, sems, 4, me)
    go_d = fetch_start((wd0, wd1, wd2, wd3), wd_ref, sems, 8, me)
    vec = lambda k: vec_ref[pl.ds(k, 1), :]
    fetch_wait(go_o)
    branch = jnp.dot(attn_ref[...], wo_ref[...], preferred_element_type=f32) + vec(VEC_OUT)
    normed, inv_std = norm_parts(x_ref[...].astype(f32) + branch)
    normed1_ref[...] = normed
    inv1_ref[...] = inv_std
    hidden = normed * vec(VEC_GAIN1) + vec(VEC_BIAS1)
    hid_t_ref[...] = hidden.T.astype(bf16)
    hid_low = hidden.astype(bf16)
    width = hidden.shape[1]
    fetch_wait(go_u)
    down = None
    for j in range(wu_ref.shape[1] // width):
        at = pl.ds(j * width, width)
        pre = jnp.dot(hid_low, wu_ref[:, at], preferred_element_type=f32) + vec(VEC_UP + j)
        cdf = 0.5 * (1.0 + lax.erf(pre * (1.0 / math.sqrt(2.0))))
        pdf = jnp.exp(-0.5 * pre * pre) * (1.0 / math.sqrt(2.0 * math.pi))
        slope_ref[:, at] = (cdf + pre * pdf).astype(bf16)
        act = (pre * cdf).astype(bf16)
        act_ref[:, at] = act
        if j == 0:
            fetch_wait(go_d)
        term = jnp.dot(act, wd_ref[at, :], preferred_element_type=f32)
        down = term if down is None else down + term
    normed, inv_std = norm_parts(hidden + (down + vec(VEC_DOWN)))
    normed2_ref[...] = normed
    inv2_ref[...] = inv_std
    out_low = (normed * vec(VEC_GAIN2) + vec(VEC_BIAS2)).astype(bf16)
    out_ref[...] = out_low
    ws, _, _ = student_tables(mats_ref[...])
    pool = ws.shape[1]
    student = jnp.dot(out_low, ws, preferred_element_type=f32) + vec(VEC_POOL)[:, :pool]
    student_ref[...] = student
    scale = 1.0 / math.sqrt(pool // POOL_HEADS)
    score = halves_sum(student * vec(VEC_POOL + 1)[:, :pool]) * scale
    score_ref[...] = score
    doc = doc_ref[...]
    tops = [
        jnp.max(jnp.where(doc == k, score, big_negative), axis=0, keepdims=True) for k in range(NDOC)
    ]
    weight = jnp.exp(score - of_docs(doc, tops))
    mixed = weight * student
    totals = [jnp.sum(jnp.where(doc == k, weight, 0.0), axis=0, keepdims=True) for k in range(NDOC)]
    sums = [jnp.sum(jnp.where(doc == k, mixed, 0.0), axis=0, keepdims=True) for k in range(NDOC)]
    part_ref[...] = jnp.concatenate(tops + totals + sums + [jnp.zeros((4, pool), f32)], axis=0)


def layer_forward_call(me, attn, x_in, vecs, mats, doc, wo, wu, wd):
    tok, width = x_in.shape
    hidden = wu[0].shape[1]
    pool = mats.shape[2]
    shape = jax.ShapeDtypeStruct
    return pl.pallas_call(
        forward_kernel,
        in_specs=[spec(pltpu.SMEM)] + [spec()] * 5 + [spec(pltpu.HBM)] * 12,
        out_specs=[spec()] * 11,
        out_shape=[
            shape((width, tok), bf16), shape((tok, width), f32), shape((tok, 1), f32),
            shape((tok, hidden), bf16), shape((tok, hidden), bf16),
            shape((tok, width), bf16), shape((tok, width), f32), shape((tok, 1), f32),
            shape((tok, pool), f32), shape((tok, pool), f32), shape((16, pool), f32),
        ],
        scratch_shapes=[
            pltpu.VMEM((width, width), bf16), pltpu.VMEM((width, hidden), bf16),
            pltpu.VMEM((hidden, width), bf16), pltpu.SemaphoreType.DMA((12,)),
        ],
        compiler_params=pltpu.CompilerParams(vmem_limit_bytes=VMEM_LIMIT),
        cost_estimate=NO_COST,
        name="layer_forward",
    )(me, attn, x_in, vecs, mats, doc, *wo, *wu, *wd)


def exact_dot(left, right, dims):
    return lax.dot_general(
        left, right, (dims, ((), ())), precision=lax.Precision.HIGHEST, preferred_element_type=f32
    )


def head_kernel(
    label_ref, owner_ref, parts_ref, vec_ref, mats_ref, doc_ref, student_ref, score_ref, out_ref, cot_ref,
    normed2_ref, inv2_ref,
    down_ref, res2_ref, logits_ref, vec_grad_ref, tables_ref,
):
    vec = lambda k: vec_ref[pl.ds(k, 1), :]
    ws, wp, wc = student_tables(mats_ref[...])
    pool = ws.shape[1]
    wp, wc = wp.astype(f32), wc.astype(f32)
    tops = jnp.max(parts_ref[:, 0:NDOC, :], axis=0)
    factor = jnp.exp(parts_ref[:, 0:NDOC, :] - tops[None])
    totals = jnp.sum(parts_ref[:, NDOC : 2 * NDOC, :] * factor, axis=0)
    pooled = jnp.sum(parts_ref[:, 2 * NDOC : 3 * NDOC, :] * factor, axis=0) / totals
    pooled = jnp.concatenate([pooled, jnp.zeros((8 - NDOC, pool), f32)], axis=0)
    act = jnp.tanh(exact_dot(pooled, wp, ((1,), (0,))) + vec(VEC_POOL + 2)[:, :pool])
    logits = exact_dot(act, wc, ((1,), (0,))) + vec(VEC_CLASS)[:, :pool]
    logits_ref[...] = logits
    lane = lax.broadcasted_iota(jnp.int32, logits.shape, 1)
    row = lax.broadcasted_iota(jnp.int32, logits.shape, 0)
    shown = jnp.where(lane < CLASSES, logits, big_negative)
    shown = jnp.exp(shown - jnp.max(shown, axis=1, keepdims=True))
    grad_logits = shown / jnp.sum(shown, axis=1, keepdims=True)
    for k in range(NDOC):
        grad_logits = grad_logits - jnp.where((row == k) & (lane == label_ref[0, k]), 1.0, 0.0)
    grad_logits = jnp.where(row < NDOC, grad_logits, 0.0)
    owner = (owner_ref[0] == 0).astype(f32)
    grad_wc = exact_dot(act, grad_logits, ((0,), (0,))) * owner
    grad_pre = exact_dot(grad_logits, wc, ((1,), (1,))) * (1.0 - act * act)
    grad_wp = exact_dot(pooled, grad_pre, ((0,), (0,))) * owner
    grad_pooled = exact_dot(grad_pre, wp, ((1,), (1,)))
    doc = doc_ref[...]
    student = student_ref[...]
    each = lambda table: [table[k : k + 1] for k in range(NDOC)]
    weight = jnp.exp(score_ref[...] - of_docs(doc, each(tops))) / of_docs(doc, each(totals))
    tok_grad = of_docs(doc, each(grad_pooled))
    grad_score = weight * halves_sum(tok_grad * (student - of_docs(doc, each(pooled))))
    scale = 1.0 / math.sqrt(pool // POOL_HEADS)
    grad_student = weight * tok_grad + grad_score * vec(VEC_POOL + 1)[:, :pool] * scale
    grad_low = grad_student.astype(bf16)
    out_low = out_ref[...]
    grad_ws = cross_rows(out_low, grad_low)
    blocks, rows = mats_ref.shape[0], mats_ref.shape[1]
    high = rows - 64
    for k in range(blocks):
        tables_ref[k, 0:high, :] = grad_ws[k * high : (k + 1) * high]
        tables_ref[k, high : high + 32, :] = grad_wp[32 * k : 32 * k + 32]
        tables_ref[k, high + 32 : high + 64, :] = grad_wc[32 * k : 32 * k + 32]
    grad_layer = cot_ref[...].astype(f32) + back_mul(grad_low, ws)
    normed = normed2_ref[...]
    grad_res = norm_back(grad_layer, normed, inv2_ref[...], vec(VEC_GAIN2))
    res2_ref[...] = grad_res
    low = grad_res.astype(bf16)
    down_ref[...] = low
    width = normed.shape[1]
    wide = lambda v: jnp.concatenate([v, jnp.zeros((1, width - pool), f32)], axis=1)
    rows = [
        column_sum(low),
        column_sum(grad_layer * normed),
        column_sum(grad_layer),
        wide(column_sum(grad_low)),
        wide(column_sum(grad_score * student) * scale),
        wide(column_sum(grad_pre) * owner),
        wide(column_sum(grad_logits) * owner),
        jnp.zeros((1, width), f32),
    ]
    vec_grad_ref[...] = jnp.concatenate(rows, axis=0)


def head_call(labels, owner, parts, vecs, mats, doc, student, score, out_low, cot, normed2, inv2):
    tok, width = out_low.shape
    shape = jax.ShapeDtypeStruct
    return pl.pallas_call(
        head_kernel,
        in_specs=[spec(pltpu.SMEM)] * 2 + [spec()] * 10,
        out_specs=[spec()] * 5,
        out_shape=[
            shape((tok, width), bf16), shape((tok, width), f32), shape((8, mats.shape[2]), f32),
            shape((8, width), f32), shape(mats.shape, f32),
        ],
        compiler_params=pltpu.CompilerParams(vmem_limit_bytes=VMEM_LIMIT),
        cost_estimate=NO_COST,
        name="head",
    )(labels, owner, parts, vecs, mats, doc, student, score, out_low, cot, normed2, inv2)


def backward_kernel(
    me_ref, low_ref, res2_ref, slope_ref, normed1_ref, inv1_ref, vec_ref,
    wo0, wo1, wo2, wo3, wu0, wu1, wu2, wu3, wd0, wd1, wd2, wd3,
    up_ref, res1_ref, branch_ref, attn_ref, vec_grad_ref,
    wo_ref, wu_ref, wd_ref, sems,
):
    me = me_ref[0]
    go_d = fetch_start((wd0, wd1, wd2, wd3), wd_ref, sems, 8, me)
    go_u = fetch_start((wu0, wu1, wu2, wu3), wu_ref, sems, 4, me)
    go_o = fetch_start((wo0, wo1, wo2, wo3), wo_ref, sems, 0, me)
    low = low_ref[...]
    width = low.shape[1]
    fetch_wait(go_d)
    total = res2_ref[...]
    rows = []
    for j in range(wu_ref.shape[1] // width):
        at = pl.ds(j * width, width)
        up = (back_mul(low, wd_ref[at, :]) * slope_ref[:, at].astype(f32)).astype(bf16)
        up_ref[:, at] = up
        rows.append(column_sum(up))
        if j == 0:
            fetch_wait(go_u)
        total = total + back_mul(up, wu_ref[:, at])
    normed = normed1_ref[...]
    rows += [column_sum(total * normed), column_sum(total)]
    grad_res = norm_back(total, normed, inv1_ref[...], vec_ref[pl.ds(VEC_GAIN1, 1), :])
    res1_ref[...] = grad_res
    branch = grad_res.astype(bf16)
    branch_ref[...] = branch
    rows += [column_sum(branch), jnp.zeros((1, width), f32)]
    vec_grad_ref[...] = jnp.concatenate(rows, axis=0)
    fetch_wait(go_o)
    attn_ref[...] = back_mul(branch, wo_ref[...]).astype(bf16)


def layer_backward_call(me, low, res2, slope, normed1, inv1, vecs, wo, wu, wd):
    tok, width = low.shape
    hidden = wu[0].shape[1]
    shape = jax.ShapeDtypeStruct
    return pl.pallas_call(
        backward_kernel,
        in_specs=[spec(pltpu.SMEM)] + [spec()] * 6 + [spec(pltpu.HBM)] * 12,
        out_specs=[spec()] * 5,
        out_shape=[
            shape((tok, hidden), bf16), shape((tok, width), f32), shape((tok, width), bf16),
            shape((tok, width), bf16), shape((8, width), f32),
        ],
        scratch_shapes=[
            pltpu.VMEM((width, width), bf16), pltpu.VMEM((width, hidden), bf16),
            pltpu.VMEM((hidden, width), bf16), pltpu.SemaphoreType.DMA((12,)),
        ],
        compiler_params=pltpu.CompilerParams(vmem_limit_bytes=VMEM_LIMIT),
        cost_estimate=NO_COST,
        name="layer_backward",
    )(me, low, res2, slope, normed1, inv1, vecs, *wo, *wu, *wd)


def down_grad_kernel(order_ref, act_ref, grad_ref, send_ref, keep_ref):
    term = cross_rows(act_ref[...], grad_ref[...]).astype(bf16)
    half = send_ref.shape[0]

    @pl.when(pl.program_id(0) < pl.num_programs(0) // 2)
    def _():
        send_ref[0] = term

    @pl.when(pl.program_id(0) >= pl.num_programs(0) // 2)
    def _():
        keep_ref[0] = term


def send_keep_specs(block):
    nd = len(block)
    zero = (0,) * (nd - 1)
    return [
        pl.BlockSpec(block, lambda i, s: (jnp.minimum(i, 1),) + zero),
        pl.BlockSpec(block, lambda i, s: (jnp.maximum(i - 2, 0),) + zero),
    ]


def down_grad(blocks, act, grad):
    tok, hidden = act.shape
    width = grad.shape[1]
    part = hidden // 4
    shape = jax.ShapeDtypeStruct((2, part, width), bf16)
    return pl.pallas_call(
        down_grad_kernel,
        grid_spec=pltpu.PrefetchScalarGridSpec(
            num_scalar_prefetch=1,
            grid=(4,),
            in_specs=[
                pl.BlockSpec((tok, part), lambda i, s: (0, s[i])),
                pl.BlockSpec((tok, width), lambda i, s: (0, 0)),
            ],
            out_specs=send_keep_specs((1, part, width)),
        ),
        out_shape=[shape, shape],
        compiler_params=pltpu.CompilerParams(vmem_limit_bytes=VMEM_LIMIT),
        cost_estimate=NO_COST,
        name="down_grad",
    )(blocks, act, grad)


def middle_grad_kernel(order_ref, hid_ref, up_ref, attn_ref, branch_ref, tables_ref, vec_a_ref, vec_b_ref, send_ref, keep_ref):
    part = attn_ref.shape[0]
    width = branch_ref.shape[1]
    pool = tables_ref.shape[2]
    half = width // 2

    def put(out):
        base = 0
        for j in range(up_ref.shape[1] // width):
            out[0, base : base + part, :] = jnp.dot(
                hid_ref[...], up_ref[:, j * width : (j + 1) * width], preferred_element_type=f32
            ).astype(bf16)
            base += part
        out[0, base : base + part, :] = jnp.dot(
            attn_ref[...], branch_ref[...], preferred_element_type=f32
        ).astype(bf16)
        base += part
        high = tables_ref.shape[1] - 64
        step = high * pool // width
        out[0, base : base + step, :] = jnp.concatenate(
            [tables_ref[0, k * step : (k + 1) * step, :] for k in range(width // pool)], axis=1
        ).astype(bf16)
        rows = jnp.concatenate([vec_a_ref[...], vec_b_ref[...]], axis=0)
        rows = jnp.concatenate([rows[:, :half], rows[:, half:]], axis=0)
        out[0, base + step : base + step + 32, :] = jnp.concatenate(
            [
                tables_ref[0, high : high + 32, :],
                tables_ref[0, high + 32 : high + 64, :],
                rows,
                jnp.zeros((32, width - 2 * pool - half), f32),
            ],
            axis=1,
        ).astype(bf16)

    pl.when(pl.program_id(0) < 2)(lambda: put(send_ref))
    pl.when(pl.program_id(0) >= 2)(lambda: put(keep_ref))


def middle_grad(blocks, hid_t, up, attn_t, branch, tables, vec_a, vec_b):
    width, tok = attn_t.shape
    part = width // 4
    hidden = up.shape[1]
    rows = hidden // 4 + part + 64
    shape = jax.ShapeDtypeStruct((2, rows, width), bf16)
    return pl.pallas_call(
        middle_grad_kernel,
        grid_spec=pltpu.PrefetchScalarGridSpec(
            num_scalar_prefetch=1,
            grid=(4,),
            in_specs=[
                pl.BlockSpec((part, tok), lambda i, s: (s[i], 0)),
                pl.BlockSpec((tok, hidden), lambda i, s: (0, 0)),
                pl.BlockSpec((part, tok), lambda i, s: (s[i], 0)),
                pl.BlockSpec((tok, width), lambda i, s: (0, 0)),
                pl.BlockSpec((1,) + tables.shape[1:], lambda i, s: (s[i], 0, 0)),
                pl.BlockSpec(vec_a.shape, lambda i, s: (0, 0)),
                pl.BlockSpec(vec_b.shape, lambda i, s: (0, 0)),
            ],
            out_specs=send_keep_specs((1, rows, width)),
        ),
        out_shape=[shape, shape],
        compiler_params=pltpu.CompilerParams(vmem_limit_bytes=VMEM_LIMIT),
        cost_estimate=NO_COST,
        name="middle_grad",
    )(blocks, hid_t, up, attn_t, branch, tables, vec_a, vec_b)


def last_grad_kernel(order_ref, xt_ref, xt_all_ref, dq_ref, dk_ref, dv_ref, send_ref, keep_ref):
    part = xt_ref.shape[0]

    def put(out):
        for k, (left, right) in enumerate(((xt_ref, dq_ref), (xt_all_ref, dk_ref), (xt_all_ref, dv_ref))):
            out[0, k * part : (k + 1) * part, :] = jnp.dot(
                left[...], right[...], preferred_element_type=f32
            ).astype(bf16)
        width = dq_ref.shape[1]
        rows = jnp.concatenate(
            [column_sum(dq_ref[...]), column_sum(dv_ref[...]), jnp.zeros((62, width), f32)], axis=0
        )
        out[0, 3 * part :, :] = rows.astype(bf16)

    pl.when(pl.program_id(0) < 2)(lambda: put(send_ref))
    pl.when(pl.program_id(0) >= 2)(lambda: put(keep_ref))


def last_grad(blocks, position, x_all_t, dq, dk, dv):
    tok, width = dq.shape
    seq = dk.shape[0]
    x_all_t = x_all_t.transpose(1, 0, 2).reshape(width, seq)
    part = width // 4
    rows = 3 * part + 64
    shape = jax.ShapeDtypeStruct((2, rows, width), bf16)
    whole = lambda r: pl.BlockSpec((r, width), lambda i, s: (0, 0), pipeline_mode=pl.Buffered(1))
    return pl.pallas_call(
        last_grad_kernel,
        grid_spec=pltpu.PrefetchScalarGridSpec(
            num_scalar_prefetch=1,
            grid=(4,),
            in_specs=[
                pl.BlockSpec((part, tok), lambda i, s: (s[i], s[4])),
                pl.BlockSpec((part, seq), lambda i, s: (s[i], 0)),
                whole(tok),
                whole(seq),
                whole(seq),
            ],
            out_specs=send_keep_specs((1, rows, width)),
        ),
        out_shape=[shape, shape],
        compiler_params=pltpu.CompilerParams(vmem_limit_bytes=VMEM_LIMIT),
        cost_estimate=NO_COST,
        name="last_grad",
    )(jnp.concatenate([blocks, position]), x_all_t, x_all_t, dq, dk, dv)


def others_kernel(
    order_ref, me_ref, q_ref, res_ref, k_ref, v_ref,
    wk0, wk1, wk2, wk3, wv0, wv1, wv2, wv3, wq0, wq1, wq2, wq3,
    send_ref, keep_ref, near_ref, wk_ref, wv_ref, wq_ref, sems,
):
    step = pl.program_id(0)
    half = pl.num_programs(0) // 2
    start = lambda pieces, target, first: fetch_start(pieces, target, sems, first, me_ref[0])

    @pl.when(step == 0)
    def _():
        copies = start((wk0, wk1, wk2, wk3), wk_ref, 0) + start((wv0, wv1, wv2, wv3), wv_ref, 4)
        query = start((wq0, wq1, wq2, wq3), wq_ref, 8)
        fetch_wait(query)
        near_ref[...] = res_ref[...] + back_mul(q_ref[...], wq_ref[...])
        fetch_wait(copies)

    flat = lambda ref: ref[...].reshape(-1, ref.shape[-1])
    term = back_mul(flat(k_ref), wk_ref[...]) + back_mul(flat(v_ref), wv_ref[...])
    term = term.astype(bf16).reshape(send_ref.shape)

    @pl.when(step < half)
    def _():
        send_ref[...] = term

    @pl.when(step >= half)
    def _():
        keep_ref[...] = term


def others_call(order, me, dq, res, dk, dv, wk, wv, wq, rows):
    seq, width = dk.shape
    tok = res.shape[0]
    half = seq // rows // 2
    group = 2 if half % 2 == 0 else 1
    n = half // group
    block = pl.BlockSpec((group, 1, rows, width), lambda i, s: (i % n, s[i // n], 0, 0))
    whole = lambda v: pl.BlockSpec(v.shape, lambda i, s: (0, 0), pipeline_mode=pl.Buffered(1))
    shape = jax.ShapeDtypeStruct((half, rows, width), bf16)
    cut = lambda v: v.reshape(half, 2, rows, width)
    return pl.pallas_call(
        others_kernel,
        grid_spec=pltpu.PrefetchScalarGridSpec(
            num_scalar_prefetch=1,
            grid=(2 * n,),
            in_specs=[spec(pltpu.SMEM), whole(dq), whole(res), block, block] + [spec(pltpu.HBM)] * 12,
            out_specs=[
                pl.BlockSpec((group, rows, width), lambda i, s: (jnp.minimum(i, n - 1), 0, 0)),
                pl.BlockSpec((group, rows, width), lambda i, s: (jnp.maximum(i - n, 0), 0, 0)),
                pl.BlockSpec((tok, width), lambda i, s: (0, 0)),
            ],
            scratch_shapes=[pltpu.VMEM((width, width), bf16)] * 3 + [pltpu.SemaphoreType.DMA((12,))],
        ),
        out_shape=[shape, shape, jax.ShapeDtypeStruct((tok, width), f32)],
        compiler_params=pltpu.CompilerParams(vmem_limit_bytes=VMEM_LIMIT),
        cost_estimate=NO_COST,
        name="others",
    )(order, me, dq, res, cut(dk), cut(dv), *wk, *wv, *wq)


def finish_kernel(
    core_ref, me_ref, q_hbm, k_hbm, v_hbm, x_hbm, res_ref,
    wk0, wk1, wk2, wk3, wv0, wv1, wv2, wv3, wq0, wq1, wq2, wq3,
    send_ref, keep_ref, far_ref, own_ref, near_ref,
    q_ref, x_ref, k_ref, v_ref, wk_ref, wv_ref, wq_ref, term_ref, sems, block_sems,
):
    core, mine = core_ref[0], core_ref[1] % 2
    count, rows = x_hbm.shape[0], q_ref.shape[0]
    half = count // 2
    me = me_ref[0]
    query = pltpu.make_async_copy(q_hbm, q_ref, sems.at[16])
    query.start()
    token = pltpu.make_async_copy(x_hbm.at[core_ref[1]], x_ref.at[2 * half], sems.at[17])
    token.start()
    tokens = [
        pltpu.make_async_copy(
            x_hbm.at[2 * (n % half) + jnp.where(n < half, 1 - mine, mine)], x_ref.at[n], block_sems.at[n]
        )
        for n in range(count)
    ]
    for copy in tokens:
        copy.start()

    def sorted_copies(src, dst, first):
        return [
            pltpu.make_async_copy(
                src.at[:, 1 - mine if n == 0 else mine], dst.at[n], sems.at[first + n]
            )
            for n in range(2)
        ]

    keys = sorted_copies(k_hbm, k_ref, 12)
    values = sorted_copies(v_hbm, v_ref, 14)
    for copy in keys + values:
        copy.start()
    weights = fetch_start((wk0, wk1, wk2, wk3), wk_ref, sems, 0, me)
    weights += fetch_start((wv0, wv1, wv2, wv3), wv_ref, sems, 4, me)
    weights += fetch_start((wq0, wq1, wq2, wq3), wq_ref, sems, 8, me)
    part = wq_ref.shape[0] // 4
    width = wq_ref.shape[1]

    def put(row, term):
        term_ref[0:width, :] = term
        for out, c in ((send_ref, 1 - core), (keep_ref, core)):
            for far in range(2):
                at = pl.multiple_of((2 * far + c) * part, part)
                out[far, row * part : (row + 1) * part, :] = term_ref[pl.ds(at, part), :].astype(bf16)

    query.wait()
    token.wait()
    put(0, jnp.dot(x_ref[2 * half], q_ref[...], preferred_element_type=f32))
    for copy in tokens:
        copy.wait()
    left = jnp.concatenate([x_ref[n] for n in range(count)], axis=1)
    for row, ref, copies in ((1, k_ref, keys), (2, v_ref, values)):
        for copy in copies:
            copy.wait()
        put(row, jnp.dot(left, ref[...].reshape(count * rows, width), preferred_element_type=f32))
    sums = column_sum(v_ref[...].reshape(count * rows, width))
    last = jnp.concatenate([column_sum(q_ref[...]), sums, jnp.zeros((62, width), f32)], axis=0).astype(bf16)
    for out in (send_ref, keep_ref):
        for far in range(2):
            out[far, 3 * part :, :] = last
    fetch_wait(weights)
    near_ref[...] = res_ref[...] + back_mul(q_ref[...], wq_ref[...])
    for n, out in ((0, far_ref), (1, own_ref)):
        term = back_mul(k_ref[n].reshape(half * rows, width), wk_ref[...])
        term = term + back_mul(v_ref[n].reshape(half * rows, width), wv_ref[...])
        out[...] = term.astype(bf16).reshape(half, rows, width)


def finish(core_position, me, dq, dk, dv, x_all_t, res, wk, wv, wq):
    count, width, rows = x_all_t.shape
    half = count // 2
    part = width // 4
    shape = jax.ShapeDtypeStruct
    grads = shape((2, 3 * part + 64, width), bf16)
    others = shape((half, rows, width), bf16)
    cut = lambda v: v.reshape(half, 2, rows, width)
    hbm = spec(pltpu.HBM)
    vmem = lambda *dims: pltpu.VMEM(dims, bf16)
    return pl.pallas_call(
        finish_kernel,
        in_specs=[spec(pltpu.SMEM)] * 2 + [hbm] * 4 + [spec()] + [hbm] * 12,
        out_specs=[spec()] * 5,
        out_shape=[grads, grads, others, others, shape((rows, width), f32)],
        scratch_shapes=[
            vmem(rows, width), vmem(count + 1, width, rows), vmem(2, half, rows, width), vmem(2, half, rows, width),
            vmem(width, width), vmem(width, width), vmem(width, width),
            pltpu.VMEM((width, width), f32), pltpu.SemaphoreType.DMA((18,)), pltpu.SemaphoreType.DMA((count,)),
        ],
        compiler_params=pltpu.CompilerParams(vmem_limit_bytes=VMEM_LIMIT),
        cost_estimate=NO_COST,
        name="finish",
    )(core_position, me, dq, cut(dk), cut(dv), x_all_t, res, *wk, *wv, *wq)


def pack_kernel(me_ref, *refs):
    vectors, (up_ref, bs_ref, qp_ref, bp_ref, bc_ref), out_ref = refs[:8], refs[8:13], refs[13]
    part = vectors[0].shape[1]
    small = bs_ref.shape[1]
    width = out_ref.shape[1]
    out_ref[...] = jnp.zeros(out_ref.shape, f32)
    for k in range(width // part):

        @pl.when(me_ref[0] == k)
        def _():
            for row, ref in enumerate(vectors):
                out_ref[row : row + 1, k * part : (k + 1) * part] = ref[...].astype(f32)
            out_ref[VEC_UP + k : VEC_UP + k + 1, :] = up_ref[...].astype(f32)
            for row, ref in enumerate((bs_ref, qp_ref, bp_ref)):
                out_ref[VEC_POOL + row : VEC_POOL + row + 1, k * small : (k + 1) * small] = ref[...].astype(f32)
            if k == 0:
                out_ref[VEC_CLASS : VEC_CLASS + 1, 0:CLASSES] = bc_ref[...].astype(f32)


def pack_call(me, vectors, up, pools, classes, width):
    operands = [v.reshape(1, -1) for v in vectors + [up] + pools + [classes]]
    return pl.pallas_call(
        pack_kernel,
        in_specs=[spec(pltpu.SMEM)] + [spec()] * len(operands),
        out_specs=spec(),
        out_shape=jax.ShapeDtypeStruct((16, width), f32),
        cost_estimate=NO_COST,
        name="pack",
    )(me, *operands)


def swap(value, axis, bit):
    count = lax.axis_size(axis)
    return lax.ppermute(value, axis, [(i, i ^ bit) for i in range(count)])


def join_far(shard):
    return double(shard, "fsdp", 2)


def join_core(column):
    core = lax.axis_index("fsdp") % 2
    across = swap(column, "fsdp", 1)
    full = jnp.where(
        core == 0, jnp.stack([column, across], axis=1), jnp.stack([across, column], axis=1)
    )
    return full.reshape(-1, column.shape[-1])


def bits_of(axis):
    return [1 << k for k in range(lax.axis_size(axis).bit_length() - 1)]


def tie(*values):
    return lax.optimization_barrier(values)


def merge_kernel(pick_ref, keep_ref, got_ref, send_ref, kept_ref):
    mine = pick_ref[0]
    for out, at in ((send_ref, 1 - mine), (kept_ref, mine)):
        out[0] = (keep_ref[0, at].astype(f32) + got_ref[0, at].astype(f32)).astype(bf16)


def merge(keep, got, mine, rows):
    n = keep.shape[-1]
    keep, got = keep.reshape(-1, 2, rows, n), got.reshape(-1, 2, rows, n)
    a = keep.shape[0]
    cuts = 1
    while rows // cuts > 256 and rows % (32 * cuts) == 0:
        cuts *= 2
    both = pl.BlockSpec((1, 2, rows // cuts, n), lambda i, j, s: (i, 0, j, 0))
    half = pl.BlockSpec((1, rows // cuts, n), lambda i, j, s: (i, j, 0))
    shape = jax.ShapeDtypeStruct((a, rows, n), bf16)
    return pl.pallas_call(
        merge_kernel,
        grid_spec=pltpu.PrefetchScalarGridSpec(
            num_scalar_prefetch=1, grid=(a, cuts), in_specs=[both, both], out_specs=[half, half]
        ),
        out_shape=[shape, shape],
        cost_estimate=NO_COST,
        compiler_params=pltpu.CompilerParams(vmem_limit_bytes=VMEM_LIMIT),
        name="merge",
    )(mine, keep, got)


def merge_cut_kernel(pick_ref, keep_ref, got_ref, first_ref, second_ref, kept_ref):
    mine = pick_ref[0]
    half = pl.num_programs(0) // 2
    total = lambda at: (keep_ref[at].astype(f32) + got_ref[at].astype(f32)).astype(bf16)
    kept_ref[...] = total(mine)

    @pl.when(pl.program_id(0) < half)
    def _():
        first_ref[...] = total(1 - mine)

    @pl.when(pl.program_id(0) >= half)
    def _():
        second_ref[...] = total(1 - mine)


def merge_cut(keep, got, mine):
    _, rows, n = keep.shape
    cuts = 4
    step = rows // cuts
    both = pl.BlockSpec((2, step, n), lambda j, s: (0, j, 0))
    part = jax.ShapeDtypeStruct((rows // 2, n), bf16)
    return pl.pallas_call(
        merge_cut_kernel,
        grid_spec=pltpu.PrefetchScalarGridSpec(
            num_scalar_prefetch=1,
            grid=(cuts,),
            in_specs=[both, both],
            out_specs=[
                pl.BlockSpec((step, n), lambda j, s: (jnp.minimum(j, cuts // 2 - 1), 0)),
                pl.BlockSpec((step, n), lambda j, s: (jnp.maximum(j - cuts // 2, 0), 0)),
                pl.BlockSpec((step, n), lambda j, s: (j, 0)),
            ],
        ),
        out_shape=[part, part, jax.ShapeDtypeStruct((rows, n), bf16)],
        cost_estimate=NO_COST,
        compiler_params=pltpu.CompilerParams(vmem_limit_bytes=VMEM_LIMIT),
        name="merge_cut",
    )(mine, keep, got)


def merge_parts_kernel(pick_ref, keep_ref, first_ref, second_ref, send_ref, kept_ref):
    def put(low_ref, high_ref):
        low_ref[...] = (keep_ref[0].astype(f32) + first_ref[...].astype(f32)).astype(bf16)
        high_ref[...] = (keep_ref[1].astype(f32) + second_ref[...].astype(f32)).astype(bf16)

    pl.when(pick_ref[0] == 0)(lambda: put(kept_ref, send_ref))
    pl.when(pick_ref[0] != 0)(lambda: put(send_ref, kept_ref))


def merge_parts(keep, first, second, mine):
    rows, n = first.shape
    shape = jax.ShapeDtypeStruct((rows, n), bf16)
    step = rows // 2
    block = pl.BlockSpec((step, n), lambda j, s: (j, 0))
    return pl.pallas_call(
        merge_parts_kernel,
        grid_spec=pltpu.PrefetchScalarGridSpec(
            num_scalar_prefetch=1,
            grid=(2,),
            in_specs=[pl.BlockSpec((2, step, n), lambda j, s: (0, j, 0)), block, block],
            out_specs=[block, block],
        ),
        out_shape=[shape, shape],
        cost_estimate=NO_COST,
        compiler_params=pltpu.CompilerParams(vmem_limit_bytes=VMEM_LIMIT),
        name="merge_parts",
    )(mine, keep.reshape(2, rows, n), first, second)


class Box:
    def __init__(self, keep):
        self.keep = keep


class Order:
    def __init__(self, holder):
        self.holder = holder
        self.results = None

    def after(self, value):
        if self.results is not None and self.results[0]:
            value, self.holder.keep, *done = tie(value, self.holder.keep, *self.results[1])
            self.results = (False, done)
        else:
            value, self.holder.keep = tie(value, self.holder.keep)
        return value

    def pin(self, value):
        box = Box(self.after(value))
        self.holder = box
        return box


class Sum:
    def __init__(self, keep, send, steps):
        self.keep, self.send, self.todo = keep, send, steps

    @staticmethod
    def mine(step):
        return (lax.axis_index(step[1]) // step[2][0]) % 2

    @staticmethod
    def shift(step, r):
        return sum(bit for k, bit in enumerate(step[2]) if (r >> k) & 1)

    def begin(self):
        step = self.todo[0]
        self.got = [swap(v, step[1], self.shift(step, r + 1)) for r, v in enumerate(self.send)]

    def end(self, order, pick=None):
        step = self.todo.pop(0)
        got = list(self.got)
        got[-1] = order.after(got[-1])
        order.holder = self
        n = self.keep.shape[-1]
        if step[0] == "gather":
            mine = self.mine(step)
            rows = self.keep.shape[0]
            out = jnp.zeros(((len(got) + 1) * rows, n), bf16)
            for r, v in enumerate([self.keep] + got):
                out = lax.dynamic_update_slice_in_dim(out, v, (mine ^ r) * rows, axis=0)
            self.keep = out
        else:
            parts = [self.keep] + got

            def total(pick):
                out = pick(parts[0]).astype(f32)
                for v in parts[1:]:
                    out = out + pick(v).astype(f32)
                return out.astype(bf16)

            following = self.todo[0] if self.todo else None
            if following is not None and following[0] == "scatter":
                mine = self.mine(following)
                ways, rows = 1 << len(following[2]), following[3]
                if pick is not None:
                    send, self.keep = merge(self.keep, got[0], pick, rows)
                    self.send = [send]
                    return

                def piece(r):
                    return lambda v: lax.dynamic_index_in_dim(
                        v.reshape(-1, ways, rows, n), mine ^ r, 1, keepdims=False
                    )

                self.send = [total(piece(r)) for r in range(1, ways)]
                self.keep = total(piece(0))
                return
            self.keep = total(lambda v: v.reshape(-1, n))
        if self.todo:
            self.send = [self.keep] * ((1 << len(self.todo[0][2])) - 1)

    def step(self, order, pick=None):
        self.end(order, pick)
        if self.todo:
            self.begin()


def bits_of(axis):
    return [1 << k for k in range(lax.axis_size(axis).bit_length() - 1)]


def double(value, axis, bit):
    mine = (lax.axis_index(axis) // bit) % 2
    got = swap(value, axis, bit)
    return jnp.where(mine == 0, jnp.stack([value, got]), jnp.stack([got, value]))


def rounds_of(axis):
    return [(bit,) for bit in bits_of(axis)]


def grad_steps(rows, far_second=False):
    steps = [("scatter", "fsdp", (1,), rows)]
    far = ("scatter", "fsdp", (2,))
    if not far_second:
        steps.append(far + (rows,))
    for k, bits in enumerate(rounds_of("ctx")):
        rows //= 2
        steps.append(("scatter", "ctx", bits, rows))
        if far_second and k == 0:
            steps.append(far + (rows,))
    return steps + [("gather", "ctx", bits, 0) for bits in rounds_of("ctx")[::-1]]


def shards(
    tokens,
    starts,
    labels,
    cotangent,
    w_query,
    b_query,
    w_key,
    w_value,
    b_value,
    w_out,
    b_out,
    norm1_gain,
    norm1_bias,
    w_up,
    b_up,
    w_down,
    b_down,
    norm2_gain,
    norm2_bias,
    w_student,
    b_student,
    pool_query,
    w_pool,
    b_pool,
    w_class,
    b_class,
):
    cycle_size = lax.axis_size("ctx")
    cycle_index = lax.axis_index("ctx")
    fsdp_size = lax.axis_size("fsdp")
    me = lax.axis_index("fsdp")
    core, far = me % 2, me // 2
    number = lambda *v: jnp.stack(v).astype(jnp.int32)
    me_row, owner, pick_far, pick_near = number(me), number(cycle_index), number(far), number(cycle_index % 2)
    blocks = number(1 - core, 3 - core, core, 2 + core)
    core_position = number(core, cycle_index)
    near_order = number(1 - cycle_index % 2, cycle_index % 2)
    tok_rows = tokens.shape[1]
    width = tokens.shape[2]
    part = width // fsdp_size
    hidden_part = b_up.shape[0]
    pool_width = w_pool.shape[1]
    seq_total = tok_rows * cycle_size
    score_scale = 1.0 / math.sqrt(HEAD_DIM)
    starts_row = starts[0]
    x_in = tokens[0]
    x_all = lax.all_gather(x_in, "ctx", axis=0, tiled=True)

    def pieces(shard, far):
        return [shard, swap(shard, "fsdp", 1), far, swap(far, "fsdp", 1)]

    far_wk, far_wv, far_wq = swap(w_key, "fsdp", 2), swap(w_value, "fsdp", 2), swap(w_query, "fsdp", 2)
    mats = jnp.concatenate([w_student, w_pool, jnp.pad(w_class, ((0, 0), (0, pool_width - CLASSES)))], axis=0)
    vectors = [b_query, b_value, b_out, norm1_gain, norm1_bias, b_down, norm2_gain, norm2_bias]
    vecs = pack_call(me_row, vectors, b_up, [b_student, pool_query, b_pool], b_class, width)
    far_vecs, mats = swap(vecs, "fsdp", 2), join_far(mats)
    far_wk, far_wv, far_wq, far_vecs, mats, w_out, w_up = tie(
        far_wk, far_wv, far_wq, far_vecs, mats, w_out, w_up
    )
    vecs = vecs + far_vecs
    vecs = vecs + swap(vecs, "fsdp", 1)
    vecs, owner, pick_far, pick_near, blocks, core_position, near_order = tie(
        vecs, owner, pick_far, pick_near, blocks, core_position, near_order
    )
    far_wo, far_w1 = swap(w_out, "fsdp", 2), swap(w_up, "fsdp", 2)
    piece_wk, piece_wv, piece_wq = pieces(w_key, far_wk), pieces(w_value, far_wv), pieces(w_query, far_wq)
    mats = join_core(mats).reshape(fsdp_size, -1, pool_width)
    far_wo, far_w1, mats, w_down, vecs, *near = tie(
        far_wo, far_w1, mats, w_down, vecs, piece_wk[3], piece_wv[3], piece_wq[3]
    )
    piece_wk[3], piece_wv[3], piece_wq[3] = near
    far_w2 = swap(w_down, "fsdp", 2)
    piece_wo, piece_w1 = pieces(w_out, far_wo), pieces(w_up, far_w1)

    local_pos = cycle_index * tok_rows + jnp.arange(tok_rows, dtype=jnp.int32)
    local_doc = doc_of(local_pos, starts_row)
    all_doc = doc_of(jnp.arange(seq_total, dtype=jnp.int32), starts_row)
    at = jnp.arange(128, dtype=jnp.int32)[None, :]
    extra = ((at == all_doc[:, None]) | ((at >= NDOC) & (at < NDOC + 3))).astype(bf16)
    docs = local_doc[None, :]
    doc_column = local_doc[:, None]

    query_s, key_b, value_b, x_all_t = project(me_row, x_in, x_all, vecs, piece_wq, piece_wk, piece_wv)
    attn_t, attn_b, attn_low_t, lse = attend(query_s, key_b, value_b, extra, docs)
    attn_b, far_w2 = tie(attn_b, far_w2)
    piece_w2 = pieces(w_down, far_w2)

    hid_t, normed1, inv1, act, slope, out_b, normed2, inv2, student, score, local = layer_forward_call(
        me_row, attn_b, x_in, vecs, mats, doc_column, piece_wo, piece_w1, piece_w2
    )
    parts = lax.all_to_all(
        jnp.broadcast_to(local[None], (cycle_size,) + local.shape), "ctx", 0, 0, tiled=True
    )
    grad_down_b, grad_res2, logits, vec_a, tables = head_call(
        labels, owner, parts, vecs, mats, doc_column, student, score, out_b, cotangent[0], normed2, inv2
    )
    logits = logits[:NDOC, :CLASSES]


    def grad_sum(pair, far_second=False):
        return Sum(pair[1], [pair[0]], grad_steps(pair[0].shape[1], far_second))

    sum_w2 = grad_sum(down_grad(blocks, act, grad_down_b))
    sum_w2.begin()
    grad_up_b, grad_res1, grad_branch_b, grad_attn_b, vec_b = layer_backward_call(
        me_row, grad_down_b, grad_res2, slope, normed1, inv1, vecs, piece_wo, piece_w1, piece_w2
    )
    order = Order(Box(grad_attn_b))
    attn_box = order.holder
    first, second, sum_w2.keep = merge_cut(sum_w2.keep, order.after(sum_w2.got[0]), pick_far)
    sum_w2.todo = sum_w2.todo[2:]
    order.holder = sum_w2
    first, second = swap(first, "fsdp", 2), swap(second, "fsdp", 2)
    grad_up_b = order.after(grad_up_b)
    sum_mid = grad_sum(
        middle_grad(blocks, hid_t, grad_up_b, attn_low_t, grad_branch_b, tables, vec_a, vec_b), True
    )
    sum_mid.keep = order.after(sum_mid.keep)
    order.holder = sum_mid
    sum_mid.begin()
    pairs = width // (2 * HEAD_DIM)
    some = (pairs + 1) // 2
    given = (query_s, key_b, value_b, extra, docs, attn_t, lse)
    grad_attn_b = order.after(attn_box.keep)
    dq, dk, dv = attend_back(0, some, (), *given, grad_attn_b)
    box = order.pin(dq)
    first = order.after(first)
    sum_mid.step(order, pick_near)
    grad_attn_b, first = tie(order.after(grad_attn_b), first)
    dq, dk, dv = attend_back(some, pairs - some, (box.keep, dk, dv), *given, grad_attn_b)
    box = order.pin(dq)
    send, sum_w2.keep = merge_parts(sum_w2.keep, first, order.after(second), pick_near)
    sum_w2.send = [send]
    order.holder = sum_w2
    sum_w2.begin()
    dq = order.after(box.keep)
    if seq_total <= 4096:
        send, keep, others_send, others_keep, near = finish(
            core_position, me_row, dq, dk, dv, x_all_t, grad_res1, piece_wk, piece_wv, piece_wq
        )
    else:
        send, keep = last_grad(blocks, core_position[1:], x_all_t, dq, dk, dv)
        others_send, others_keep, near = others_call(
            near_order, me_row, dq, grad_res1, dk, dv, piece_wk, piece_wv, piece_wq, tok_rows
        )
    near = order.after(near)
    sum_mid.step(order)
    sum_last = grad_sum((order.after(send), keep))
    sum_last.begin()
    sum_last.step(order, pick_far)
    sum_others = Sum(
        others_keep, [order.after(others_send)], [("scatter", "ctx", bits, tok_rows) for bits in rounds_of("ctx")]
    )
    sum_others.begin()
    sum_w2.step(order)

    def early_results():
        middle = sum_mid.keep.astype(f32)
        ups_sum, middle = middle[:hidden_part], middle[hidden_part:]
        high = part * pool_width // width
        tall = middle[part : part + high]
        done_ws = jnp.concatenate(jnp.split(tall, width // pool_width, axis=1), axis=0)
        rest = middle[part + high :]
        base, half = 2 * pool_width, width // 2
        rows = jnp.concatenate([rest[:16, base : base + half], rest[16:, base : base + half]], axis=1)
        return (
            middle[:part],
            done_ws,
            rest[:, :pool_width],
            rest[:, pool_width : pool_width + CLASSES],
            lax.dynamic_slice_in_dim(rows, me * part, part, axis=1),
            lax.dynamic_slice_in_dim(rows[3:6], me * w_pool.shape[0], w_pool.shape[0], axis=1),
            rows[6, :CLASSES],
            lax.dynamic_index_in_dim(rows, 8 + me, 0, keepdims=False),
            jnp.concatenate(jnp.split(ups_sum, hidden_part // part, axis=0), axis=1),
            sum_w2.keep.astype(f32),
        )

    waves = [sum_w2, sum_mid, sum_others, sum_last]
    plan = PLAN if cycle_size == 8 else []
    for k in plan:
        if k == 30:
            order.results = (True, early_results())
            continue
        wave = waves[k % 10]
        if k < 20 and wave.todo:
            wave.end(order)
        if k >= 20:
            wave.send = [order.after(wave.send[0])]
        if k // 10 != 1 and wave.todo:
            wave.begin()
    while any(w.todo for w in waves):
        for w in waves:
            if w.todo:
                w.step(order)
    if order.results is None:
        order.results = (False, early_results())

    grad_tokens = near + sum_others.keep.reshape(tok_rows, width).astype(f32)
    (
        done_wo, done_ws, done_wp, done_wc, own, pools, done_bc, done_c1, done_w1, done_w2,
    ) = order.results[1]
    last = sum_last.keep.astype(f32)
    late = lax.dynamic_slice_in_dim(last[3 * part : 3 * part + 8], me * part, part, axis=1)
    return (
        out_b[None],
        logits[None],
        grad_tokens[None],
        last[:part],
        late[0],
        last[part : 2 * part],
        last[2 * part : 3 * part],
        late[1],
        done_wo,
        own[14],
        own[12],
        own[13],
        done_w1,
        done_c1,
        done_w2,
        own[0],
        own[1],
        own[2],
        done_ws,
        pools[0],
        pools[1],
        done_wp,
        pools[2],
        done_wc,
        done_bc,
    )


def solution(mesh):
    in_specs = (
        P("fsdp", "ctx", None),
        P("fsdp", None),
        P("fsdp", None),
        P("fsdp", "ctx", None),
        P("fsdp", None),
        P("fsdp"),
        P("fsdp", None),
        P("fsdp", None),
        P("fsdp"),
        P("fsdp", None),
        P("fsdp"),
        P("fsdp"),
        P("fsdp"),
        P("fsdp", None),
        P("fsdp"),
        P("fsdp", None),
        P("fsdp"),
        P("fsdp"),
        P("fsdp"),
        P("fsdp", None),
        P("fsdp"),
        P("fsdp"),
        P("fsdp", None),
        P("fsdp"),
        P("fsdp", None),
        P(),
    )
    out_specs = (
        P("fsdp", "ctx", None),
        P("fsdp", None, None),
        P("fsdp", "ctx", None),
        P("fsdp", None),
        P("fsdp"),
        P("fsdp", None),
        P("fsdp", None),
        P("fsdp"),
        P("fsdp", None),
        P("fsdp"),
        P("fsdp"),
        P("fsdp"),
        P("fsdp", None),
        P("fsdp"),
        P("fsdp", None),
        P("fsdp"),
        P("fsdp"),
        P("fsdp"),
        P("fsdp", None),
        P("fsdp"),
        P("fsdp"),
        P("fsdp", None),
        P("fsdp"),
        P("fsdp", None),
        P(),
    )
    return jax.shard_map(shards, mesh=mesh, in_specs=in_specs, out_specs=out_specs, check_vma=False)
```
